32 devices in a mesh: dp: 8 (over z, y), mp: 4 (over x, core).
Axes of the slice: x: 2, y: 2, z: 4, core: 2. Of those that a mesh axis runs over, the one named last changes fastest.
Arguments:
- block_in: bfloat16 [2, 8192, 1536], P(None, ('dp', 'mp')), may hold values from -6 to 6
- doc_ids: int32 [2, 8192], P(None, 'dp'), may hold values from 0 to 19, never falling along the last dimension, each value on 1 to 800 neighbouring positions
- mix_gain: bfloat16 [1536], replicated, may hold values from 0.099609375 to 1.8984375
- proj_x: bfloat16 [1536, 2048], P('dp', 'mp'), may hold values from -0.15625 to 0.15625
- proj_y: bfloat16 [1536, 2048], P('dp', 'mp'), may hold values from -0.15625 to 0.15625
- conv_taps: bfloat16 [4, 2048], P(None, 'mp'), may hold values from -3 to 3
- recur_gate: bfloat16 [16, 128, 128], P('mp', None, 'dp'), may hold values from -0.5 to 0.5
- input_gate: bfloat16 [16, 128, 128], P('mp', None, 'dp'), may hold values from -0.5 to 0.5
- decay_param: bfloat16 [2048], P('mp'), may hold values from 0.5 to 7
- proj_out: bfloat16 [2048, 1536], P('mp', 'dp'), may hold values from -0.375 to 0.375
- ffn_gain: bfloat16 [1536], replicated, may hold values from 0.099609375 to 1.8984375
- ffn_gate: bfloat16 [1536, 4608], P('dp', 'mp'), may hold values from -0.15625 to 0.15625
- ffn_up: bfloat16 [1536, 4608], P('dp', 'mp'), may hold values from -0.15625 to 0.15625
- ffn_down: bfloat16 [4608, 1536], P('mp', 'dp'), may hold values from -0.1875 to 0.1875
- out_grad: bfloat16 [2, 8192, 1536], P(None, ('dp', 'mp')), may hold values from -6 to 6
Outputs:
- block_out: bfloat16 [2, 8192, 1536], P(None, ('dp', 'mp'))
- block_in_grad: float32 [2, 8192, 1536], P(None, ('dp', 'mp'))
- mix_gain_grad: float32 [1536], replicated
- proj_x_grad: float32 [1536, 2048], P('dp', 'mp')
- proj_y_grad: float32 [1536, 2048], P('dp', 'mp')
- conv_taps_grad: float32 [4, 2048], P(None, 'mp')
- recur_gate_grad: float32 [16, 128, 128], P('mp', None, 'dp')
- input_gate_grad: float32 [16, 128, 128], P('mp', None, 'dp')
- decay_param_grad: float32 [2048], P('mp')
- proj_out_grad: float32 [2048, 1536], P('mp', 'dp')
- ffn_gain_grad: float32 [1536], replicated
- ffn_gate_grad: float32 [1536, 4608], P('dp', 'mp')
- ffn_up_grad: float32 [1536, 4608], P('dp', 'mp')
- ffn_down_grad: float32 [4608, 1536], P('mp', 'dp')
The draws below stay inside these ranges and needn't reach their ends.
Inputs may be any that keep to these rules, and one draw needn't show every extreme that they name: `doc_ids`: within a micro-batch document numbers never fall along the tokens; each document has 1 to 800 tokens and one has exactly 800.
All inputs are finite; a program needn't handle non-finite values.
Results may differ from the reference program's by a relative error of at most 0.017.
The reference program's roundings to bfloat16 on the way count: a program that leaves them out, or rounds other values in their place, can miss the bound.
Values may be sent and summed in bfloat16 or wider, within the bound.
No kernel may reach another device: no remote copies, remote signals or barrier semaphores. Data moves between devices by JAX's collectives and lax.ppermute only.
A program may use at most 256 MiB of HBM per device.

```python
import math
import jax
import jax.numpy as jnp
import numpy as np
from jax import lax

D = 1536
R = 2048
F = 4608
NB = 16
BS = 128
KW = 4
LEN = 1024
SEQS = 1
MB = 2
DOC_MOST = 800
BT = 8192
DOC_COUNT = 20
N_DP = 8


def levels(own_key, dims, cuts, smallest, high):
    def one(axis_at, shards_of):
        steps = jax.random.uniform(jax.random.fold_in(jax.random.fold_in(own_key, 6), axis_at), (shards_of,), jnp.float32, smallest / len(cuts), high / len(cuts))
        return jnp.repeat(jnp.exp(steps), dims[axis_at] // shards_of).reshape((-1,) + (1,) * (len(dims) - axis_at - 1))

    loudness = one(*cuts[0])
    for cut in cuts[1:]:
        loudness = loudness * one(*cut)
    return loudness


def profile(amount, total, limit, lean):
    weights = [(1 << 20) // math.isqrt(grade ** lean) + 1 for grade in range(2, amount + 1)]
    rest, counts = total - limit - (amount - 1), [1] * (amount - 1)
    while rest > 0:
        movable = [i for i in range(amount - 1) if counts[i] < limit]
        whole, remaining = sum([weights[i] for i in movable]), rest
        for i in movable:
            more = min(limit - counts[i], max(1, remaining * weights[i] // whole), rest)
            counts[i] = counts[i] + more
            rest = rest - more
    return np.array([limit] + counts)


def uneven_parts(rng, amount, total, reach, slope):
    if amount == 2:
        one = jax.random.randint(rng, (), max(1, total - reach), min(reach, total - 1) + 1)
        return jnp.stack([one, total - one])
    sizes = jnp.asarray(profile(amount, total, reach, slope), jnp.int32)
    couples = (amount - 1) // 2
    source_of, receiver = sizes[1:1 + 2 * couples:2], sizes[2:2 + 2 * couples:2]
    slack = jnp.minimum(source_of - 1, reach - receiver)
    moved = jax.random.randint(jax.random.fold_in(rng, 1), (couples,), 0, 1 << 20) % (slack + 1)
    sizes = sizes.at[1:1 + 2 * couples:2].set(source_of - moved).at[2:2 + 2 * couples:2].set(receiver + moved)
    return sizes[jax.random.permutation(jax.random.fold_in(rng, 2), amount)]


def normal_values(rng, dims, deviation, bound, split=(), kind=jnp.bfloat16):
    entries = deviation * jax.random.normal(rng, dims, jnp.float32)
    if split:
        entries = entries * levels(rng, dims, split, -0.22, 0.18)
    return jnp.clip(entries, -bound, bound).astype(kind)


def setup_inputs(seed: int = 0) -> dict:
    key_list = jax.random.split(jax.random.key(seed), 16)
    return {
        "block_in": normal_values(key_list[0], (MB, BT, D), 1.0, 6.0, ((1, 32),)),
        "doc_ids": jax.vmap(lambda own: jnp.searchsorted(jnp.cumsum(uneven_parts(own, DOC_COUNT, BT, DOC_MOST, 0)), jnp.arange(BT), side="right"))(jax.random.split(key_list[1], MB)).reshape((MB, BT)).astype(jnp.int32),
        "mix_gain": jnp.clip(1.0 + 0.18 * jax.random.normal(key_list[2], (D,), jnp.float32), 0.099609375, 1.8984375).astype(jnp.bfloat16),
        "proj_x": normal_values(key_list[3], (D, R), D ** -0.5, 0.15625, ((0, 8), (1, 4))),
        "proj_y": normal_values(key_list[4], (D, R), D ** -0.5, 0.15625, ((0, 8), (1, 4))),
        "conv_taps": normal_values(key_list[5], (KW, R), 0.5, 3.0, ((1, 4),)),
        "recur_gate": normal_values(key_list[6], (NB, BS, BS), BS ** -0.5, 0.5, ((0, 4), (2, 8))),
        "input_gate": normal_values(key_list[7], (NB, BS, BS), BS ** -0.5, 0.5, ((0, 4), (2, 8))),
        "decay_param": jnp.clip(0.5 + 6.5 * jax.random.uniform(key_list[8], (R,), jnp.float32) ** levels(key_list[8], (R,), ((0, 4),), -0.2, 0.2), 0.5, 7.0).astype(jnp.bfloat16),
        "proj_out": normal_values(key_list[9], (R, D), (R // 8) ** -0.5, 0.375, ((0, 4), (1, 8))),
        "ffn_gain": jnp.clip(1.0 + 0.18 * jax.random.normal(key_list[10], (D,), jnp.float32), 0.099609375, 1.8984375).astype(jnp.bfloat16),
        "ffn_gate": normal_values(key_list[11], (D, F), D ** -0.5, 0.15625, ((0, 8), (1, 4))),
        "ffn_up": normal_values(key_list[12], (D, F), D ** -0.5, 0.15625, ((0, 8), (1, 4))),
        "ffn_down": normal_values(key_list[13], (F, D), (F // 4) ** -0.5, 0.1875, ((0, 4), (1, 8))),
        "out_grad": normal_values(key_list[14], (MB, BT, D), 1.0, 6.0, ((1, 32),)),
    }


@jax.custom_vjp
def low(v):
    return lax.optimization_barrier(v.astype(jnp.bfloat16)).astype(jnp.float32)

@jax.custom_vjp
def low_back(v):
    return v

def low_keep(v):
    return (low(v), None)

def low_pass(kept, grad):
    return (grad,)

def back_keep(v):
    return (v, None)

def back_low(kept, grad):
    return (low(grad),)
low.defvjp(low_keep, low_pass)
low_back.defvjp(back_keep, back_low)
norm_eps = 1e-06
root_floor = 0.01
decay_scale = 8.0
highest = lax.Precision.HIGHEST

def matmul(left, right):
    return jnp.dot(left, right, precision=highest, preferred_element_type=jnp.float32)

def rms_scale(values, gain):
    inverse = lax.rsqrt(lax.optimization_barrier(jnp.mean(values * values, axis=-1, keepdims=True)) + norm_eps)
    return values * inverse * gain

def shifted(values, offset):
    return jnp.concatenate([jnp.zeros((offset,) + values.shape[1:], values.dtype), values[:-offset]], axis=0)

def lru_gates(recur_logit, input_logit, conv_values, decay_values, resets):
    log_decay = -decay_scale * jax.nn.sigmoid(recur_logit) * jax.nn.softplus(-decay_values)
    decay = jnp.exp(log_decay)
    margin = jnp.maximum(1.0 - jnp.exp(2.0 * log_decay), root_floor)
    multiplier = jnp.where(resets[:, None], 1.0, jnp.sqrt(margin))
    driven = conv_values * jax.nn.sigmoid(input_logit) * multiplier
    carried = jnp.where(resets[:, None], 0.0, decay)
    return (carried, driven)

def recur_step(state, pair):
    state = pair[0] * state + pair[1]
    return (state, state)

def group_forward(weights, values, docs):
    mix_gain, proj_x, proj_y, conv_taps, recur_gate, input_gate, decay_param, proj_out, ffn_gain, ffn_gate, ffn_up, ffn_down = weights
    count = values.shape[0]
    position = jnp.arange(count, dtype=jnp.int32) % LEN
    previous = jnp.concatenate([docs[:1], docs[:-1]])
    resets = jnp.logical_or(position == 0, docs != previous)
    normed = low(rms_scale(values, mix_gain))
    branch_x = low_back(matmul(normed, proj_x))
    branch_y = low_back(matmul(normed, proj_y))
    mixed = conv_taps[0] * branch_x
    for offset in range(1, KW):
        earlier_ids = jnp.concatenate([jnp.full((offset,), -1, jnp.int32), docs[:-offset]])
        keep_mask = jnp.logical_and(docs == earlier_ids, position >= offset)[:, None]
        mixed = mixed + conv_taps[offset] * jnp.where(keep_mask, shifted(branch_x, offset), 0.0)
    conv_values = low(mixed)
    blocks = conv_values.reshape(count, NB, BS)
    recur_logit = low_back(jnp.einsum('tnb,nbc->tnc', blocks, recur_gate, precision=highest).reshape(count, R))
    input_logit = low_back(jnp.einsum('tnb,nbc->tnc', blocks, input_gate, precision=highest).reshape(count, R))
    carried, driven = lru_gates(recur_logit, input_logit, conv_values, decay_param, resets)
    _, states = lax.scan(recur_step, jnp.zeros((R,), jnp.float32), (carried, driven))
    gated = low(states * jax.nn.gelu(branch_y))
    middle = values + low_back(matmul(gated, proj_out))
    normed_two = low(rms_scale(middle, ffn_gain))
    gate_pre = low_back(matmul(normed_two, ffn_gate))
    up_pre = low_back(matmul(normed_two, ffn_up))
    hidden = low(jax.nn.gelu(gate_pre) * up_pre)
    return middle + low_back(matmul(hidden, ffn_down))

def reference(block_in, doc_ids, mix_gain, proj_x, proj_y, conv_taps, recur_gate, input_gate, decay_param, proj_out, ffn_gain, ffn_gate, ffn_up, ffn_down, out_grad):
    weights = (mix_gain.astype(jnp.float32), proj_x.astype(jnp.float32), proj_y.astype(jnp.float32), conv_taps.astype(jnp.float32), recur_gate.astype(jnp.float32), input_gate.astype(jnp.float32), decay_param.astype(jnp.float32), proj_out.astype(jnp.float32), ffn_gain.astype(jnp.float32), ffn_gate.astype(jnp.float32), ffn_up.astype(jnp.float32), ffn_down.astype(jnp.float32))
    inputs = block_in.astype(jnp.float32)
    groups = MB * N_DP
    group_rows = SEQS * LEN
    grouped_docs = doc_ids.reshape(groups, group_rows)
    checked = jax.checkpoint(group_forward)

    def whole(params, values):
        grouped = values.reshape(groups, group_rows, D)

        def one_group(pair):
            return checked(params, pair[0], pair[1])
        result = lax.map(one_group, (grouped, grouped_docs))
        return result.reshape(MB, N_DP * group_rows, D)
    result, pullback = jax.vjp(whole, weights, inputs)
    grads, input_grad = pullback(out_grad.astype(jnp.float32))
    return (result.astype(jnp.bfloat16), input_grad, grads[0], grads[1], grads[2], grads[3], grads[4], grads[5], grads[6], grads[7], grads[8], grads[9], grads[10], grads[11])
```

```python
import functools

import jax
import jax.numpy as jnp
import numpy as np
from jax import lax
from jax.experimental import pallas as pl
from jax.experimental.pallas import tpu as pltpu
from jax.sharding import PartitionSpec as P

LEN = 1024
BS = 128
KW = 4
SEGS = 8

norm_eps = 1e-06
root_floor = 0.01
decay_scale = 8.0
gelu_a = 0.7978845608028654
gelu_b = 0.044715

f32 = jnp.float32
bf16 = jnp.bfloat16


BLOCK_AT = (2, 0, 3, 1)


def project(left, right):
    return jnp.dot(left, right, preferred_element_type=f32)


def inner(left, right):
    return lax.dot_general(left, right, (((0,), (0,)), ((), ())), preferred_element_type=f32)


def against(left, right):
    return lax.dot_general(left, right, (((1,), (1,)), ((), ())), preferred_element_type=f32)


def norm_back(grad_normed, unit_rows, inverse, gain):
    scaled = grad_normed * gain
    return inverse * (scaled - unit_rows * jnp.mean(scaled * unit_rows, axis=-1, keepdims=True))


def gelu_parts(v):
    squared = v * v
    inside = gelu_a * v * (1.0 + gelu_b * squared)
    t = jnp.tanh(inside)
    half = 0.5 * (1.0 + t)
    value = v * half
    slope = half + 0.5 * v * (1.0 - t * t) * (gelu_a * (1.0 + 3.0 * gelu_b * squared))
    return value, slope


def gelu_value(v):
    return 0.5 * v * (1.0 + jnp.tanh(gelu_a * v * (1.0 + gelu_b * v * v)))


def place_of(me, block):
    differ = lax.bitwise_xor(me, block)
    low = lax.bitwise_and(differ, 1)
    high = lax.shift_right_logical(differ, 1)
    return 2 * (1 - low) + high


CHUNK = 64


def mixing_forward_kernel(me_ref, branch, ids, taps, gates, rate, gated, states, conv, sig_r, sig_i,
                          xpad, idpad, a_buf, b_buf, p_buf):
    rows = LEN
    quarter = rows // 4
    me = me_ref[0]
    xpad[0:8, :] = jnp.zeros((8, BS), f32)
    idpad[0:8, :] = jnp.full((8, BS), -1, jnp.int32)
    idpad[8:8 + rows, :] = ids[...]
    for block in range(4):
        at = place_of(me, block)
        xpad[8 + block * quarter: 8 + (block + 1) * quarter, :] = branch[at, :, 0:BS]
    rate_row = rate[0:1, :]

    def convolve(step, _):
        base = step * CHUNK
        own_ids = idpad[pl.ds(base + 8, CHUNK), :]
        total = taps[0:1, :] * xpad[pl.ds(base + 8, CHUNK), :]
        for k in range(1, KW):
            same = idpad[pl.ds(base + 8 - k, CHUNK), :] == own_ids
            total = total + taps[k:k + 1, :] * jnp.where(same, xpad[pl.ds(base + 8 - k, CHUNK), :], 0.0)
        conv[pl.ds(base, CHUNK), :] = total.astype(bf16)
        return 0

    lax.fori_loop(0, rows // CHUNK, convolve, 0, unroll=2)

    logits = lax.dot_general(conv[...], gates[...], (((1,), (1,)), ((), ())), preferred_element_type=f32)
    a_buf[...] = logits[:, 0:BS]
    b_buf[...] = logits[:, BS:2 * BS]

    def gate(step, _):
        base = step * CHUNK
        here = pl.ds(base, CHUNK)
        sr = jax.nn.sigmoid(a_buf[here, :])
        si = jax.nn.sigmoid(b_buf[here, :])
        sig_r[here, :] = sr
        sig_i[here, :] = si
        same = idpad[pl.ds(base + 7, CHUNK), :] == idpad[pl.ds(base + 8, CHUNK), :]
        decay = jnp.exp(rate_row * sr)
        margin = jnp.maximum(1.0 - decay * decay, root_floor)
        multiplier = jnp.where(same, jnp.sqrt(margin), 1.0)
        b_buf[here, :] = conv[here, :].astype(f32) * si * multiplier
        a_buf[here, :] = jnp.where(same, decay, 0.0)
        return 0

    lax.fori_loop(0, rows // CHUNK, gate, 0, unroll=2)

    seg = rows // SEGS

    def scan(step, carry):
        h, p = carry
        rows_at = pl.ds(step, SEGS, stride=seg)
        a = a_buf[rows_at, :]
        h = a * h + b_buf[rows_at, :]
        p = a * p
        b_buf[rows_at, :] = h
        p_buf[rows_at, :] = p
        return h, p

    h, p = lax.fori_loop(0, seg, scan, (jnp.zeros((SEGS, BS), f32), jnp.ones((SEGS, BS), f32)), unroll=8)
    carry = jnp.zeros((1, BS), f32)
    for s in range(SEGS):
        at = place_of(me, s // 2)
        inside = (s % 2) * seg
        for c in range(seg // CHUNK):
            here = slice(s * seg + c * CHUNK, s * seg + (c + 1) * CHUNK)
            state = b_buf[here, :] + p_buf[here, :] * carry
            states[here, :] = state
            there = slice(inside + c * CHUNK, inside + (c + 1) * CHUNK)
            gated[at, there, :] = (state * gelu_value(branch[at, there, BS:2 * BS])).astype(bf16)
        carry = h[s:s + 1, :] + p[s:s + 1, :] * carry


def mixing_backward_kernel(me_ref, grad_gated, branch, states, conv, sig_r, sig_i, ids, taps, gates, rate, slope,
                           grad_branch, grad_gates, small,
                           xpad, idpad, spad, a_buf, g_buf, p_buf, low, gcpad):
    rows = LEN
    quarter = rows // 4
    me = me_ref[0]
    zero8 = jnp.zeros((8, BS), f32)
    xpad[0:8, :] = zero8
    spad[0:8, :] = zero8
    spad[8:8 + rows, :] = states[...]
    idpad[0:8, :] = jnp.full((8, BS), -1, jnp.int32)
    idpad[8:8 + rows, :] = ids[...]
    idpad[8 + rows:16 + rows, :] = jnp.full((8, BS), -1, jnp.int32)
    a_buf[rows:rows + 8, :] = zero8
    gcpad[rows:rows + 8, :] = zero8
    rate_row = rate[0:1, :]
    slope_row = slope[0:1, :]
    per = quarter // CHUNK
    for block in range(4):
        at = place_of(me, block)
        xpad[8 + block * quarter: 8 + (block + 1) * quarter, :] = branch[at, :, 0:BS]

        def enter(step, _, at=at, block=block):
            there = pl.ds(step * CHUNK, CHUNK)
            base = block * quarter + step * CHUNK
            here = pl.ds(base, CHUNK)
            value, gradient = gelu_parts(branch[at, there, BS:2 * BS])
            incoming = grad_gated[at, there, :]
            g_buf[here, :] = incoming * value
            grad_branch[at, there, BS:2 * BS] = (gradient * states[here, :] * incoming).astype(bf16)
            same = idpad[pl.ds(base + 7, CHUNK), :] == idpad[pl.ds(base + 8, CHUNK), :]
            a_buf[here, :] = jnp.where(same, jnp.exp(rate_row * sig_r[here, :]), 0.0)
            return 0

        lax.fori_loop(0, per, enter, 0, unroll=2)

    seg = rows // SEGS

    def scan(step, carry):
        h, p = carry
        t = seg - 1 - step
        a = a_buf[pl.ds(t + 1, SEGS, stride=seg), :]
        rows_at = pl.ds(t, SEGS, stride=seg)
        h = a * h + g_buf[rows_at, :]
        p = a * p
        g_buf[rows_at, :] = h
        p_buf[rows_at, :] = p
        return h, p

    h, p = lax.fori_loop(0, seg, scan, (jnp.zeros((SEGS, BS), f32), jnp.ones((SEGS, BS), f32)), unroll=8)

    carry = jnp.zeros((1, BS), f32)
    decay_sum = jnp.zeros((8, BS), f32)
    for s in reversed(range(SEGS)):

        def leave(step, acc, s=s, carry=carry):
            base = s * seg + step * CHUNK
            here = pl.ds(base, CHUNK)
            g = g_buf[here, :] + p_buf[here, :] * carry
            grad_carried = g * spad[pl.ds(base + 7, CHUNK), :]
            same = idpad[pl.ds(base + 7, CHUNK), :] == idpad[pl.ds(base + 8, CHUNK), :]
            decay = a_buf[here, :]
            square = decay * decay
            inside = 1.0 - square
            root = jnp.sqrt(jnp.maximum(inside, root_floor))
            sr = sig_r[here, :]
            si = sig_i[here, :]
            cv = conv[here, :].astype(f32)
            multiplier = jnp.where(same, root, 1.0)
            gsi = g * si
            gcsi = gsi * cv
            grad_log = jnp.where(
                same,
                grad_carried * decay - jnp.where(inside > root_floor, gcsi * square / root, 0.0),
                0.0,
            )
            gcpad[here, :] = gsi * multiplier
            weighted = grad_log * sr
            low[here, 0:BS] = (weighted * (1.0 - sr) * rate_row).astype(bf16)
            low[here, BS:2 * BS] = (gcsi * multiplier * (1.0 - si)).astype(bf16)
            return acc + jnp.sum(weighted.reshape(CHUNK // 8, 8, BS), axis=0)

        decay_sum = lax.fori_loop(0, seg // CHUNK, leave, decay_sum, unroll=2)
        carry = h[s:s + 1, :] + p[s:s + 1, :] * carry

    grad_gates[0] = lax.dot_general(low[...], conv[...], (((0,), (0,)), ((), ())), preferred_element_type=f32)
    p_buf[...] = lax.dot_general(low[...], gates[...], (((1,), (0,)), ((), ())), preferred_element_type=f32)

    def add_gates(step, _):
        here = pl.ds(step * CHUNK, CHUNK)
        gcpad[here, :] = gcpad[here, :] + p_buf[here, :]
        return 0

    lax.fori_loop(0, rows // CHUNK, add_gates, 0, unroll=2)

    sums = tuple(jnp.zeros((8, BS), f32) for _ in range(KW))
    for block in range(4):
        at = place_of(me, block)

        def finish(step, sums, at=at, block=block):
            there = pl.ds(step * CHUNK, CHUNK)
            base = block * quarter + step * CHUNK
            gc = gcpad[pl.ds(base, CHUNK), :]
            own_ids = idpad[pl.ds(base + 8, CHUNK), :]
            fold = lambda v: jnp.sum(v.reshape(CHUNK // 8, 8, BS), axis=0)
            new = [sums[0] + fold(gc * xpad[pl.ds(base + 8, CHUNK), :])]
            grad_x = taps[0:1, :] * gc
            for k in range(1, KW):
                same = idpad[pl.ds(base + 8 - k, CHUNK), :] == own_ids
                new.append(sums[k] + fold(jnp.where(same, gc * xpad[pl.ds(base + 8 - k, CHUNK), :], 0.0)))
                after = idpad[pl.ds(base + 8 + k, CHUNK), :] == own_ids
                grad_x = grad_x + taps[k:k + 1, :] * jnp.where(after, gcpad[pl.ds(base + k, CHUNK), :], 0.0)
            grad_branch[at, there, 0:BS] = grad_x.astype(bf16)
            return tuple(new)

        sums = lax.fori_loop(0, per, finish, sums, unroll=2)
    small[...] = jnp.zeros((8, BS), f32)
    for k in range(KW):
        small[k:k + 1, :] = jnp.sum(sums[k], axis=0, keepdims=True)
    small[KW:KW + 1, :] = jnp.sum(decay_sum, axis=0, keepdims=True) * slope_row


def mixing_forward(me, branch, ids, taps, gates, rate):
    rows = LEN
    blocks = branch.shape[2] // (2 * BS)
    channels = blocks * BS
    flat = lambda n, me: (0, n)
    return pl.pallas_call(
        mixing_forward_kernel,
        grid_spec=pltpu.PrefetchScalarGridSpec(
            num_scalar_prefetch=1,
            grid=(blocks,),
            in_specs=[
                pl.BlockSpec((4, rows // 4, 2 * BS), lambda n, me: (0, 0, n)),
                pl.BlockSpec((rows, BS), lambda n, me: (0, 0)),
                pl.BlockSpec((8, BS), flat),
                pl.BlockSpec((2 * BS, BS), flat),
                pl.BlockSpec((8, BS), flat),
            ],
            out_specs=[
                pl.BlockSpec((4, rows // 4, BS), lambda n, me: (0, 0, n)),
                pl.BlockSpec((rows, BS), flat),
                pl.BlockSpec((rows, BS), flat),
                pl.BlockSpec((rows, BS), flat),
                pl.BlockSpec((rows, BS), flat),
            ],
            scratch_shapes=[
                pltpu.VMEM((rows + 8, BS), f32),
                pltpu.VMEM((rows + 8, BS), jnp.int32),
                pltpu.VMEM((rows, BS), f32),
                pltpu.VMEM((rows, BS), f32),
                pltpu.VMEM((rows, BS), f32),
            ],
        ),
        out_shape=[
            jax.ShapeDtypeStruct((4, rows // 4, channels), bf16),
            jax.ShapeDtypeStruct((rows, channels), f32),
            jax.ShapeDtypeStruct((rows, channels), bf16),
            jax.ShapeDtypeStruct((rows, channels), f32),
            jax.ShapeDtypeStruct((rows, channels), f32),
        ],
        cost_estimate=pl.CostEstimate(flops=2 * rows * channels * 256, bytes_accessed=24_000_000, transcendentals=0),
        name="mixing_forward",
    )(me, branch, ids, taps, gates, rate)


def mixing_backward(me, grad_gated, branch, states, conv, sig_r, sig_i, ids, taps, gates, rate, slope):
    rows = LEN
    blocks = branch.shape[2] // (2 * BS)
    channels = blocks * BS
    flat = lambda n, me: (0, n)
    cube = lambda n, me: (0, 0, n)
    return pl.pallas_call(
        mixing_backward_kernel,
        grid_spec=pltpu.PrefetchScalarGridSpec(
            num_scalar_prefetch=1,
            grid=(blocks,),
            in_specs=[
                pl.BlockSpec((4, rows // 4, BS), cube),
                pl.BlockSpec((4, rows // 4, 2 * BS), cube),
                pl.BlockSpec((rows, BS), flat),
                pl.BlockSpec((rows, BS), flat),
                pl.BlockSpec((rows, BS), flat),
                pl.BlockSpec((rows, BS), flat),
                pl.BlockSpec((rows, BS), lambda n, me: (0, 0)),
                pl.BlockSpec((8, BS), flat),
                pl.BlockSpec((2 * BS, BS), flat),
                pl.BlockSpec((8, BS), flat),
                pl.BlockSpec((8, BS), flat),
            ],
            out_specs=[
                pl.BlockSpec((4, rows // 4, 2 * BS), cube),
                pl.BlockSpec((1, 2 * BS, BS), lambda n, me: (n, 0, 0)),
                pl.BlockSpec((8, BS), flat),
            ],
            scratch_shapes=[
                pltpu.VMEM((rows + 8, BS), f32),
                pltpu.VMEM((rows + 16, BS), jnp.int32),
                pltpu.VMEM((rows + 8, BS), f32),
                pltpu.VMEM((rows + 8, BS), f32),
                pltpu.VMEM((rows, BS), f32),
                pltpu.VMEM((rows, BS), f32),
                pltpu.VMEM((rows, 2 * BS), bf16),
                pltpu.VMEM((rows + 8, BS), f32),
            ],
        ),
        out_shape=[
            jax.ShapeDtypeStruct((4, rows // 4, 2 * channels), bf16),
            jax.ShapeDtypeStruct((blocks, 2 * BS, BS), f32),
            jax.ShapeDtypeStruct((8, channels), f32),
        ],
        cost_estimate=pl.CostEstimate(flops=2 * rows * channels * 512, bytes_accessed=48_000_000, transcendentals=0),
        name="mixing_backward",
    )(me, grad_gated, branch, states, conv, sig_r, sig_i, ids, taps, gates, rate, slope)


def folded(count):
    return list(range(0, 1)) + list(range(1, count, 2)) + list(range((count - 1) // 2 * 2, 0, -2))


class Links:
    def __init__(self, dp, mp):
        assert mp == 4 and dp % 2 == 0
        self.dp, self.mp = dp, mp
        self.line = dp // 2
        self.order = folded(self.line)
        self.place = {a: k for k, a in enumerate(self.order)}
        self.ring = [
            (2 * a + b, 2 * self.order[(self.place[a] + 1) % self.line] + b)
            for a in range(self.line)
            for b in range(2)
        ]

    def to_core(self, v):
        return lax.ppermute(v, "mp", [(i, i ^ 1) for i in range(self.mp)])

    def to_x(self, v):
        return lax.ppermute(v, "mp", [(i, i ^ 2) for i in range(self.mp)])

    def to_pair(self, v):
        return lax.ppermute(v, "dp", [(i, i ^ 1) for i in range(self.dp)])

    def along(self, v):
        return lax.ppermute(v, "dp", self.ring)

    def behind(self, me, steps):
        table = np.zeros((self.dp,), np.int32)
        for i in range(self.dp):
            table[i] = self.order[(self.place[i // 2] - steps) % self.line]
        return jnp.asarray(table)[me]


def gather_rows(links, me, shard):
    rows, columns = shard.shape
    pair = lax.bitwise_and(me, 1)
    whole = jnp.zeros((links.dp, rows, columns), shard.dtype)
    moving = shard
    for step in range(links.line):
        other = links.to_pair(moving)
        following = links.along(moving) if step < links.line - 1 else None
        base = 2 * links.behind(me, step)
        whole = lax.dynamic_update_slice(whole, moving[None], (base + pair, 0, 0))
        whole = lax.dynamic_update_slice(whole, other[None], (base + 1 - pair, 0, 0))
        moving = following
    return whole


def scatter_rows(links, me, parts):
    pair = lax.bitwise_and(me, 1)
    take = lambda line, bit: lax.dynamic_index_in_dim(parts, 2 * line + bit, 0, keepdims=False)
    moving = None
    for step in range(links.line):
        line = links.behind(me, step + 1)
        received = links.to_pair(take(line, 1 - pair).astype(bf16))
        total = take(line, pair).astype(f32) + received.astype(f32)
        if moving is not None:
            total = total + moving.astype(f32)
        if step < links.line - 1:
            moving = links.along(total.astype(bf16))
    return total


def gather_tokens(links, v):
    core = links.to_core(v)
    x = links.to_x(v)
    return core, links.to_core(x), v, x


def scatter_tokens(links, partial):
    sent = links.to_core(partial[0:2].astype(bf16))
    kept = partial[2:4].astype(f32) + sent.astype(f32)
    return kept[0] + links.to_x(kept[1].astype(bf16)).astype(f32)


def all_sum(v, axis, count):
    step = 1
    while step < count:
        v = v + lax.ppermute(v, axis, [(i, i ^ step) for i in range(count)])
        step *= 2
    return v


def body(links, block_in, doc_ids, mix_gain, proj_x, proj_y, conv_taps, recur_gate, input_gate, decay_param,
         proj_out, ffn_gain, ffn_gate, ffn_up, ffn_down, out_grad):
    micro_count, own_rows, width = block_in.shape
    group_rows = doc_ids.shape[1]
    assert group_rows == LEN and own_rows * 4 == group_rows
    d_rows, channels = proj_x.shape
    blocks = channels // BS
    hidden_units = ffn_gate.shape[1]
    gate_columns = recur_gate.shape[2]
    dp_me = lax.axis_index("dp")
    mp_me = lax.axis_index("mp")
    me = mp_me.astype(jnp.int32).reshape(1)
    gain_one = mix_gain.astype(f32)
    gain_two = ffn_gain.astype(f32)
    decay_values = decay_param.astype(f32)
    rate = jnp.broadcast_to((-decay_scale * jax.nn.softplus(-decay_values))[None], (8, channels))
    slope = jnp.broadcast_to((decay_scale * jax.nn.sigmoid(-decay_values))[None], (8, channels))
    taps = jnp.concatenate([conv_taps.astype(f32), jnp.zeros((8 - KW, channels), f32)])

    both = jnp.stack([proj_x.reshape(d_rows, blocks, BS), proj_y.reshape(d_rows, blocks, BS)], axis=2)
    gates_t = jnp.stack([recur_gate, input_gate], axis=1)
    gates_t = jnp.transpose(gates_t, (3, 1, 0, 2)).reshape(-1, 2 * channels)
    first = gather_rows(links, dp_me, jnp.concatenate([both.reshape(d_rows, 2 * channels), gates_t]))
    w_branch = first[:, :d_rows].reshape(width, 2 * channels)
    gates = first[:, d_rows:].reshape(links.dp * gate_columns, 2, blocks, BS)
    gates = jnp.transpose(gates, (2, 1, 0, 3)).reshape(blocks, 2 * BS, BS)
    gates = jnp.transpose(gates, (1, 0, 2)).reshape(2 * BS, blocks * BS)
    w_out = gather_rows(links, dp_me, proj_out.T).reshape(width, channels)
    w_up = gather_rows(links, dp_me, jnp.concatenate([ffn_gate, ffn_up], axis=1)).reshape(width, 2 * hidden_units)
    w_down = gather_rows(links, dp_me, ffn_down.T).reshape(width, hidden_units)

    xin = block_in.astype(f32)
    inverse_one = lax.rsqrt(jnp.mean(xin * xin, axis=-1, keepdims=True) + norm_eps)
    unit_one = xin * inverse_one
    normed = (unit_one * gain_one).astype(bf16)
    normed_parts = gather_tokens(links, normed)
    cot_parts = gather_tokens(links, out_grad)

    outputs, input_grads = [], []
    keep = []
    for micro in range(micro_count):
        normed_all = jnp.concatenate([part[micro] for part in normed_parts])
        branch = project(normed_all, w_branch).reshape(4, own_rows, 2 * channels)
        ids = jnp.broadcast_to(doc_ids[micro][:, None], (group_rows, BS))
        gated, states, conv, sig_r, sig_i = mixing_forward(me, branch, ids, taps, gates, rate)
        gated = gated.reshape(group_rows, channels)
        middle = xin[micro] + scatter_tokens(
            links, against(gated, w_out).astype(bf16).reshape(4, own_rows, width))
        inverse_two = lax.rsqrt(jnp.mean(middle * middle, axis=-1, keepdims=True) + norm_eps)
        unit_two = middle * inverse_two
        normed_two = (unit_two * gain_two).astype(bf16)
        normed_two_all = jnp.concatenate(gather_tokens(links, normed_two))
        pre = project(normed_two_all, w_up)
        gate_pre, up_pre = pre[:, :hidden_units], pre[:, hidden_units:]
        gelu_gate, gelu_slope = gelu_parts(gate_pre)
        hidden = (gelu_gate * up_pre).astype(bf16)
        down = scatter_tokens(links, against(hidden, w_down).astype(bf16).reshape(4, own_rows, width))
        outputs.append((middle + down).astype(bf16))
        cot_all = jnp.concatenate([part[micro] for part in cot_parts])
        grad_hidden = project(cot_all, w_down)
        grad_pre = jnp.concatenate(
            [(grad_hidden * up_pre * gelu_slope).astype(bf16), (grad_hidden * gelu_gate).astype(bf16)], axis=1)
        grad_normed_two = scatter_tokens(
            links, against(grad_pre, w_up).astype(bf16).reshape(4, own_rows, width))
        grad_middle = out_grad[micro].astype(f32) + norm_back(grad_normed_two, unit_two, inverse_two, gain_two)
        gain_two_part = jnp.sum(grad_normed_two * unit_two, axis=0)
        grad_mid_all = jnp.concatenate(gather_tokens(links, grad_middle.astype(bf16)))
        grad_gated = project(grad_mid_all, w_out).reshape(4, own_rows, channels)
        grad_branch, grad_gates, small = mixing_backward(
            me, grad_gated, branch, states, conv, sig_r, sig_i, ids, taps, gates, rate, slope)
        grad_branch = grad_branch.reshape(group_rows, 2 * channels)
        grad_normed = scatter_tokens(
            links, against(grad_branch, w_branch).astype(bf16).reshape(4, own_rows, width))
        input_grads.append(grad_middle + norm_back(grad_normed, unit_one[micro], inverse_one[micro], gain_one))
        gain_one_part = jnp.sum(grad_normed * unit_one[micro], axis=0)
        keep.append((normed_two_all, grad_pre, cot_all, hidden, grad_mid_all, gated, normed_all, grad_branch,
                     grad_gates, small, gain_one_part, gain_two_part))

    def weight_grad(left, right):
        total = inner(keep[0][left], keep[0][right])
        for kept in keep[1:]:
            total = total + inner(kept[left], kept[right])
        return total.reshape(links.dp, d_rows, -1)

    def added(at):
        total = keep[0][at]
        for kept in keep[1:]:
            total = total + kept[at]
        return total

    up_grad = scatter_rows(links, dp_me, weight_grad(0, 1))
    down_grad = scatter_rows(links, dp_me, weight_grad(2, 3))
    out_grad_w = scatter_rows(links, dp_me, weight_grad(4, 5))
    gate_grads = added(8).reshape(blocks, 2, links.dp, gate_columns, BS)
    gate_grads = jnp.transpose(gate_grads, (2, 3, 1, 0, 4)).reshape(links.dp, -1, 2 * channels)
    first_grad = scatter_rows(links, dp_me, jnp.concatenate([weight_grad(6, 7), gate_grads], axis=1))
    both_grad = first_grad[:d_rows].reshape(d_rows, blocks, 2, BS)
    gate_grad = jnp.transpose(first_grad[d_rows:].reshape(gate_columns, 2, blocks, BS), (1, 2, 3, 0))
    small = all_sum(added(9), "dp", links.dp)
    gains = all_sum(all_sum(jnp.stack([added(10), added(11)]), "mp", links.mp), "dp", links.dp)
    return (
        jnp.stack(outputs),
        jnp.stack(input_grads),
        gains[0],
        both_grad[:, :, 0].reshape(d_rows, channels),
        both_grad[:, :, 1].reshape(d_rows, channels),
        small[0:KW],
        gate_grad[0],
        gate_grad[1],
        small[KW],
        out_grad_w.T,
        gains[1],
        up_grad[:, :hidden_units],
        up_grad[:, hidden_units:],
        down_grad.T,
    )


def solution(mesh):
    links = Links(mesh.shape["dp"], mesh.shape["mp"])
    tokens = P(None, ("dp", "mp"), None)
    rows, columns, gate = P("dp", "mp"), P("mp", "dp"), P("mp", None, "dp")
    return jax.shard_map(
        functools.partial(body, links),
        mesh=mesh,
        in_specs=(tokens, P(None, "dp"), P(), rows, rows, P(None, "mp"), gate, gate, P("mp"), columns, P(), rows,
                  rows, columns, tokens),
        out_specs=(tokens, tokens, P(), rows, rows, P(None, "mp"), gate, gate, P("mp"), columns, P(), rows, rows,
                   columns),
        check_vma=False,
    )
```

```python
import functools

import jax
import jax.numpy as jnp
import numpy as np
from jax import lax
from jax.experimental import pallas as pl
from jax.experimental.pallas import tpu as pltpu
from jax.sharding import PartitionSpec as P

LEN = 1024
BS = 128
KW = 4
SEGS = 8

norm_eps = 1e-06
root_floor = 0.01
decay_scale = 8.0
gelu_a = 0.7978845608028654
gelu_b = 0.044715

f32 = jnp.float32
bf16 = jnp.bfloat16


BLOCK_AT = (2, 0, 3, 1)


def project(left, right):
    return jnp.dot(left, right, preferred_element_type=f32)


def inner(left, right):
    return lax.dot_general(left, right, (((0,), (0,)), ((), ())), preferred_element_type=f32)


def against(left, right):
    return lax.dot_general(left, right, (((1,), (1,)), ((), ())), preferred_element_type=f32)


def norm_back(grad_normed, unit_rows, inverse, gain):
    scaled = grad_normed * gain
    return inverse * (scaled - unit_rows * jnp.mean(scaled * unit_rows, axis=-1, keepdims=True))


def gelu_parts(v):
    squared = v * v
    inside = gelu_a * v * (1.0 + gelu_b * squared)
    t = jnp.tanh(inside)
    half = 0.5 * (1.0 + t)
    value = v * half
    slope = half + 0.5 * v * (1.0 - t * t) * (gelu_a * (1.0 + 3.0 * gelu_b * squared))
    return value, slope


def gelu_value(v):
    return 0.5 * v * (1.0 + jnp.tanh(gelu_a * v * (1.0 + gelu_b * v * v)))


def place_of(me, block):
    differ = lax.bitwise_xor(me, block)
    low = lax.bitwise_and(differ, 1)
    high = lax.shift_right_logical(differ, 1)
    return 2 * (1 - low) + high


CHUNK = 64


def mixing_forward_kernel(me_ref, branch, ids, taps, gates, rate, gated, states, conv, sig_r, sig_i,
                          xpad, idpad, a_buf, b_buf, p_buf):
    rows = LEN
    quarter = rows // 4
    me = me_ref[0]
    xpad[0:8, :] = jnp.zeros((8, BS), f32)
    idpad[0:8, :] = jnp.full((8, BS), -1, jnp.int32)
    idpad[8:8 + rows, :] = ids[...]
    for block in range(4):
        at = place_of(me, block)
        xpad[8 + block * quarter: 8 + (block + 1) * quarter, :] = branch[at, :, 0:BS]
    rate_row = rate[0:1, :]

    def convolve(step, _):
        base = step * CHUNK
        own_ids = idpad[pl.ds(base + 8, CHUNK), :]
        total = taps[0:1, :] * xpad[pl.ds(base + 8, CHUNK), :]
        for k in range(1, KW):
            same = idpad[pl.ds(base + 8 - k, CHUNK), :] == own_ids
            total = total + taps[k:k + 1, :] * jnp.where(same, xpad[pl.ds(base + 8 - k, CHUNK), :], 0.0)
        conv[pl.ds(base, CHUNK), :] = total.astype(bf16)
        return 0

    lax.fori_loop(0, rows // CHUNK, convolve, 0, unroll=2)

    logits = lax.dot_general(conv[...], gates[...], (((1,), (1,)), ((), ())), preferred_element_type=f32)
    a_buf[...] = logits[:, 0:BS]
    b_buf[...] = logits[:, BS:2 * BS]

    def gate(step, _):
        base = step * CHUNK
        here = pl.ds(base, CHUNK)
        sr = jax.nn.sigmoid(a_buf[here, :])
        si = jax.nn.sigmoid(b_buf[here, :])
        sig_r[here, :] = sr
        sig_i[here, :] = si
        same = idpad[pl.ds(base + 7, CHUNK), :] == idpad[pl.ds(base + 8, CHUNK), :]
        decay = jnp.exp(rate_row * sr)
        margin = jnp.maximum(1.0 - decay * decay, root_floor)
        multiplier = jnp.where(same, jnp.sqrt(margin), 1.0)
        b_buf[here, :] = conv[here, :].astype(f32) * si * multiplier
        a_buf[here, :] = jnp.where(same, decay, 0.0)
        return 0

    lax.fori_loop(0, rows // CHUNK, gate, 0, unroll=2)

    seg = rows // SEGS

    def scan(step, carry):
        h, p = carry
        rows_at = pl.ds(step, SEGS, stride=seg)
        a = a_buf[rows_at, :]
        h = a * h + b_buf[rows_at, :]
        p = a * p
        b_buf[rows_at, :] = h
        p_buf[rows_at, :] = p
        return h, p

    h, p = lax.fori_loop(0, seg, scan, (jnp.zeros((SEGS, BS), f32), jnp.ones((SEGS, BS), f32)), unroll=8)
    carry = jnp.zeros((1, BS), f32)
    for s in range(SEGS):
        at = place_of(me, s // 2)
        inside = (s % 2) * seg
        for c in range(seg // CHUNK):
            here = slice(s * seg + c * CHUNK, s * seg + (c + 1) * CHUNK)
            state = b_buf[here, :] + p_buf[here, :] * carry
            states[here, :] = state
            there = slice(inside + c * CHUNK, inside + (c + 1) * CHUNK)
            gated[at, there, :] = (state * gelu_value(branch[at, there, BS:2 * BS])).astype(bf16)
        carry = h[s:s + 1, :] + p[s:s + 1, :] * carry


def mixing_backward_kernel(me_ref, grad_gated, branch, states, conv, sig_r, sig_i, ids, taps, gates, rate, slope,
                           grad_branch, grad_gates, small,
                           xpad, idpad, spad, a_buf, g_buf, p_buf, low, gcpad):
    rows = LEN
    quarter = rows // 4
    me = me_ref[0]
    zero8 = jnp.zeros((8, BS), f32)
    xpad[0:8, :] = zero8
    spad[0:8, :] = zero8
    spad[8:8 + rows, :] = states[...]
    idpad[0:8, :] = jnp.full((8, BS), -1, jnp.int32)
    idpad[8:8 + rows, :] = ids[...]
    idpad[8 + rows:16 + rows, :] = jnp.full((8, BS), -1, jnp.int32)
    a_buf[rows:rows + 8, :] = zero8
    gcpad[rows:rows + 8, :] = zero8
    rate_row = rate[0:1, :]
    slope_row = slope[0:1, :]
    per = quarter // CHUNK
    for block in range(4):
        at = place_of(me, block)
        xpad[8 + block * quarter: 8 + (block + 1) * quarter, :] = branch[at, :, 0:BS]

        def enter(step, _, at=at, block=block):
            there = pl.ds(step * CHUNK, CHUNK)
            base = block * quarter + step * CHUNK
            here = pl.ds(base, CHUNK)
            value, gradient = gelu_parts(branch[at, there, BS:2 * BS])
            incoming = grad_gated[at, there, :]
            g_buf[here, :] = incoming * value
            grad_branch[at, there, BS:2 * BS] = (gradient * states[here, :] * incoming).astype(bf16)
            same = idpad[pl.ds(base + 7, CHUNK), :] == idpad[pl.ds(base + 8, CHUNK), :]
            a_buf[here, :] = jnp.where(same, jnp.exp(rate_row * sig_r[here, :]), 0.0)
            return 0

        lax.fori_loop(0, per, enter, 0, unroll=2)

    seg = rows // SEGS

    def scan(step, carry):
        h, p = carry
        t = seg - 1 - step
        a = a_buf[pl.ds(t + 1, SEGS, stride=seg), :]
        rows_at = pl.ds(t, SEGS, stride=seg)
        h = a * h + g_buf[rows_at, :]
        p = a * p
        g_buf[rows_at, :] = h
        p_buf[rows_at, :] = p
        return h, p

    h, p = lax.fori_loop(0, seg, scan, (jnp.zeros((SEGS, BS), f32), jnp.ones((SEGS, BS), f32)), unroll=8)

    carry = jnp.zeros((1, BS), f32)
    decay_sum = jnp.zeros((8, BS), f32)
    for s in reversed(range(SEGS)):

        def leave(step, acc, s=s, carry=carry):
            base = s * seg + step * CHUNK
            here = pl.ds(base, CHUNK)
            g = g_buf[here, :] + p_buf[here, :] * carry
            grad_carried = g * spad[pl.ds(base + 7, CHUNK), :]
            same = idpad[pl.ds(base + 7, CHUNK), :] == idpad[pl.ds(base + 8, CHUNK), :]
            decay = a_buf[here, :]
            square = decay * decay
            inside = 1.0 - square
            root = jnp.sqrt(jnp.maximum(inside, root_floor))
            sr = sig_r[here, :]
            si = sig_i[here, :]
            cv = conv[here, :].astype(f32)
            multiplier = jnp.where(same, root, 1.0)
            gsi = g * si
            gcsi = gsi * cv
            grad_log = jnp.where(
                same,
                grad_carried * decay - jnp.where(inside > root_floor, gcsi * square / root, 0.0),
                0.0,
            )
            gcpad[here, :] = gsi * multiplier
            weighted = grad_log * sr
            low[here, 0:BS] = (weighted * (1.0 - sr) * rate_row).astype(bf16)
            low[here, BS:2 * BS] = (gcsi * multiplier * (1.0 - si)).astype(bf16)
            return acc + jnp.sum(weighted.reshape(CHUNK // 8, 8, BS), axis=0)

        decay_sum = lax.fori_loop(0, seg // CHUNK, leave, decay_sum, unroll=2)
        carry = h[s:s + 1, :] + p[s:s + 1, :] * carry

    grad_gates[0] = lax.dot_general(low[...], conv[...], (((0,), (0,)), ((), ())), preferred_element_type=f32)
    p_buf[...] = lax.dot_general(low[...], gates[...], (((1,), (0,)), ((), ())), preferred_element_type=f32)

    def add_gates(step, _):
        here = pl.ds(step * CHUNK, CHUNK)
        gcpad[here, :] = gcpad[here, :] + p_buf[here, :]
        return 0

    lax.fori_loop(0, rows // CHUNK, add_gates, 0, unroll=2)

    sums = tuple(jnp.zeros((8, BS), f32) for _ in range(KW))
    for block in range(4):
        at = place_of(me, block)

        def finish(step, sums, at=at, block=block):
            there = pl.ds(step * CHUNK, CHUNK)
            base = block * quarter + step * CHUNK
            gc = gcpad[pl.ds(base, CHUNK), :]
            own_ids = idpad[pl.ds(base + 8, CHUNK), :]
            fold = lambda v: jnp.sum(v.reshape(CHUNK // 8, 8, BS), axis=0)
            new = [sums[0] + fold(gc * xpad[pl.ds(base + 8, CHUNK), :])]
            grad_x = taps[0:1, :] * gc
            for k in range(1, KW):
                same = idpad[pl.ds(base + 8 - k, CHUNK), :] == own_ids
                new.append(sums[k] + fold(jnp.where(same, gc * xpad[pl.ds(base + 8 - k, CHUNK), :], 0.0)))
                after = idpad[pl.ds(base + 8 + k, CHUNK), :] == own_ids
                grad_x = grad_x + taps[k:k + 1, :] * jnp.where(after, gcpad[pl.ds(base + k, CHUNK), :], 0.0)
            grad_branch[at, there, 0:BS] = grad_x.astype(bf16)
            return tuple(new)

        sums = lax.fori_loop(0, per, finish, sums, unroll=2)
    small[...] = jnp.zeros((8, BS), f32)
    for k in range(KW):
        small[k:k + 1, :] = jnp.sum(sums[k], axis=0, keepdims=True)
    small[KW:KW + 1, :] = jnp.sum(decay_sum, axis=0, keepdims=True) * slope_row


def mixing_forward(me, branch, ids, taps, gates, rate):
    rows = LEN
    blocks = branch.shape[2] // (2 * BS)
    channels = blocks * BS
    flat = lambda n, me: (0, n)
    return pl.pallas_call(
        mixing_forward_kernel,
        grid_spec=pltpu.PrefetchScalarGridSpec(
            num_scalar_prefetch=1,
            grid=(blocks,),
            in_specs=[
                pl.BlockSpec((4, rows // 4, 2 * BS), lambda n, me: (0, 0, n)),
                pl.BlockSpec((rows, BS), lambda n, me: (0, 0)),
                pl.BlockSpec((8, BS), flat),
                pl.BlockSpec((2 * BS, BS), flat),
                pl.BlockSpec((8, BS), flat),
            ],
            out_specs=[
                pl.BlockSpec((4, rows // 4, BS), lambda n, me: (0, 0, n)),
                pl.BlockSpec((rows, BS), flat),
                pl.BlockSpec((rows, BS), flat),
                pl.BlockSpec((rows, BS), flat),
                pl.BlockSpec((rows, BS), flat),
            ],
            scratch_shapes=[
                pltpu.VMEM((rows + 8, BS), f32),
                pltpu.VMEM((rows + 8, BS), jnp.int32),
                pltpu.VMEM((rows, BS), f32),
                pltpu.VMEM((rows, BS), f32),
                pltpu.VMEM((rows, BS), f32),
            ],
        ),
        out_shape=[
            jax.ShapeDtypeStruct((4, rows // 4, channels), bf16),
            jax.ShapeDtypeStruct((rows, channels), f32),
            jax.ShapeDtypeStruct((rows, channels), bf16),
            jax.ShapeDtypeStruct((rows, channels), f32),
            jax.ShapeDtypeStruct((rows, channels), f32),
        ],
        cost_estimate=pl.CostEstimate(flops=2 * rows * channels * 256, bytes_accessed=24_000_000, transcendentals=0),
        name="mixing_forward",
    )(me, branch, ids, taps, gates, rate)


def mixing_backward(me, grad_gated, branch, states, conv, sig_r, sig_i, ids, taps, gates, rate, slope):
    rows = LEN
    blocks = branch.shape[2] // (2 * BS)
    channels = blocks * BS
    flat = lambda n, me: (0, n)
    cube = lambda n, me: (0, 0, n)
    return pl.pallas_call(
        mixing_backward_kernel,
        grid_spec=pltpu.PrefetchScalarGridSpec(
            num_scalar_prefetch=1,
            grid=(blocks,),
            in_specs=[
                pl.BlockSpec((4, rows // 4, BS), cube),
                pl.BlockSpec((4, rows // 4, 2 * BS), cube),
                pl.BlockSpec((rows, BS), flat),
                pl.BlockSpec((rows, BS), flat),
                pl.BlockSpec((rows, BS), flat),
                pl.BlockSpec((rows, BS), flat),
                pl.BlockSpec((rows, BS), lambda n, me: (0, 0)),
                pl.BlockSpec((8, BS), flat),
                pl.BlockSpec((2 * BS, BS), flat),
                pl.BlockSpec((8, BS), flat),
                pl.BlockSpec((8, BS), flat),
            ],
            out_specs=[
                pl.BlockSpec((4, rows // 4, 2 * BS), cube),
                pl.BlockSpec((1, 2 * BS, BS), lambda n, me: (n, 0, 0)),
                pl.BlockSpec((8, BS), flat),
            ],
            scratch_shapes=[
                pltpu.VMEM((rows + 8, BS), f32),
                pltpu.VMEM((rows + 16, BS), jnp.int32),
                pltpu.VMEM((rows + 8, BS), f32),
                pltpu.VMEM((rows + 8, BS), f32),
                pltpu.VMEM((rows, BS), f32),
                pltpu.VMEM((rows, BS), f32),
                pltpu.VMEM((rows, 2 * BS), bf16),
                pltpu.VMEM((rows + 8, BS), f32),
            ],
        ),
        out_shape=[
            jax.ShapeDtypeStruct((4, rows // 4, 2 * channels), bf16),
            jax.ShapeDtypeStruct((blocks, 2 * BS, BS), f32),
            jax.ShapeDtypeStruct((8, channels), f32),
        ],
        cost_estimate=pl.CostEstimate(flops=2 * rows * channels * 512, bytes_accessed=48_000_000, transcendentals=0),
        name="mixing_backward",
    )(me, grad_gated, branch, states, conv, sig_r, sig_i, ids, taps, gates, rate, slope)


def folded(count):
    return list(range(0, 1)) + list(range(1, count, 2)) + list(range((count - 1) // 2 * 2, 0, -2))


class Links:
    def __init__(self, dp, mp):
        assert mp == 4 and dp % 2 == 0
        self.dp, self.mp = dp, mp
        self.line = dp // 2
        self.order = folded(self.line)
        self.place = {a: k for k, a in enumerate(self.order)}
        self.ring = [
            (2 * a + b, 2 * self.order[(self.place[a] + 1) % self.line] + b)
            for a in range(self.line)
            for b in range(2)
        ]

    def to_core(self, v):
        return lax.ppermute(v, "mp", [(i, i ^ 1) for i in range(self.mp)])

    def to_x(self, v):
        return lax.ppermute(v, "mp", [(i, i ^ 2) for i in range(self.mp)])

    def to_pair(self, v):
        return lax.ppermute(v, "dp", [(i, i ^ 1) for i in range(self.dp)])

    def along(self, v):
        return lax.ppermute(v, "dp", self.ring)

    def behind(self, me, steps):
        at = lax.shift_right_logical(me, 1)
        place = jnp.int32(0)
        for a in range(self.line):
            place = jnp.where(at == a, self.order[(self.place[a] - steps) % self.line], place)
        return place.astype(jnp.int32)


def tile_kernel_params():
    return pltpu.CompilerParams(vmem_limit_bytes=60 * 1024 * 1024)


UNIT = 384


def assemble(pieces, whole):
    @pl.when(pl.program_id(0) == 0)
    def _():
        rows = pieces[0].shape[0]
        for k, piece in enumerate(pieces):
            whole[k * rows:(k + 1) * rows, :] = piece[...]


def rows_call(kernel, pieces, more, more_specs, outs, out_specs, grid, flops, name):
    own, width = pieces[0].shape
    whole = pl.BlockSpec((4 * own, width), lambda n: (0, 0))

    def run(*refs):
        assemble(refs[:4], refs[4 + len(more)])
        kernel(refs[4 + len(more)], *refs[4:4 + len(more)], *refs[5 + len(more):])

    moved = sum(2 * v.size * v.dtype.itemsize for v in (*pieces, *more))
    return pl.pallas_call(
        run,
        grid=(grid,),
        in_specs=[pl.BlockSpec((own, width), lambda n: (0, 0))] * 4 + more_specs,
        out_specs=[whole] + out_specs,
        out_shape=[jax.ShapeDtypeStruct((4 * own, width), bf16)] + outs,
        compiler_params=tile_kernel_params(),
        cost_estimate=pl.CostEstimate(flops=flops, bytes_accessed=moved, transcendentals=0),
        name=name,
    )(*pieces, *more)


def project_kernel(x, w, out):
    out[...] = jnp.dot(x[...], w[...], preferred_element_type=f32)


def project_rows(pieces, w, tile, name):
    own, width = pieces[0].shape
    columns = w.shape[1]
    return rows_call(
        project_kernel, pieces, [w], [pl.BlockSpec((width, tile), lambda n: (0, n))],
        [jax.ShapeDtypeStruct((4 * own, columns), f32)], [pl.BlockSpec((4 * own, tile), lambda n: (0, n))],
        columns // tile, 8 * own * width * columns, name)


def ffn_forward_kernel(x, w, hidden, by_gate, by_up):
    both = jnp.dot(x[...], w[...], preferred_element_type=f32)
    up = both[:, UNIT:]
    value, slope = gelu_parts(both[:, :UNIT])
    hidden[...] = (value * up).astype(bf16)
    by_gate[...] = (up * slope).astype(bf16)
    by_up[...] = value.astype(bf16)


def ffn_forward(pieces, w):
    own, width = pieces[0].shape
    units = w.shape[1] // 2
    tile = pl.BlockSpec((4 * own, UNIT), lambda n: (0, n))
    return rows_call(
        ffn_forward_kernel, pieces, [w], [pl.BlockSpec((width, 2 * UNIT), lambda n: (0, n))],
        [jax.ShapeDtypeStruct((4 * own, units), bf16)] * 3, [tile] * 3,
        units // UNIT, 16 * own * width * units, "ffn_forward")


def ffn_backward_kernel(x, w, by_gate, by_up, out):
    grad = jnp.dot(x[...], w[...], preferred_element_type=f32)
    out[:, :UNIT] = (grad * by_gate[...].astype(f32)).astype(bf16)
    out[:, UNIT:] = (grad * by_up[...].astype(f32)).astype(bf16)


def ffn_backward(pieces, w, by_gate, by_up):
    own, width = pieces[0].shape
    units = w.shape[1]
    tile = pl.BlockSpec((4 * own, UNIT), lambda n: (0, n))
    return rows_call(
        ffn_backward_kernel, pieces, [w, by_gate, by_up],
        [pl.BlockSpec((width, UNIT), lambda n: (0, n)), tile, tile],
        [jax.ShapeDtypeStruct((4 * own, 2 * units), bf16)],
        [pl.BlockSpec((4 * own, 2 * UNIT), lambda n: (0, n))],
        units // UNIT, 8 * own * width * units, "ffn_backward")


def pack_kernel(x, y, out, recur, inp, packed):
    rows, channels = x.shape
    columns = recur.shape[2]
    for n in range(channels // BS):
        block = slice(n * BS, (n + 1) * BS)
        packed[0:rows, 2 * n * BS:(2 * n + 1) * BS] = x[:, block]
        packed[0:rows, (2 * n + 1) * BS:(2 * n + 2) * BS] = y[:, block]
        packed[rows:rows + columns, block] = recur[n].astype(f32).T.astype(bf16)
        packed[rows:rows + columns, channels + n * BS:channels + (n + 1) * BS] = inp[n].astype(f32).T.astype(bf16)
    packed[0:rows, 2 * channels:3 * channels] = out[...].astype(f32).T.astype(bf16)
    packed[rows:rows + columns, 2 * channels:3 * channels] = jnp.zeros((columns, channels), bf16)


def pack(x, y, out, recur, inp):
    rows, channels = x.shape
    return pl.pallas_call(
        pack_kernel,
        out_shape=jax.ShapeDtypeStruct((rows + recur.shape[2], 3 * channels), bf16),
        name="pack",
    )(x, y, out, recur, inp)


def weight_grad_kernel(line, shard, extra, groups, table, *refs):
    if extra:
        left_a, right_a, left_b, right_b, extra_a, extra_b, *sent, kept, total = refs
    else:
        left_a, right_a, left_b, right_b, *sent, kept, total = refs
    dims = (((0,), (0,)), ((), ()))
    total[...] = lax.dot_general(
        left_a[...], right_a[...], dims, preferred_element_type=f32
    ) + lax.dot_general(left_b[...], right_b[...], dims, preferred_element_type=f32)
    bit = table[line]
    size = line // groups
    for k in range(line):
        at = 2 * table[k]
        out = sent[k // size]
        mine = pl.ds(pl.multiple_of((at + bit) * shard, 16), shard)
        other = pl.ds(pl.multiple_of((at + 1 - bit) * shard, 16), shard)
        kept[k, 0:shard, :] = total[mine, :]
        out[k % size, 0:shard, :] = total[other, :].astype(bf16)
        if extra:
            kept[k, shard:shard + extra, :] = extra_a[at + bit] + extra_b[at + bit]
            out[k % size, shard:shard + extra, :] = (extra_a[at + 1 - bit] + extra_b[at + 1 - bit]).astype(bf16)


def weight_grad(table, left, right, tile, groups, extras=None):
    line = table.shape[0] - 1
    rows, width = left[0].shape
    columns = right[0].shape[1]
    shard = width // (2 * line)
    extra = extras[0].shape[1] if extras else 0
    lefts = pl.BlockSpec((rows, width), lambda n, t: (0, 0))
    rights = pl.BlockSpec((rows, tile), lambda n, t: (0, n))
    more = [pl.BlockSpec((2 * line, extra, tile), lambda n, t: (0, 0, n))] * 2 if extra else []
    parts = lambda count: pl.BlockSpec((count, shard + extra, tile), lambda n, t: (0, 0, n))
    size = line // groups
    *sent, kept = pl.pallas_call(
        functools.partial(weight_grad_kernel, line, shard, extra, groups),
        grid_spec=pltpu.PrefetchScalarGridSpec(
            num_scalar_prefetch=1,
            grid=(columns // tile,),
            in_specs=[lefts, rights, lefts, rights] + more,
            out_specs=[parts(size)] * groups + [parts(line)],
            scratch_shapes=[pltpu.VMEM((width, tile), f32)],
        ),
        out_shape=[jax.ShapeDtypeStruct((size, shard + extra, columns), bf16)] * groups
        + [jax.ShapeDtypeStruct((line, shard + extra, columns), f32)],
        compiler_params=pltpu.CompilerParams(vmem_limit_bytes=62 * 1024 * 1024),
        cost_estimate=pl.CostEstimate(
            flops=4 * rows * width * columns, bytes_accessed=30_000_000, transcendentals=0),
        name="weight_grad",
    )(table, left[0], right[0], left[1], right[1], *(extras or ()))
    return sent, kept


class Bag(dict):
    def fence(self):
        values, tree = jax.tree.flatten(dict(self))
        values = lax.optimization_barrier(values)
        self.update(jax.tree.unflatten(tree, values))

    def take(self, *names):
        out = [self.pop(name) for name in names]
        return out if len(out) > 1 else out[0]


class Gather:
    def __init__(self, links, me, bag, name, shard, parts=None):
        self.links, self.me, self.bag, self.name = links, me, bag, name
        self.along_steps, self.pair_steps, self.placed, self.other_placed = 0, 0, 0, 0
        self.parts = parts or [(slice(0, shard.shape[0]), slice(0, shard.shape[1]))]
        bag[name] = {"z": [shard], "y": [], "whole": None}

    def along(self, steps=1):
        z = self.bag[self.name]["z"]
        for _ in range(steps):
            if self.along_steps < self.links.line - 1:
                z.append(self.links.along(z[self.along_steps]))
                self.along_steps += 1

    def pair(self, steps=1):
        held = self.bag[self.name]
        for _ in range(steps):
            if self.pair_steps <= self.along_steps and self.pair_steps < self.links.line:
                held["y"].append(self.links.to_pair(held["z"][self.pair_steps]))
                self.pair_steps += 1

    def put(self, pieces, at, bit):
        held = self.bag[self.name]
        base = 2 * self.links.behind(self.me, at)
        wholes = []
        for k, (rows, columns) in enumerate(self.parts):
            piece = pieces[at][rows, columns][None]
            whole = jnp.zeros((self.links.dp,) + piece.shape[1:], bf16) if held["whole"] is None else held["whole"][k]
            wholes.append(lax.dynamic_update_slice(whole, piece, (base + bit, 0, 0)))
        held["whole"] = wholes

    def place(self, z=0, y=0):
        held = self.bag[self.name]
        bit = lax.bitwise_and(self.me, 1)
        for _ in range(z):
            if self.placed < self.links.line:
                self.put(held["z"], self.placed, bit)
                self.placed += 1
        for _ in range(y):
            if self.other_placed < self.links.line:
                self.put(held["y"], self.other_placed, 1 - bit)
                self.other_placed += 1
        for k in range(min(self.placed, self.pair_steps, self.along_steps)):
            held["z"][k] = None
        for k in range(self.other_placed):
            held["y"][k] = None

    def finish(self):
        line = self.links.line
        while self.pair_steps < line:
            self.along()
            self.pair()
        self.place(line, line)
        return self.bag.pop(self.name)["whole"]


class Scatter:
    def __init__(self, links, bag, name, sent, kept):
        self.links, self.bag, self.name = links, bag, name
        self.pair_steps, self.along_steps = 0, 0
        self.size = links.line // len(sent)
        bag[name] = {"sent": list(sent), "kept": kept, "moving": None}

    def pair(self):
        sent = self.bag[self.name]["sent"]
        if self.pair_steps < len(sent):
            sent[self.pair_steps] = self.links.to_pair(sent[self.pair_steps])
            self.pair_steps += 1

    def along(self):
        held = self.bag[self.name]
        at = self.along_steps
        if at < self.links.line - 1 and at // self.size < self.pair_steps:
            held["moving"] = self.links.along(self.sum_here().astype(bf16))
            self.along_steps += 1

    def sum_here(self):
        held = self.bag[self.name]
        at = self.along_steps
        total = held["kept"][at] + held["sent"][at // self.size][at % self.size].astype(f32)
        if held["moving"] is not None:
            total = total + held["moving"].astype(f32)
        return total

    def finish(self):
        while self.pair_steps < len(self.bag[self.name]["sent"]):
            self.pair()
        while self.along_steps < self.links.line - 1:
            self.along()
        total = self.sum_here()
        self.bag.pop(self.name)
        return total


class AllSum:
    def __init__(self, bag, name, value, axes):
        self.bag, self.name = bag, name
        self.steps = [(axis, count, 1 << k) for axis, count in axes for k in range(count.bit_length() - 1)]
        assert all(count & (count - 1) == 0 for _, count in axes)
        bag[name] = value

    def step(self):
        if self.steps:
            axis, count, bit = self.steps.pop(0)
            value = self.bag[self.name]
            self.bag[self.name] = value + lax.ppermute(value, axis, [(i, i ^ bit) for i in range(count)])

    def finish(self):
        while self.steps:
            self.step()
        return self.bag.pop(self.name)


def body(links, block_in, doc_ids, mix_gain, proj_x, proj_y, conv_taps, recur_gate, input_gate, decay_param,
         proj_out, ffn_gain, ffn_gate, ffn_up, ffn_down, out_grad):
    micro_count, own_rows, width = block_in.shape
    group_rows = doc_ids.shape[1]
    assert group_rows == LEN and own_rows * 4 == group_rows and micro_count == 2
    d_rows, channels = proj_x.shape
    blocks = channels // BS
    hidden_units = ffn_gate.shape[1]
    assert hidden_units % UNIT == 0
    gate_columns = recur_gate.shape[2]
    dp_me = lax.axis_index("dp")
    me = lax.axis_index("mp").astype(jnp.int32).reshape(1)
    gain_one = mix_gain.astype(f32)
    gain_two = ffn_gain.astype(f32)
    to_core, to_x = links.to_core, links.to_x
    halves = lambda v: v.reshape(4, own_rows, width)
    bag = Bag()

    def exchange(name, partial):
        partial = halves(partial)
        kept = partial[2:4].astype(f32) + to_core(partial[0:2]).astype(f32)
        bag[name + "_own"], bag[name + "_x"] = kept[0], kept[1].astype(bf16)

    def summed(name):
        return bag.pop(name + "_own") + bag.pop(name + "_x").astype(f32)

    def across(name):
        bag[name + "_x"] = to_x(bag[name + "_x"])

    def rows_of(name):
        own, core, x, diagonal = bag.take(name, name + "_core", name + "_x", name + "_diagonal")
        return core, diagonal, own, x

    packed = pack(proj_x, proj_y, proj_out, recur_gate, input_gate)
    inner_rows, outer_rows = slice(0, d_rows), slice(d_rows, d_rows + gate_columns)
    wide, narrow = slice(0, 2 * channels), slice(2 * channels, 3 * channels)
    first = Gather(links, dp_me, bag, "first", packed, [(inner_rows, wide), (inner_rows, narrow), (outer_rows, wide)])
    bag.fence()

    first.along()
    first.pair()
    for micro in range(2):
        xin = block_in[micro].astype(f32)
        inverse = lax.rsqrt(jnp.mean(xin * xin, axis=-1, keepdims=True) + norm_eps)
        bag[f"inverse_one{micro}"] = inverse
        bag[f"normed{micro}"] = (xin * inverse * gain_one).astype(bf16)
    bag["cot0"], bag["cot1"] = out_grad[0], out_grad[1]
    bag.fence()

    first.along()
    first.pair()
    bag["normed0_x"] = to_x(bag["normed0"])
    bag["normed0_core"] = to_core(bag["normed0"])
    first.place(2, 1)
    decay_values = decay_param.astype(f32)
    bag["rate"] = jnp.broadcast_to((-decay_scale * jax.nn.softplus(-decay_values))[None], (8, channels))
    bag["slope"] = jnp.broadcast_to((decay_scale * jax.nn.sigmoid(-decay_values))[None], (8, channels))
    bag["taps"] = jnp.concatenate([conv_taps.astype(f32), jnp.zeros((8 - KW, channels), f32)])
    bag["table"] = jnp.stack(
        [links.behind(dp_me, step + 1) for step in range(links.line)] + [lax.bitwise_and(dp_me, 1).astype(jnp.int32)])
    bag.fence()

    first.along()
    first.pair()
    bag["normed1_x"] = to_x(bag["normed1"])
    bag["normed0_diagonal"] = to_core(bag["normed0_x"])
    first.place(1, 1)
    gate_up = jnp.stack([ffn_gate.reshape(d_rows, -1, UNIT), ffn_up.reshape(d_rows, -1, UNIT)], axis=2)
    second = Gather(links, dp_me, bag, "second", gate_up.reshape(d_rows, 2 * hidden_units))
    third = Gather(links, dp_me, bag, "third", ffn_down.T)
    for micro in range(2):
        bag[f"ids{micro}"] = jnp.broadcast_to(doc_ids[micro][:, None], (group_rows, BS))
    bag.fence()

    first.pair()
    second.along()
    bag["normed1_core"] = to_core(bag["normed1"])
    bag["normed1_diagonal"] = to_core(bag["normed1_x"])
    bag["cot0_x"] = to_x(bag["cot0"])
    first.place(1, 1)
    bag.fence()

    def mix(micro):
        bag[f"normed_all{micro}"], branch = project_rows(rows_of(f"normed{micro}"), bag["w_branch"], 512, "branch")
        branch = branch.reshape(4, own_rows, 2 * channels)
        gated, *rest = mixing_forward(me, branch, bag[f"ids{micro}"], bag["taps"], bag["gates"], bag["rate"])
        gated = gated.reshape(group_rows, channels)
        bag[f"mixed{micro}"] = [branch] + rest
        bag[f"gated{micro}"] = gated
        bag[f"partial{micro}"] = against(gated, bag["w_out"]).astype(bf16)

    def middle_of(micro):
        middle = block_in[micro].astype(f32) + summed(f"first{micro}")
        inverse = lax.rsqrt(jnp.mean(middle * middle, axis=-1, keepdims=True) + norm_eps)
        bag[f"middle{micro}"], bag[f"inverse_two{micro}"] = middle, inverse
        bag[f"two{micro}"] = (middle * inverse * gain_two).astype(bf16)

    second.along()
    second.pair()
    bag["cot1_x"] = to_x(bag["cot1"])
    w_branch, w_out, gates = first.finish()
    bag["w_branch"] = w_branch.reshape(width, 2 * channels)
    gates = gates.reshape(links.dp * gate_columns, 2, blocks, BS)
    bag["gates"] = jnp.transpose(gates, (1, 0, 2, 3)).reshape(2 * BS, blocks * BS)
    bag["w_out"] = w_out.reshape(width, channels)
    mix(0)
    bag.fence()

    exchange("first0", bag.pop("partial0"))
    second.place(2, 1)
    bag.fence()

    second.along()
    second.pair()
    across("first0")
    mix(1)
    bag.fence()

    exchange("first1", bag.pop("partial1"))
    second.place(1, 1)
    bag.fence()

    third.along()
    second.pair()
    across("first1")
    bag["cot0_diagonal"] = to_core(bag["cot0_x"])
    middle_of(0)
    second.place(1)
    bag.fence()

    third.along()
    second.pair()
    bag["two0_x"] = to_x(bag["two0"])
    bag["two0_core"] = to_core(bag["two0"])
    middle_of(1)
    second.place(0, 1)
    third.place(2)
    bag.fence()

    def forward(micro):
        bag[f"two_all{micro}"], bag[f"hidden{micro}"], *bag[f"by{micro}"] = ffn_forward(
            rows_of(f"two{micro}"), bag["w_up"])

    third.along()
    third.pair()
    bag["two1_x"] = to_x(bag["two1"])
    bag["two0_diagonal"] = to_core(bag["two0_x"])
    bag["w_up"] = second.finish()[0].reshape(width, 2 * hidden_units)
    third.place(1)
    forward(0)
    bag.fence()

    third.pair(3)
    bag["two1_core"] = to_core(bag["two1"])
    bag["two1_diagonal"] = to_core(bag["two1_x"])
    third.place(1, 1)
    forward(1)
    bag.fence()

    def back_of(micro):
        bag[f"cot_all{micro}"], bag[f"grad_pre{micro}"] = ffn_backward(
            rows_of(f"cot{micro}"), bag["w_down"], *bag.pop(f"by{micro}"))
        bag[f"partial{micro}"] = against(bag[f"grad_pre{micro}"], bag["w_up"]).astype(bf16)

    def down_of(micro):
        bag[f"down_partial{micro}"] = against(bag[f"hidden{micro}"], bag["w_down"]).astype(bf16)

    def grad_middle_of(micro):
        grad = summed(f"second{micro}")
        inverse, middle = bag[f"inverse_two{micro}"], bag[f"middle{micro}"]
        unit = middle * inverse
        total = out_grad[micro].astype(f32) + norm_back(grad, unit, inverse, gain_two)
        bag[f"grad_middle{micro}"] = total
        bag[f"gain_two{micro}"] = jnp.sum(grad * unit, axis=0)
        bag[f"low{micro}"] = total.astype(bf16)

    def hide(micro):
        bag[f"cot_all{micro}"], bag[f"grad_pre{micro}"] = ffn_backward(
            rows_of(f"cot{micro}"), bag["w_down"], *bag.pop(f"by{micro}"))

    def back(micro):
        bag[f"partial{micro}"] = against(bag[f"grad_pre{micro}"], bag["w_up"]).astype(bf16)

    bag["cot0_core"] = to_core(bag["cot0"])
    bag["cot1_core"] = to_core(bag["cot1"])
    bag["cot1_diagonal"] = to_core(bag["cot1_x"])
    bag["w_down"] = third.finish()[0].reshape(width, hidden_units)
    hide(0)
    back(0)
    down_of(0)
    bag.fence()

    exchange("second0", bag.pop("partial0"))
    exchange("down0", bag.pop("down_partial0"))
    hide(1)
    bag.fence()

    across("second0")
    back(1)
    down_grad = Scatter(links, bag, "down_grad", *weight_grad(
        bag["table"], bag.take("cot_all0", "cot_all1"), [bag["hidden0"], bag["hidden1"]], UNIT, 2))
    bag.fence()

    across("down0")
    down_grad.pair()
    exchange("second1", bag.pop("partial1"))
    grad_middle_of(0)
    down_of(1)
    bag.fence()

    across("second1")
    down_grad.pair()
    bag["low0_core"] = to_core(bag["low0"])
    exchange("down1", bag.pop("down_partial1"))
    up_grad = Scatter(links, bag, "up_grad", *weight_grad(
        bag["table"], bag.take("two_all0", "two_all1"), bag.take("grad_pre0", "grad_pre1"), 2 * UNIT, 4))
    bag.fence()

    def output_of(micro):
        bag[f"output{micro}"] = (bag[f"middle{micro}"] + summed(f"down{micro}")).astype(bf16)

    bag["low0_x"] = to_x(bag["low0"])
    up_grad.pair()
    down_grad.along()
    grad_middle_of(1)
    output_of(0)
    bag.fence()

    def into_mix(micro):
        bag[f"low_all{micro}"], bag[f"grad_gated{micro}"] = project_rows(
            rows_of(f"low{micro}"), bag["w_out"], 512, "grad_gated")

    def mix_back(micro):
        grad, bag[f"gates_grad{micro}"], bag[f"small{micro}"] = mixing_backward(
            me, bag.pop(f"grad_gated{micro}").reshape(4, own_rows, channels), *bag.pop(f"mixed{micro}"),
            bag[f"ids{micro}"], bag["taps"], bag["gates"], bag["rate"], bag["slope"])
        bag[f"grad_branch{micro}"] = grad.reshape(group_rows, 2 * channels)
        bag[f"partial{micro}"] = against(bag[f"grad_branch{micro}"], bag["w_branch"]).astype(bf16)

    bag["low1_x"] = to_x(bag["low1"])
    bag["low0_diagonal"] = to_core(bag["low0_x"])
    up_grad.pair()
    down_grad.along()
    into_mix(0)
    mix_back(0)
    bag.fence()

    bag["low1_core"] = to_core(bag["low1"])
    bag["low1_diagonal"] = to_core(bag["low1_x"])
    exchange("third0", bag.pop("partial0"))
    up_grad.pair()
    down_grad.along()
    into_mix(1)
    out_grad_w = Scatter(links, bag, "out_grad", *weight_grad(
        bag["table"], bag.take("low_all0", "low_all1"), bag.take("gated0", "gated1"), 512, 1))
    bag.fence()

    across("third0")
    up_grad.pair()
    up_grad.along()
    mix_back(1)
    bag.fence()

    def leave(micro):
        grad = summed(f"third{micro}")
        inverse = bag[f"inverse_one{micro}"]
        unit = block_in[micro].astype(f32) * inverse
        bag[f"input_grad{micro}"] = bag[f"grad_middle{micro}"] + norm_back(grad, unit, inverse, gain_one)
        bag[f"gain_one{micro}"] = jnp.sum(grad * unit, axis=0)

    across("down1")
    out_grad_w.pair()
    up_grad.along()
    exchange("third1", bag.pop("partial1"))
    gates_grads = []
    for micro in range(2):
        part = bag.pop(f"gates_grad{micro}").reshape(blocks, 2, links.dp, gate_columns, BS)
        gates_grads.append(jnp.transpose(part, (2, 3, 1, 0, 4)).reshape(links.dp, gate_columns, 2 * channels))
    first_grad = Scatter(links, bag, "first_grad", *weight_grad(
        bag["table"], bag.take("normed_all0", "normed_all1"), bag.take("grad_branch0", "grad_branch1"), 512, 4,
        gates_grads))
    small = AllSum(bag, "small", bag.pop("small0") + bag.pop("small1"), [("dp", links.dp)])
    bag.fence()

    across("third1")
    first_grad.pair()
    up_grad.along()
    out_grad_w.along()
    leave(0)
    bag["down_total"] = down_grad.finish()
    bag.fence()

    first_grad.pair()
    first_grad.along()
    out_grad_w.along()
    small.step()
    leave(1)
    bag["up_total"] = up_grad.finish()
    bag.fence()

    first_grad.pair()
    first_grad.along()
    out_grad_w.along()
    gains = jnp.stack([bag.pop("gain_one0") + bag.pop("gain_one1"), bag.pop("gain_two0") + bag.pop("gain_two1")])
    gains = AllSum(bag, "gains", gains, [("mp", links.mp), ("dp", links.dp)])
    gains.step()
    gains.step()
    output_of(1)
    bag["outputs"] = jnp.stack(bag.take("output0", "output1"))
    bag.fence()

    first_grad.pair()
    first_grad.along()
    gains.step()
    small.step()
    bag["input_grads"] = jnp.stack([bag.pop("input_grad0"), bag.pop("input_grad1")])
    bag["out_total"] = out_grad_w.finish()
    bag.fence()

    gains = gains.finish()
    small = small.finish()
    total = first_grad.finish()
    both_grad = total[:d_rows].reshape(d_rows, blocks, 2, BS)
    gate_grad = jnp.transpose(total[d_rows:].reshape(gate_columns, 2, blocks, BS), (1, 2, 3, 0))
    up_total = bag["up_total"].reshape(d_rows, -1, 2, UNIT)
    return (
        bag["outputs"],
        bag["input_grads"],
        gains[0],
        both_grad[:, :, 0].reshape(d_rows, channels),
        both_grad[:, :, 1].reshape(d_rows, channels),
        small[0:KW],
        gate_grad[0],
        gate_grad[1],
        small[KW],
        bag["out_total"].T,
        gains[1],
        up_total[:, :, 0].reshape(d_rows, hidden_units),
        up_total[:, :, 1].reshape(d_rows, hidden_units),
        bag["down_total"].T,
    )


def solution(mesh):
    links = Links(mesh.shape["dp"], mesh.shape["mp"])
    tokens = P(None, ("dp", "mp"), None)
    rows, columns, gate = P("dp", "mp"), P("mp", "dp"), P("mp", None, "dp")
    return jax.shard_map(
        functools.partial(body, links),
        mesh=mesh,
        in_specs=(tokens, P(None, "dp"), P(), rows, rows, P(None, "mp"), gate, gate, P("mp"), columns, P(), rows,
                  rows, columns, tokens),
        out_specs=(tokens, tokens, P(), rows, rows, P(None, "mp"), gate, gate, P("mp"), columns, P(), rows, rows,
                   columns),
        check_vma=False,
    )
```

```python
import functools

import jax
import jax.numpy as jnp
import numpy as np
from jax import lax
from jax.experimental import pallas as pl
from jax.experimental.pallas import tpu as pltpu
from jax.sharding import PartitionSpec as P

LEN = 1024
BS = 128
KW = 4

norm_eps = 1e-06
root_floor = 0.01
decay_scale = 8.0
gelu_a = 0.7978845608028654
gelu_b = 0.044715

f32 = jnp.float32
bf16 = jnp.bfloat16


BLOCK_AT = (2, 0, 3, 1)


def project(left, right):
    return jnp.dot(left, right, preferred_element_type=f32)


def inner(left, right):
    return lax.dot_general(left, right, (((0,), (0,)), ((), ())), preferred_element_type=f32)


def against(left, right):
    return lax.dot_general(left, right, (((1,), (1,)), ((), ())), preferred_element_type=f32)


def norm_back(grad_normed, unit_rows, inverse, gain):
    scaled = grad_normed * gain
    return inverse * (scaled - unit_rows * jnp.mean(scaled * unit_rows, axis=-1, keepdims=True))


def gelu_parts(v):
    squared = v * v
    inside = gelu_a * v * (1.0 + gelu_b * squared)
    t = jnp.tanh(inside)
    half = 0.5 * (1.0 + t)
    value = v * half
    slope = half + 0.5 * v * (1.0 - t * t) * (gelu_a * (1.0 + 3.0 * gelu_b * squared))
    return value, slope


def gelu_value(v):
    return 0.5 * v * (1.0 + jnp.tanh(gelu_a * v * (1.0 + gelu_b * v * v)))


def place_of(me, block):
    differ = lax.bitwise_xor(me, block)
    low = lax.bitwise_and(differ, 1)
    high = lax.shift_right_logical(differ, 1)
    return 2 * (1 - low) + high


CHUNK = 64
STEP = 32


def tile_scan(a, b, row):
    for d in (1, 2, 4):
        use = row >= d
        b = b + a * jnp.where(use, pltpu.roll(b, d, 0), 0.0)
        a = a * jnp.where(use, pltpu.roll(a, d, 0), 1.0)
    return a, b


def tile_scan_back(a, b, row):
    for d in (1, 2, 4):
        use = row < 8 - d
        b = b + a * jnp.where(use, pltpu.roll(b, 8 - d, 0), 0.0)
        a = a * jnp.where(use, pltpu.roll(a, 8 - d, 0), 1.0)
    return a, b


def spread(row):
    return jnp.broadcast_to(row, (8, BS))


def mixing_forward_kernel(me_ref, branch, ids, taps, gates, rate, gated, states, conv, sig_r, sig_i,
                          xpad, idpad, logits):
    rows = LEN
    quarter = rows // 4
    me = me_ref[0]
    xpad[0:8, :] = jnp.zeros((8, BS), f32)
    idpad[0:8, :] = jnp.full((8, BS), -1, jnp.int32)
    idpad[8:8 + rows, :] = ids[...]
    for block in range(4):
        at = place_of(me, block)
        xpad[8 + block * quarter: 8 + (block + 1) * quarter, :] = branch[at, :, 0:BS]
    rate_row = rate[0:1, :]

    def convolve(step, _):
        base = pl.multiple_of(step * CHUNK, CHUNK)
        own_ids = idpad[pl.ds(base + 8, CHUNK), :]
        total = taps[0:1, :] * xpad[pl.ds(base + 8, CHUNK), :]
        for k in range(1, KW):
            same = idpad[pl.ds(base + 8 - k, CHUNK), :] == own_ids
            total = total + taps[k:k + 1, :] * jnp.where(same, xpad[pl.ds(base + 8 - k, CHUNK), :], 0.0)
        conv[pl.ds(base, CHUNK), :] = total.astype(bf16)
        return 0

    lax.fori_loop(0, rows // CHUNK, convolve, 0, unroll=2)
    logits[...] = lax.dot_general(conv[...], gates[...], (((1,), (1,)), ((), ())), preferred_element_type=f32)
    row = lax.broadcasted_iota(jnp.int32, (8, BS), 0)

    def advance(step, carry):
        base = pl.multiple_of(step * STEP, STEP)
        here = pl.ds(base, STEP)
        block = lax.div(step, quarter // STEP)
        at = place_of(me, block)
        there = pl.ds(pl.multiple_of(base - block * quarter, STEP), STEP)
        sr = jax.nn.sigmoid(logits[here, 0:BS])
        si = jax.nn.sigmoid(logits[here, BS:2 * BS])
        sig_r[here, :] = sr
        sig_i[here, :] = si
        same = idpad[pl.ds(base + 7, STEP), :] == idpad[pl.ds(base + 8, STEP), :]
        a = jnp.where(same, jnp.exp(rate_row * sr), 0.0)
        margin = jnp.maximum(1.0 - a * a, root_floor)
        b = conv[here, :].astype(f32) * si * (margin * lax.rsqrt(margin))
        tiles = []
        for k in range(STEP // 8):
            part = slice(8 * k, 8 * k + 8)
            product, local = tile_scan(a[part], b[part], row)
            tiles.append(local + product * carry)
            carry = spread(local[7:8]) + spread(product[7:8]) * carry
        state = jnp.concatenate(tiles, axis=0)
        states[here, :] = state
        gated[at, there, :] = (state * gelu_value(branch[at, there, BS:2 * BS])).astype(bf16)
        return carry

    lax.fori_loop(0, rows // STEP, advance, jnp.zeros((8, BS), f32), unroll=2)


def mixing_backward_kernel(me_ref, grad_gated, branch, states, conv, sig_r, sig_i, ids, taps, gates, rate, slope,
                           grad_branch, grad_gates, small,
                           xpad, idpad, spad, low, gcpad, through):
    rows = LEN
    quarter = rows // 4
    me = me_ref[0]
    zero8 = jnp.zeros((8, BS), f32)
    xpad[0:8, :] = zero8
    spad[0:8, :] = zero8
    spad[8:8 + rows, :] = states[...]
    idpad[0:8, :] = jnp.full((8, BS), -1, jnp.int32)
    idpad[8:8 + rows, :] = ids[...]
    idpad[8 + rows:16 + rows, :] = jnp.full((8, BS), -1, jnp.int32)
    gcpad[rows:rows + 8, :] = zero8
    rate_row = rate[0:1, :]
    slope_row = slope[0:1, :]
    for block in range(4):
        at = place_of(me, block)
        xpad[8 + block * quarter: 8 + (block + 1) * quarter, :] = branch[at, :, 0:BS]
    row = lax.broadcasted_iota(jnp.int32, (8, BS), 0)
    fold = lambda v: jnp.sum(v.reshape(v.shape[0] // 8, 8, BS), axis=0)
    steps = rows // STEP

    def retreat(count, held):
        carry, decay_sum = held
        step = steps - 1 - count
        base = pl.multiple_of(step * STEP, STEP)
        here = pl.ds(base, STEP)
        block = lax.div(step, quarter // STEP)
        at = place_of(me, block)
        there = pl.ds(pl.multiple_of(base - block * quarter, STEP), STEP)
        value, gradient = gelu_parts(branch[at, there, BS:2 * BS])
        incoming = grad_gated[at, there, :]
        grad_states = incoming * value
        grad_branch[at, there, BS:2 * BS] = (gradient * states[here, :] * incoming).astype(bf16)
        same = idpad[pl.ds(base + 7, STEP), :] == idpad[pl.ds(base + 8, STEP), :]
        sr = sig_r[here, :]
        si = sig_i[here, :]
        a = jnp.where(same, jnp.exp(rate_row * sr), 0.0)
        pushed = a * grad_states
        us, gs = [], []
        for k in reversed(range(STEP // 8)):
            part = slice(8 * k, 8 * k + 8)
            product, local = tile_scan_back(a[part], pushed[part], row)
            u = local + product * carry
            us.insert(0, u)
            gs.insert(0, grad_states[part] + jnp.where(row == 7, carry, pltpu.roll(u, 7, 0)))
            carry = spread(local[0:1]) + spread(product[0:1]) * carry
        u = jnp.concatenate(us, axis=0)
        g = jnp.concatenate(gs, axis=0)
        square = a * a
        inside = 1.0 - square
        margin = jnp.maximum(inside, root_floor)
        inverse = lax.rsqrt(margin)
        multiplier = margin * inverse
        gsi = g * si
        gcsi = gsi * conv[here, :].astype(f32)
        grad_log = u * spad[pl.ds(base + 7, STEP), :] - jnp.where(inside > root_floor, gcsi * square * inverse, 0.0)
        gcpad[here, :] = gsi * multiplier
        weighted = grad_log * sr
        low[here, 0:BS] = (weighted * (1.0 - sr) * rate_row).astype(bf16)
        low[here, BS:2 * BS] = (gcsi * multiplier * (1.0 - si)).astype(bf16)
        return carry, decay_sum + fold(weighted)

    _, decay_sum = lax.fori_loop(0, steps, retreat, (zero8, zero8), unroll=2)

    both_gates = lax.dot_general(low[...], conv[...], (((0,), (0,)), ((), ())), preferred_element_type=f32)
    grad_gates[0] = both_gates[0:BS]
    grad_gates[1] = both_gates[BS:2 * BS]
    through[...] = lax.dot_general(low[...], gates[...], (((1,), (0,)), ((), ())), preferred_element_type=f32)

    def add_gates(step, _):
        here = pl.ds(pl.multiple_of(step * CHUNK, CHUNK), CHUNK)
        gcpad[here, :] = gcpad[here, :] + through[here, :]
        return 0

    lax.fori_loop(0, rows // CHUNK, add_gates, 0, unroll=4)

    def finish(step, sums):
        base = pl.multiple_of(step * CHUNK, CHUNK)
        block = lax.div(step, quarter // CHUNK)
        at = place_of(me, block)
        there = pl.ds(pl.multiple_of(base - block * quarter, CHUNK), CHUNK)
        gc = gcpad[pl.ds(base, CHUNK), :]
        own_ids = idpad[pl.ds(base + 8, CHUNK), :]
        new = [sums[0] + fold(gc * xpad[pl.ds(base + 8, CHUNK), :])]
        grad_x = taps[0:1, :] * gc
        for k in range(1, KW):
            same = idpad[pl.ds(base + 8 - k, CHUNK), :] == own_ids
            new.append(sums[k] + fold(jnp.where(same, gc * xpad[pl.ds(base + 8 - k, CHUNK), :], 0.0)))
            after = idpad[pl.ds(base + 8 + k, CHUNK), :] == own_ids
            grad_x = grad_x + taps[k:k + 1, :] * jnp.where(after, gcpad[pl.ds(base + k, CHUNK), :], 0.0)
        grad_branch[at, there, 0:BS] = grad_x.astype(bf16)
        return tuple(new)

    sums = lax.fori_loop(0, rows // CHUNK, finish, (zero8,) * KW, unroll=2)
    small[...] = jnp.zeros((8, BS), f32)
    for k in range(KW):
        small[k:k + 1, :] = jnp.sum(sums[k], axis=0, keepdims=True)
    small[KW:KW + 1, :] = jnp.sum(decay_sum, axis=0, keepdims=True) * slope_row


def mixing_forward(me, branch, ids, taps, gates, rate):
    rows = LEN
    blocks = branch.shape[2] // (2 * BS)
    channels = blocks * BS
    flat = lambda n, me: (0, n)
    return pl.pallas_call(
        mixing_forward_kernel,
        grid_spec=pltpu.PrefetchScalarGridSpec(
            num_scalar_prefetch=1,
            grid=(blocks,),
            in_specs=[
                pl.BlockSpec((4, rows // 4, 2 * BS), lambda n, me: (0, 0, n)),
                pl.BlockSpec((rows, BS), lambda n, me: (0, 0)),
                pl.BlockSpec((8, BS), flat),
                pl.BlockSpec((2 * BS, BS), flat),
                pl.BlockSpec((8, BS), flat),
            ],
            out_specs=[
                pl.BlockSpec((4, rows // 4, BS), lambda n, me: (0, 0, n)),
                pl.BlockSpec((rows, BS), flat),
                pl.BlockSpec((rows, BS), flat),
                pl.BlockSpec((rows, BS), flat),
                pl.BlockSpec((rows, BS), flat),
            ],
            scratch_shapes=[
                pltpu.VMEM((rows + 8, BS), f32),
                pltpu.VMEM((rows + 8, BS), jnp.int32),
                pltpu.VMEM((rows, 2 * BS), f32),
            ],
        ),
        out_shape=[
            jax.ShapeDtypeStruct((4, rows // 4, channels), bf16),
            jax.ShapeDtypeStruct((rows, channels), f32),
            jax.ShapeDtypeStruct((rows, channels), bf16),
            jax.ShapeDtypeStruct((rows, channels), f32),
            jax.ShapeDtypeStruct((rows, channels), f32),
        ],
        compiler_params=vmem(16),
        cost_estimate=pl.CostEstimate(flops=2 * rows * channels * 256, bytes_accessed=24_000_000, transcendentals=0),
        name="mixing_forward",
    )(me, branch, ids, taps, gates, rate)


def mixing_backward(me, grad_gated, branch, states, conv, sig_r, sig_i, ids, taps, gates, rate, slope):
    rows = LEN
    blocks = branch.shape[2] // (2 * BS)
    channels = blocks * BS
    flat = lambda n, me: (0, n)
    cube = lambda n, me: (0, 0, n)
    return pl.pallas_call(
        mixing_backward_kernel,
        grid_spec=pltpu.PrefetchScalarGridSpec(
            num_scalar_prefetch=1,
            grid=(blocks,),
            in_specs=[
                pl.BlockSpec((4, rows // 4, BS), cube),
                pl.BlockSpec((4, rows // 4, 2 * BS), cube),
                pl.BlockSpec((rows, BS), flat),
                pl.BlockSpec((rows, BS), flat),
                pl.BlockSpec((rows, BS), flat),
                pl.BlockSpec((rows, BS), flat),
                pl.BlockSpec((rows, BS), lambda n, me: (0, 0)),
                pl.BlockSpec((8, BS), flat),
                pl.BlockSpec((2 * BS, BS), flat),
                pl.BlockSpec((8, BS), flat),
                pl.BlockSpec((8, BS), flat),
            ],
            out_specs=[
                pl.BlockSpec((4, rows // 4, 2 * BS), cube),
                pl.BlockSpec((2, BS, BS), cube),
                pl.BlockSpec((8, BS), flat),
            ],
            scratch_shapes=[
                pltpu.VMEM((rows + 8, BS), f32),
                pltpu.VMEM((rows + 16, BS), jnp.int32),
                pltpu.VMEM((rows + 8, BS), f32),
                pltpu.VMEM((rows, 2 * BS), bf16),
                pltpu.VMEM((rows + 8, BS), f32),
                pltpu.VMEM((rows, BS), f32),
            ],
        ),
        out_shape=[
            jax.ShapeDtypeStruct((4, rows // 4, 2 * channels), bf16),
            jax.ShapeDtypeStruct((2, BS, channels), f32),
            jax.ShapeDtypeStruct((8, channels), f32),
        ],
        compiler_params=vmem(24),
        cost_estimate=pl.CostEstimate(flops=2 * rows * channels * 512, bytes_accessed=48_000_000, transcendentals=0),
        name="mixing_backward",
    )(me, grad_gated, branch, states, conv, sig_r, sig_i, ids, taps, gates, rate, slope)


def folded(count):
    return list(range(0, 1)) + list(range(1, count, 2)) + list(range((count - 1) // 2 * 2, 0, -2))


class Links:
    def __init__(self, dp, mp):
        assert mp == 4 and dp % 2 == 0
        self.dp, self.mp = dp, mp
        self.line = dp // 2
        self.order = folded(self.line)
        self.place = {a: k for k, a in enumerate(self.order)}
        self.ring = [
            (2 * a + b, 2 * self.order[(self.place[a] + 1) % self.line] + b)
            for a in range(self.line)
            for b in range(2)
        ]

    def to_core(self, v):
        return lax.ppermute(v, "mp", [(i, i ^ 1) for i in range(self.mp)])

    def to_x(self, v):
        return lax.ppermute(v, "mp", [(i, i ^ 2) for i in range(self.mp)])

    def to_pair(self, v):
        return lax.ppermute(v, "dp", [(i, i ^ 1) for i in range(self.dp)])

    def along(self, v):
        return lax.ppermute(v, "dp", self.ring)

    def behind(self, me, steps):
        at = lax.shift_right_logical(me, 1)
        place = jnp.int32(0)
        for a in range(self.line):
            place = jnp.where(at == a, self.order[(self.place[a] - steps) % self.line], place)
        return place.astype(jnp.int32)


def vmem(mib):
    return pltpu.CompilerParams(vmem_limit_bytes=mib * 1024 * 1024)


UNIT = 384


def assemble(pieces, whole):
    @pl.when(pl.program_id(0) == 0)
    def _():
        rows = pieces[0].shape[0]
        for k, piece in enumerate(pieces):
            whole[k * rows:(k + 1) * rows, :] = piece[...]


def rows_call(kernel, pieces, more, more_specs, outs, out_specs, grid, flops, name, mib, scratch=()):
    own, width = pieces[0].shape
    count = len(pieces)
    whole = pl.BlockSpec((count * own, width), lambda n: (0, 0))
    joined = count > 1

    def run(*refs):
        x, others = refs[0], refs[count:]
        if joined:
            x = refs[count + len(more)]
            assemble(refs[:count], x)
            others = refs[count:count + len(more)] + refs[count + len(more) + 1:]
        kernel(x, *others)

    moved = sum(2 * v.size * v.dtype.itemsize for v in (*pieces, *more))
    return pl.pallas_call(
        run,
        grid=(grid,),
        in_specs=[pl.BlockSpec((own, width), lambda n: (0, 0))] * count + more_specs,
        out_specs=[whole] * joined + out_specs,
        out_shape=[jax.ShapeDtypeStruct((count * own, width), bf16)] * joined + outs,
        scratch_shapes=list(scratch),
        compiler_params=vmem(mib),
        cost_estimate=pl.CostEstimate(flops=flops, bytes_accessed=moved, transcendentals=0),
        name=name,
    )(*pieces, *more)


def against_kernel(x, w, send, keep):
    half = send.shape[0]
    result = lax.dot_general(x[...], w[...], (((1,), (1,)), ((), ())), preferred_element_type=f32).astype(bf16)
    send[...] = result[:half]
    keep[...] = result[half:]


def against_rows(x, w, name):
    rows, depth = x.shape
    width = w.shape[0]
    tile = 256
    half = pl.BlockSpec((rows // 2, tile), lambda n: (0, n))
    return rows_call(
        against_kernel, [x], [w], [pl.BlockSpec((tile, depth), lambda n: (n, 0))],
        [jax.ShapeDtypeStruct((rows // 2, width), bf16)] * 2, [half] * 2, width // tile,
        2 * rows * width * depth, name, 20)


def project_kernel(x, w, out):
    out[...] = jnp.dot(x[...], w[...], preferred_element_type=f32)


def project_rows(pieces, w, tile, name):
    own, width = pieces[0].shape
    columns = w.shape[1]
    return rows_call(
        project_kernel, pieces, [w], [pl.BlockSpec((width, tile), lambda n: (0, n))],
        [jax.ShapeDtypeStruct((4 * own, columns), f32)], [pl.BlockSpec((4 * own, tile), lambda n: (0, n))],
        columns // tile, 8 * own * width * columns, name, 24)


def ffn_forward_kernel(x, w, hidden, by_gate, by_up):
    both = jnp.dot(x[...], w[...], preferred_element_type=f32)
    up = both[:, UNIT:]
    value, slope = gelu_parts(both[:, :UNIT])
    hidden[...] = (value * up).astype(bf16)
    by_gate[...] = (up * slope).astype(bf16)
    by_up[...] = value.astype(bf16)


def ffn_forward(pieces, w):
    own, width = pieces[0].shape
    units = w.shape[1] // 2
    tile = pl.BlockSpec((4 * own, UNIT), lambda n: (0, n))
    return rows_call(
        ffn_forward_kernel, pieces, [w], [pl.BlockSpec((width, 2 * UNIT), lambda n: (0, n))],
        [jax.ShapeDtypeStruct((4 * own, units), bf16)] * 3, [tile] * 3,
        units // UNIT, 16 * own * width * units, "ffn_forward", 34)


def ffn_backward_kernel(x, w, by_gate, by_up, w_up, out, send, keep, total):
    grad = jnp.dot(x[...], w[...], preferred_element_type=f32)
    out[:, :UNIT] = (grad * by_gate[...].astype(f32)).astype(bf16)
    out[:, UNIT:] = (grad * by_up[...].astype(f32)).astype(bf16)
    more = lax.dot_general(out[...], w_up[...], (((1,), (1,)), ((), ())), preferred_element_type=f32)
    at, last = pl.program_id(0), pl.num_programs(0) - 1

    @pl.when(at == 0)
    def _():
        total[...] = more

    @pl.when(jnp.logical_and(at > 0, at < last))
    def _():
        total[...] += more

    @pl.when(at == last)
    def _():
        half = send.shape[0]
        result = (total[...] + more).astype(bf16)
        send[...] = result[:half]
        keep[...] = result[half:]


def ffn_backward(x, w, by_gate, by_up, w_up):
    rows, width = x.shape
    units = w.shape[1]
    assert units // UNIT > 1
    tile = pl.BlockSpec((rows, UNIT), lambda n: (0, n))
    half = pl.BlockSpec((rows // 2, width), lambda n: (0, 0))
    return rows_call(
        ffn_backward_kernel, [x], [w, by_gate, by_up, w_up],
        [pl.BlockSpec((width, UNIT), lambda n: (0, n)), tile, tile,
         pl.BlockSpec((width, 2 * UNIT), lambda n: (0, n))],
        [jax.ShapeDtypeStruct((rows, 2 * units), bf16)] + [jax.ShapeDtypeStruct((rows // 2, width), bf16)] * 2,
        [pl.BlockSpec((rows, 2 * UNIT), lambda n: (0, n)), half, half],
        units // UNIT, 6 * rows * width * units, "ffn_backward", 46, [pltpu.VMEM((rows, width), f32)])


def pack_kernel(x, y, out, recur, inp, packed):
    rows, channels = x.shape
    columns = recur.shape[2]
    for n in range(channels // BS):
        block = slice(n * BS, (n + 1) * BS)
        packed[0:rows, 2 * n * BS:(2 * n + 1) * BS] = x[:, block]
        packed[0:rows, (2 * n + 1) * BS:(2 * n + 2) * BS] = y[:, block]
        packed[rows:rows + columns, block] = recur[n].astype(f32).T.astype(bf16)
        packed[rows:rows + columns, channels + n * BS:channels + (n + 1) * BS] = inp[n].astype(f32).T.astype(bf16)
    packed[0:rows, 2 * channels:3 * channels] = out[...].astype(f32).T.astype(bf16)
    packed[rows:rows + columns, 2 * channels:3 * channels] = jnp.zeros((columns, channels), bf16)


def pack(x, y, out, recur, inp):
    rows, channels = x.shape
    return pl.pallas_call(
        pack_kernel,
        out_shape=jax.ShapeDtypeStruct((rows + recur.shape[2], 3 * channels), bf16),
        name="pack",
    )(x, y, out, recur, inp)


def weight_grad_kernel(line, shard, extra, groups, table, *refs):
    if extra:
        left_a, right_a, left_b, right_b, extra_a, extra_b, *sent, kept, total = refs
    else:
        left_a, right_a, left_b, right_b, *sent, kept, total = refs
    dims = (((0,), (0,)), ((), ()))
    total[...] = lax.dot_general(
        left_a[...], right_a[...], dims, preferred_element_type=f32
    ) + lax.dot_general(left_b[...], right_b[...], dims, preferred_element_type=f32)
    bit = table[line]
    size = line // groups
    for k in range(line):
        at = 2 * table[k]
        out = sent[k // size]
        mine = pl.ds(pl.multiple_of((at + bit) * shard, 16), shard)
        other = pl.ds(pl.multiple_of((at + 1 - bit) * shard, 16), shard)
        kept[k, 0:shard, :] = total[mine, :]
        out[k % size, 0:shard, :] = total[other, :].astype(bf16)
        if extra:
            kept[k, shard:shard + extra, :] = extra_a[0, at + bit] + extra_b[0, at + bit]
            out[k % size, shard:shard + extra, :] = (
                extra_a[0, at + 1 - bit] + extra_b[0, at + 1 - bit]).astype(bf16)


def weight_grad(table, left, right, tile, groups, extras=None):
    line = table.shape[0] - 1
    rows, width = left[0].shape
    columns = right[0].shape[1]
    shard = width // (2 * line)
    extra = extras[0].shape[2] if extras else 0
    lefts = pl.BlockSpec((rows, width), lambda n, t: (0, 0))
    rights = pl.BlockSpec((rows, tile), lambda n, t: (0, n))
    more = [pl.BlockSpec((1, 2 * line, extra, tile), lambda n, t: (n, 0, 0, 0))] * 2 if extra else []
    parts = lambda count: pl.BlockSpec((count, shard + extra, tile), lambda n, t: (0, 0, n))
    size = line // groups
    *sent, kept = pl.pallas_call(
        functools.partial(weight_grad_kernel, line, shard, extra, groups),
        grid_spec=pltpu.PrefetchScalarGridSpec(
            num_scalar_prefetch=1,
            grid=(columns // tile,),
            in_specs=[lefts, rights, lefts, rights] + more,
            out_specs=[parts(size)] * groups + [parts(line)],
            scratch_shapes=[pltpu.VMEM((width, tile), f32)],
        ),
        out_shape=[jax.ShapeDtypeStruct((size, shard + extra, columns), bf16)] * groups
        + [jax.ShapeDtypeStruct((line, shard + extra, columns), f32)],
        compiler_params=vmem(44),
        cost_estimate=pl.CostEstimate(
            flops=4 * rows * width * columns, bytes_accessed=30_000_000, transcendentals=0),
        name="weight_grad",
    )(table, left[0], right[0], left[1], right[1], *(extras or ()))
    return sent, kept


def last_sum(write, held, at, outs, name):
    kept, sent, moving = held["kept"], held["sent"][at // held["size"]], held["moving"]
    shape = (1,) + kept.shape[1:]
    inside = at % held["size"]

    def kernel(kept, sent, moving, *outs):
        write(kept[0] + sent[0].astype(f32) + moving[...].astype(f32), *outs)

    return pl.pallas_call(
        kernel,
        grid=(1,),
        in_specs=[pl.BlockSpec(shape, lambda n: (at, 0, 0)), pl.BlockSpec(shape, lambda n: (inside, 0, 0)),
                  pl.BlockSpec(shape[1:], lambda n: (0, 0))],
        out_specs=[pl.BlockSpec(out, lambda n, rank=len(out): (0,) * rank) for out in outs],
        out_shape=[jax.ShapeDtypeStruct(out, f32) for out in outs],
        compiler_params=vmem(16),
        name=name,
    )(kept, sent, moving)


def write_turned(total, out):
    out[...] = total.T


def write_gate_up(total, gate, up):
    for k in range(gate.shape[1] // UNIT):
        gate[:, k * UNIT:(k + 1) * UNIT] = total[:, 2 * k * UNIT:(2 * k + 1) * UNIT]
        up[:, k * UNIT:(k + 1) * UNIT] = total[:, (2 * k + 1) * UNIT:(2 * k + 2) * UNIT]


def write_first(total, x, y, recur, inp):
    rows, channels = x.shape
    for n in range(channels // BS):
        block = slice(n * BS, (n + 1) * BS)
        x[:, block] = total[:rows, 2 * n * BS:(2 * n + 1) * BS]
        y[:, block] = total[:rows, (2 * n + 1) * BS:(2 * n + 2) * BS]
        recur[n] = total[rows:, block].T
        inp[n] = total[rows:, channels + n * BS:channels + (n + 1) * BS].T


class Bag(dict):
    def fence(self):
        values, tree = jax.tree.flatten(dict(self))
        values = lax.optimization_barrier(values)
        self.update(jax.tree.unflatten(tree, values))

    def take(self, *names):
        out = [self.pop(name) for name in names]
        return out if len(out) > 1 else out[0]


class Gather:
    def __init__(self, links, me, bag, name, shard, parts=None):
        self.links, self.me, self.bag, self.name = links, me, bag, name
        self.along_steps, self.pair_steps, self.placed, self.other_placed = 0, 0, 0, 0
        self.parts = parts or [(slice(0, shard.shape[0]), slice(0, shard.shape[1]))]
        bag[name] = {"z": [shard], "y": [], "whole": None}

    def along(self, steps=1):
        z = self.bag[self.name]["z"]
        for _ in range(steps):
            if self.along_steps < self.links.line - 1:
                z.append(self.links.along(z[self.along_steps]))
                self.along_steps += 1

    def pair(self, steps=1):
        held = self.bag[self.name]
        for _ in range(steps):
            if self.pair_steps <= self.along_steps and self.pair_steps < self.links.line:
                held["y"].append(self.links.to_pair(held["z"][self.pair_steps]))
                self.pair_steps += 1

    def put(self, pieces, at, bit):
        held = self.bag[self.name]
        base = 2 * self.links.behind(self.me, at)
        wholes = []
        for k, (rows, columns) in enumerate(self.parts):
            piece = pieces[at][rows, columns][None]
            whole = jnp.zeros((self.links.dp,) + piece.shape[1:], bf16) if held["whole"] is None else held["whole"][k]
            wholes.append(lax.dynamic_update_slice(whole, piece, (base + bit, 0, 0)))
        held["whole"] = wholes

    def place(self, z=0, y=0):
        held = self.bag[self.name]
        bit = lax.bitwise_and(self.me, 1)
        for _ in range(z):
            if self.placed <= self.along_steps:
                self.put(held["z"], self.placed, bit)
                self.placed += 1
        for _ in range(y):
            if self.other_placed < self.pair_steps:
                self.put(held["y"], self.other_placed, 1 - bit)
                self.other_placed += 1
        for k in range(min(self.placed, self.pair_steps, self.along_steps)):
            held["z"][k] = None
        for k in range(self.other_placed):
            held["y"][k] = None

    def finish(self):
        line = self.links.line
        while self.pair_steps < line:
            self.along()
            self.pair()
        self.place(line, line)
        return self.bag.pop(self.name)["whole"]


class Scatter:
    def __init__(self, links, bag, name, sent, kept):
        self.links, self.bag, self.name = links, bag, name
        self.pair_steps, self.along_steps = 0, 0
        self.size = links.line // len(sent)
        bag[name] = {"sent": list(sent), "kept": kept, "moving": None}

    def pair(self):
        sent = self.bag[self.name]["sent"]
        if self.pair_steps < len(sent):
            sent[self.pair_steps] = self.links.to_pair(sent[self.pair_steps])
            self.pair_steps += 1

    def along(self):
        held = self.bag[self.name]
        at = self.along_steps
        if at < self.links.line - 1 and at // self.size < self.pair_steps:
            held["moving"] = self.links.along(self.sum_here().astype(bf16))
            self.along_steps += 1

    def sum_here(self):
        held = self.bag[self.name]
        at = self.along_steps
        total = held["kept"][at] + held["sent"][at // self.size][at % self.size].astype(f32)
        if held["moving"] is not None:
            total = total + held["moving"].astype(f32)
        return total

    def finish(self, write, *outs):
        while self.pair_steps < len(self.bag[self.name]["sent"]):
            self.pair()
        while self.along_steps < self.links.line - 1:
            self.along()
        held = self.bag.pop(self.name)
        return last_sum(write, {**held, "size": self.size}, self.along_steps, outs, self.name)


class AllSum:
    def __init__(self, bag, name, value, axes):
        self.bag, self.name = bag, name
        self.steps = [(axis, count, 1 << k) for axis, count in axes for k in range(count.bit_length() - 1)]
        assert all(count & (count - 1) == 0 for _, count in axes)
        bag[name] = value

    def step(self):
        if self.steps:
            axis, count, bit = self.steps.pop(0)
            value = self.bag[self.name]
            self.bag[self.name] = value + lax.ppermute(value, axis, [(i, i ^ bit) for i in range(count)])

    def finish(self):
        while self.steps:
            self.step()
        return self.bag.pop(self.name)


def body(links, block_in, doc_ids, mix_gain, proj_x, proj_y, conv_taps, recur_gate, input_gate, decay_param,
         proj_out, ffn_gain, ffn_gate, ffn_up, ffn_down, out_grad):
    micro_count, own_rows, width = block_in.shape
    group_rows = doc_ids.shape[1]
    assert group_rows == LEN and own_rows * 4 == group_rows and micro_count == 2
    d_rows, channels = proj_x.shape
    blocks = channels // BS
    hidden_units = ffn_gate.shape[1]
    assert hidden_units % UNIT == 0
    gate_columns = recur_gate.shape[2]
    dp_me = lax.axis_index("dp")
    me = lax.axis_index("mp").astype(jnp.int32).reshape(1)
    gain_one = mix_gain.astype(f32)
    gain_two = ffn_gain.astype(f32)
    to_core, to_x = links.to_core, links.to_x
    bag = Bag()

    def exchange(name):
        send, keep = bag.pop(name + "_send"), bag.pop(name + "_keep")
        own_rows_of = lambda v, k: v[k * own_rows:(k + 1) * own_rows].astype(f32)
        sent = to_core(send)
        bag[name + "_own"] = (keep, sent)
        bag[name + "_x"] = (own_rows_of(keep, 1) + own_rows_of(sent, 1)).astype(bf16)

    def summed(name):
        keep, sent = bag.pop(name + "_own")
        return (keep[:own_rows].astype(f32) + sent[:own_rows].astype(f32)) + bag.pop(name + "_x").astype(f32)

    def across(name):
        bag[name + "_x"] = to_x(bag[name + "_x"])

    def rows_of(name):
        own, core, x, diagonal = bag.take(name, name + "_core", name + "_x", name + "_diagonal")
        return core, diagonal, own, x

    packed = pack(proj_x, proj_y, proj_out, recur_gate, input_gate)
    inner_rows, outer_rows = slice(0, d_rows), slice(d_rows, d_rows + gate_columns)
    wide, narrow = slice(0, 2 * channels), slice(2 * channels, 3 * channels)
    first = Gather(links, dp_me, bag, "first", packed, [(inner_rows, wide), (inner_rows, narrow), (outer_rows, wide)])
    bag.fence()

    bag["cot0"], bag["cot1"] = out_grad[0], out_grad[1]
    first.along()
    first.pair()
    for micro in range(2):
        xin = block_in[micro].astype(f32)
        inverse = lax.rsqrt(jnp.mean(xin * xin, axis=-1, keepdims=True) + norm_eps)
        bag[f"inverse_one{micro}"] = inverse
        bag[f"normed{micro}"] = (xin * inverse * gain_one).astype(bf16)
    bag.fence()

    first.along()
    first.pair()
    bag["normed0_x"] = to_x(bag["normed0"])
    bag["normed0_core"] = to_core(bag["normed0"])
    first.place(2, 1)
    decay_values = decay_param.astype(f32)
    bag["rate"] = jnp.broadcast_to((-decay_scale * jax.nn.softplus(-decay_values))[None], (8, channels))
    bag["slope"] = jnp.broadcast_to((decay_scale * jax.nn.sigmoid(-decay_values))[None], (8, channels))
    bag["taps"] = jnp.concatenate([conv_taps.astype(f32), jnp.zeros((8 - KW, channels), f32)])
    bag["table"] = jnp.stack(
        [links.behind(dp_me, step + 1) for step in range(links.line)] + [lax.bitwise_and(dp_me, 1).astype(jnp.int32)])
    bag.fence()

    first.along()
    first.pair()
    bag["normed1_x"] = to_x(bag["normed1"])
    bag["normed0_diagonal"] = to_core(bag["normed0_x"])
    first.place(1, 1)
    gate_up = jnp.stack([ffn_gate.reshape(d_rows, -1, UNIT), ffn_up.reshape(d_rows, -1, UNIT)], axis=2)
    second = Gather(links, dp_me, bag, "second", gate_up.reshape(d_rows, 2 * hidden_units))
    third = Gather(links, dp_me, bag, "third", ffn_down.T)
    for micro in range(2):
        bag[f"ids{micro}"] = jnp.broadcast_to(doc_ids[micro][:, None], (group_rows, BS))
    bag.fence()

    first.pair()
    bag["cot0_x"] = to_x(bag["cot0"])
    first.place(1, 1)
    bag.fence()

    def mix(micro):
        bag[f"normed_all{micro}"], branch = project_rows(rows_of(f"normed{micro}"), bag["w_branch"], 256, "branch")
        branch = branch.reshape(4, own_rows, 2 * channels)
        gated, *rest = mixing_forward(me, branch, bag[f"ids{micro}"], bag["taps"], bag["gates"], bag["rate"])
        bag[f"mixed{micro}"] = [branch] + rest
        bag[f"gated{micro}"] = gated.reshape(group_rows, channels)

    def against_of(name, left, weight):
        bag[name + "_send"], bag[name + "_keep"] = against_rows(bag[left], bag[weight], weight + "_turned")

    def middle_of(micro):
        middle = block_in[micro].astype(f32) + summed(f"first{micro}")
        inverse = lax.rsqrt(jnp.mean(middle * middle, axis=-1, keepdims=True) + norm_eps)
        bag[f"middle{micro}"], bag[f"inverse_two{micro}"] = middle, inverse
        bag[f"two{micro}"] = (middle * inverse * gain_two).astype(bf16)

    second.along()
    third.along()
    second.pair()
    third.pair()
    w_branch, w_out, gates = first.finish()
    bag["w_branch"] = w_branch.reshape(width, 2 * channels)
    gates = gates.reshape(links.dp * gate_columns, 2, blocks, BS)
    bag["gates"] = jnp.transpose(gates, (1, 0, 2, 3)).reshape(2 * BS, blocks * BS)
    bag["w_out"] = w_out.reshape(width, channels)
    mix(0)
    against_of("first0", "gated0", "w_out")
    bag.fence()

    bag["normed1_core"] = to_core(bag["normed1"])
    bag["normed1_diagonal"] = to_core(bag["normed1_x"])
    exchange("first0")
    second.place(1)
    bag.fence()

    second.along()
    second.pair()
    third.pair()
    across("first0")
    second.place(1)
    mix(1)
    bag.fence()

    middle_of(0)
    against_of("first1", "gated1", "w_out")
    bag.fence()

    second.along()
    third.along()
    second.pair()
    bag["two0_x"] = to_x(bag["two0"])
    bag["two0_core"] = to_core(bag["two0"])
    exchange("first1")
    second.place(3, 1)
    bag.fence()

    def forward(micro):
        bag[f"two_all{micro}"], bag[f"hidden{micro}"], *bag[f"by{micro}"] = ffn_forward(
            rows_of(f"two{micro}"), bag["w_up"])

    third.along()
    second.pair()
    across("first1")
    bag["two0_diagonal"] = to_core(bag["two0_x"])
    bag["cot0_core"] = to_core(bag["cot0"])
    second.place(1, 2)
    third.place(2, 2)
    bag.fence()

    middle_of(1)
    bag.fence()

    third.pair(2)
    bag["two1_x"] = to_x(bag["two1"])
    bag["cot0_diagonal"] = to_core(bag["cot0_x"])
    bag["w_up"] = second.finish()[0].reshape(width, 2 * hidden_units)
    third.place(2)
    forward(0)
    bag.fence()

    def back(micro):
        name = f"second{micro}"
        bag[f"grad_pre{micro}"], bag[name + "_send"], bag[name + "_keep"] = ffn_backward(
            bag[f"cot_all{micro}"], bag["w_down"], *bag.pop(f"by{micro}"), bag["w_up"])

    def grad_middle_of(micro):
        grad = summed(f"second{micro}")
        inverse, middle = bag[f"inverse_two{micro}"], bag[f"middle{micro}"]
        unit = middle * inverse
        total = out_grad[micro].astype(f32) + norm_back(grad, unit, inverse, gain_two)
        bag[f"grad_middle{micro}"] = total
        bag[f"gain_two{micro}"] = jnp.sum(grad * unit, axis=0)
        bag[f"low{micro}"] = total.astype(bf16)

    bag["cot1_x"] = to_x(bag["cot1"])
    bag["two1_core"] = to_core(bag["two1"])
    bag["two1_diagonal"] = to_core(bag["two1_x"])
    bag["cot_all0"] = jnp.concatenate(rows_of("cot0"))
    bag["w_down"] = third.finish()[0].reshape(width, hidden_units)
    back(0)
    bag.fence()

    bag["cot1_core"] = to_core(bag["cot1"])
    bag["cot1_diagonal"] = to_core(bag["cot1_x"])
    exchange("second0")
    bag["cot_all1"] = jnp.concatenate(rows_of("cot1"))
    forward(1)
    against_of("down0", "hidden0", "w_down")
    bag.fence()

    across("second0")
    exchange("down0")
    down_grad = Scatter(links, bag, "down_grad", *weight_grad(
        bag["table"], [bag["cot_all0"], bag["cot_all1"]], [bag["hidden0"], bag["hidden1"]], UNIT, 2))
    bag.fence()

    across("down0")
    down_grad.pair()
    back(1)
    bag.fence()

    exchange("second1")
    grad_middle_of(0)
    bag.fence()

    across("second1")
    down_grad.pair()
    bag["low0_core"] = to_core(bag["low0"])
    up_grad = Scatter(links, bag, "up_grad", *weight_grad(
        bag["table"], bag.take("two_all0", "two_all1"), bag.take("grad_pre0", "grad_pre1"), 2 * UNIT, 4))
    bag.fence()

    def output_of(micro):
        bag[f"output{micro}"] = (bag[f"middle{micro}"] + summed(f"down{micro}")).astype(bf16)

    bag["low0_x"] = to_x(bag["low0"])
    up_grad.pair()
    down_grad.along()
    grad_middle_of(1)
    against_of("down1", "hidden1", "w_down")
    bag.fence()

    def into_mix(micro):
        bag[f"low_all{micro}"], bag[f"grad_gated{micro}"] = project_rows(
            rows_of(f"low{micro}"), bag["w_out"], 256, "grad_gated")

    def mix_back(micro):
        grad, bag[f"gates_grad{micro}"], bag[f"small{micro}"] = mixing_backward(
            me, bag.pop(f"grad_gated{micro}").reshape(4, own_rows, channels), *bag.pop(f"mixed{micro}"),
            bag[f"ids{micro}"], bag["taps"], bag["gates"], bag["rate"], bag["slope"])
        bag[f"grad_branch{micro}"] = grad.reshape(group_rows, 2 * channels)
        against_of(f"third{micro}", f"grad_branch{micro}", "w_branch")

    bag["low1_x"] = to_x(bag["low1"])
    bag["low0_diagonal"] = to_core(bag["low0_x"])
    up_grad.pair()
    up_grad.along()
    exchange("down1")
    into_mix(0)
    mix_back(0)
    bag.fence()

    across("down1")
    bag["low1_core"] = to_core(bag["low1"])
    bag["low1_diagonal"] = to_core(bag["low1_x"])
    exchange("third0")
    up_grad.pair()
    up_grad.along()
    into_mix(1)
    out_grad_w = Scatter(links, bag, "out_grad", *weight_grad(
        bag["table"], bag.take("low_all0", "low_all1"), bag.take("gated0", "gated1"), 512, 1))
    bag.fence()

    across("third0")
    up_grad.pair()
    up_grad.along()
    down_grad.along()
    mix_back(1)
    bag.fence()

    exchange("third1")
    bag.fence()

    def leave(micro):
        grad = summed(f"third{micro}")
        inverse = bag[f"inverse_one{micro}"]
        unit = block_in[micro].astype(f32) * inverse
        bag[f"input_grad{micro}"] = bag[f"grad_middle{micro}"] + norm_back(grad, unit, inverse, gain_one)
        bag[f"gain_one{micro}"] = jnp.sum(grad * unit, axis=0)

    across("third1")
    out_grad_w.pair()
    down_grad.along()
    gates_grads = [bag.pop(f"gates_grad{micro}").reshape(2, links.dp, gate_columns, channels) for micro in range(2)]
    first_grad = Scatter(links, bag, "first_grad", *weight_grad(
        bag["table"], bag.take("normed_all0", "normed_all1"), bag.take("grad_branch0", "grad_branch1"), channels, 4,
        gates_grads))
    leave(0)
    bag.fence()

    first_grad.pair()
    small = AllSum(bag, "small", bag.pop("small0") + bag.pop("small1"), [("dp", links.dp)])
    small.step()
    out_grad_w.along()
    leave(1)
    gains = jnp.stack([bag.pop("gain_one0") + bag.pop("gain_one1"), bag.pop("gain_two0") + bag.pop("gain_two1")])
    gains = AllSum(bag, "gains", gains, [("mp", links.mp), ("dp", links.dp)])
    bag.fence()

    first_grad.pair()
    first_grad.along()
    gains.step()
    gains.step()
    small.step()
    output_of(0)
    bag["up_total"] = up_grad.finish(write_gate_up, (d_rows, hidden_units), (d_rows, hidden_units))
    bag.fence()

    first_grad.pair()
    first_grad.along()
    out_grad_w.along()
    gains.step()
    small.step()
    output_of(1)
    bag["down_total"] = down_grad.finish(write_turned, (hidden_units, d_rows))
    bag.fence()

    first_grad.pair()
    first_grad.along()
    out_grad_w.along()
    gains.step()
    gains.step()
    bag["outputs"] = jnp.stack(bag.take("output0", "output1"))
    bag["input_grads"] = jnp.stack([bag.pop("input_grad0"), bag.pop("input_grad1")])
    bag.fence()

    bag["out_total"] = out_grad_w.finish(write_turned, (channels, d_rows))
    x_grad, y_grad, recur, inp = first_grad.finish(
        write_first, (d_rows, channels), (d_rows, channels), (blocks, BS, gate_columns), (blocks, BS, gate_columns))
    gains = gains.finish()
    small = small.finish()
    return (
        bag["outputs"],
        bag["input_grads"],
        gains[0],
        x_grad,
        y_grad,
        small[0:KW],
        recur,
        inp,
        small[KW],
        bag["out_total"][0],
        gains[1],
        *bag["up_total"],
        bag["down_total"][0],
    )


def solution(mesh):
    links = Links(mesh.shape["dp"], mesh.shape["mp"])
    tokens = P(None, ("dp", "mp"), None)
    rows, columns, gate = P("dp", "mp"), P("mp", "dp"), P("mp", None, "dp")
    return jax.shard_map(
        functools.partial(body, links),
        mesh=mesh,
        in_specs=(tokens, P(None, "dp"), P(), rows, rows, P(None, "mp"), gate, gate, P("mp"), columns, P(), rows,
                  rows, columns, tokens),
        out_specs=(tokens, tokens, P(), rows, rows, P(None, "mp"), gate, gate, P("mp"), columns, P(), rows, rows,
                   columns),
        check_vma=False,
    )
```

```python
import functools

import jax
import jax.numpy as jnp
import numpy as np
from jax import lax
from jax.experimental import pallas as pl
from jax.experimental.pallas import tpu as pltpu
from jax.sharding import PartitionSpec as P

LEN = 1024
BS = 128
KW = 4

norm_eps = 1e-06
root_floor = 0.01
decay_scale = 8.0
gelu_a = 0.7978845608028654
gelu_b = 0.044715

f32 = jnp.float32
bf16 = jnp.bfloat16


BLOCK_AT = (2, 0, 3, 1)


def project(left, right):
    return jnp.dot(left, right, preferred_element_type=f32)


def inner(left, right):
    return lax.dot_general(left, right, (((0,), (0,)), ((), ())), preferred_element_type=f32)


def against(left, right):
    return lax.dot_general(left, right, (((1,), (1,)), ((), ())), preferred_element_type=f32)


def norm_back(grad_normed, unit_rows, inverse, gain):
    scaled = grad_normed * gain
    return inverse * (scaled - unit_rows * jnp.mean(scaled * unit_rows, axis=-1, keepdims=True))


def gelu_parts(v):
    squared = v * v
    inside = gelu_a * v * (1.0 + gelu_b * squared)
    t = jnp.tanh(inside)
    half = 0.5 * (1.0 + t)
    value = v * half
    slope = half + 0.5 * v * (1.0 - t * t) * (gelu_a * (1.0 + 3.0 * gelu_b * squared))
    return value, slope


def gelu_value(v):
    return 0.5 * v * (1.0 + jnp.tanh(gelu_a * v * (1.0 + gelu_b * v * v)))


def place_of(me, block):
    differ = lax.bitwise_xor(me, block)
    low = lax.bitwise_and(differ, 1)
    high = lax.shift_right_logical(differ, 1)
    return 2 * (1 - low) + high


CHUNK = 64
STEP = 32


def tile_scan(a, b, row):
    for d in (1, 2, 4):
        use = row >= d
        b = b + a * jnp.where(use, pltpu.roll(b, d, 0), 0.0)
        a = a * jnp.where(use, pltpu.roll(a, d, 0), 1.0)
    return a, b


def tile_scan_back(a, b, row):
    for d in (1, 2, 4):
        use = row < 8 - d
        b = b + a * jnp.where(use, pltpu.roll(b, 8 - d, 0), 0.0)
        a = a * jnp.where(use, pltpu.roll(a, 8 - d, 0), 1.0)
    return a, b


def spread(row):
    return jnp.broadcast_to(row, (8, BS))


def mixing_forward_kernel(me_ref, branch, ids, taps, gate_r, gate_i, rate, gated, states, conv, sig_r, sig_i,
                          xpad, idpad, logits, gates):
    gates[0:BS, :] = gate_r[...]
    gates[BS:2 * BS, :] = gate_i[...]
    rows = LEN
    quarter = rows // 4
    me = me_ref[0]
    xpad[0:8, :] = jnp.zeros((8, BS), f32)
    idpad[0:8, :] = jnp.full((8, BS), -1, jnp.int32)
    idpad[8:8 + rows, :] = ids[...]
    for block in range(4):
        at = place_of(me, block)
        xpad[8 + block * quarter: 8 + (block + 1) * quarter, :] = branch[at, :, 0:BS]
    rate_row = rate[0:1, :]

    def convolve(step, _):
        base = pl.multiple_of(step * CHUNK, CHUNK)
        own_ids = idpad[pl.ds(base + 8, CHUNK), :]
        total = taps[0:1, :] * xpad[pl.ds(base + 8, CHUNK), :]
        for k in range(1, KW):
            same = idpad[pl.ds(base + 8 - k, CHUNK), :] == own_ids
            total = total + taps[k:k + 1, :] * jnp.where(same, xpad[pl.ds(base + 8 - k, CHUNK), :], 0.0)
        conv[pl.ds(base, CHUNK), :] = total.astype(bf16)
        return 0

    lax.fori_loop(0, rows // CHUNK, convolve, 0, unroll=2)
    logits[...] = lax.dot_general(conv[...], gates[...], (((1,), (1,)), ((), ())), preferred_element_type=f32)
    row = lax.broadcasted_iota(jnp.int32, (8, BS), 0)

    def advance(step, carry):
        base = pl.multiple_of(step * STEP, STEP)
        here = pl.ds(base, STEP)
        block = lax.div(step, quarter // STEP)
        at = place_of(me, block)
        there = pl.ds(pl.multiple_of(base - block * quarter, STEP), STEP)
        sr = jax.nn.sigmoid(logits[here, 0:BS])
        si = jax.nn.sigmoid(logits[here, BS:2 * BS])
        sig_r[here, :] = sr
        sig_i[here, :] = si
        same = idpad[pl.ds(base + 7, STEP), :] == idpad[pl.ds(base + 8, STEP), :]
        a = jnp.where(same, jnp.exp(rate_row * sr), 0.0)
        margin = jnp.maximum(1.0 - a * a, root_floor)
        b = conv[here, :].astype(f32) * si * (margin * lax.rsqrt(margin))
        tiles = []
        for k in range(STEP // 8):
            part = slice(8 * k, 8 * k + 8)
            product, local = tile_scan(a[part], b[part], row)
            tiles.append(local + product * carry)
            carry = spread(local[7:8]) + spread(product[7:8]) * carry
        state = jnp.concatenate(tiles, axis=0)
        states[here, :] = state
        gated[at, there, :] = (state * gelu_value(branch[at, there, BS:2 * BS])).astype(bf16)
        return carry

    lax.fori_loop(0, rows // STEP, advance, jnp.zeros((8, BS), f32), unroll=2)


def mixing_backward_kernel(me_ref, grad_gated, branch, states, conv, sig_r, sig_i, ids, taps, gate_r, gate_i, rate,
                           slope, grad_branch, grad_gates, small,
                           xpad, idpad, spad, low, gcpad, through, gates):
    gates[0:BS, :] = gate_r[...]
    gates[BS:2 * BS, :] = gate_i[...]
    rows = LEN
    quarter = rows // 4
    me = me_ref[0]
    zero8 = jnp.zeros((8, BS), f32)
    xpad[0:8, :] = zero8
    spad[0:8, :] = zero8
    spad[8:8 + rows, :] = states[...]
    idpad[0:8, :] = jnp.full((8, BS), -1, jnp.int32)
    idpad[8:8 + rows, :] = ids[...]
    idpad[8 + rows:16 + rows, :] = jnp.full((8, BS), -1, jnp.int32)
    gcpad[rows:rows + 8, :] = zero8
    rate_row = rate[0:1, :]
    slope_row = slope[0:1, :]
    for block in range(4):
        at = place_of(me, block)
        xpad[8 + block * quarter: 8 + (block + 1) * quarter, :] = branch[at, :, 0:BS]
    row = lax.broadcasted_iota(jnp.int32, (8, BS), 0)
    fold = lambda v: jnp.sum(v.reshape(v.shape[0] // 8, 8, BS), axis=0)
    steps = rows // STEP

    def retreat(count, held):
        carry, decay_sum = held
        step = steps - 1 - count
        base = pl.multiple_of(step * STEP, STEP)
        here = pl.ds(base, STEP)
        block = lax.div(step, quarter // STEP)
        at = place_of(me, block)
        there = pl.ds(pl.multiple_of(base - block * quarter, STEP), STEP)
        value, gradient = gelu_parts(branch[at, there, BS:2 * BS])
        incoming = grad_gated[at, there, :]
        grad_states = incoming * value
        grad_branch[at, there, BS:2 * BS] = (gradient * states[here, :] * incoming).astype(bf16)
        same = idpad[pl.ds(base + 7, STEP), :] == idpad[pl.ds(base + 8, STEP), :]
        sr = sig_r[here, :]
        si = sig_i[here, :]
        a = jnp.where(same, jnp.exp(rate_row * sr), 0.0)
        pushed = a * grad_states
        us, gs = [], []
        for k in reversed(range(STEP // 8)):
            part = slice(8 * k, 8 * k + 8)
            product, local = tile_scan_back(a[part], pushed[part], row)
            u = local + product * carry
            us.insert(0, u)
            gs.insert(0, grad_states[part] + jnp.where(row == 7, carry, pltpu.roll(u, 7, 0)))
            carry = spread(local[0:1]) + spread(product[0:1]) * carry
        u = jnp.concatenate(us, axis=0)
        g = jnp.concatenate(gs, axis=0)
        square = a * a
        inside = 1.0 - square
        margin = jnp.maximum(inside, root_floor)
        inverse = lax.rsqrt(margin)
        multiplier = margin * inverse
        gsi = g * si
        gcsi = gsi * conv[here, :].astype(f32)
        grad_log = u * spad[pl.ds(base + 7, STEP), :] - jnp.where(inside > root_floor, gcsi * square * inverse, 0.0)
        gcpad[here, :] = gsi * multiplier
        weighted = grad_log * sr
        low[here, 0:BS] = (weighted * (1.0 - sr) * rate_row).astype(bf16)
        low[here, BS:2 * BS] = (gcsi * multiplier * (1.0 - si)).astype(bf16)
        return carry, decay_sum + fold(weighted)

    _, decay_sum = lax.fori_loop(0, steps, retreat, (zero8, zero8), unroll=2)

    both_gates = lax.dot_general(low[...], conv[...], (((0,), (0,)), ((), ())), preferred_element_type=f32)
    grad_gates[0] = both_gates[0:BS]
    grad_gates[1] = both_gates[BS:2 * BS]
    through[...] = lax.dot_general(low[...], gates[...], (((1,), (0,)), ((), ())), preferred_element_type=f32)

    def add_gates(step, _):
        here = pl.ds(pl.multiple_of(step * CHUNK, CHUNK), CHUNK)
        gcpad[here, :] = gcpad[here, :] + through[here, :]
        return 0

    lax.fori_loop(0, rows // CHUNK, add_gates, 0, unroll=4)

    def finish(step, sums):
        base = pl.multiple_of(step * CHUNK, CHUNK)
        block = lax.div(step, quarter // CHUNK)
        at = place_of(me, block)
        there = pl.ds(pl.multiple_of(base - block * quarter, CHUNK), CHUNK)
        gc = gcpad[pl.ds(base, CHUNK), :]
        own_ids = idpad[pl.ds(base + 8, CHUNK), :]
        new = [sums[0] + fold(gc * xpad[pl.ds(base + 8, CHUNK), :])]
        grad_x = taps[0:1, :] * gc
        for k in range(1, KW):
            same = idpad[pl.ds(base + 8 - k, CHUNK), :] == own_ids
            new.append(sums[k] + fold(jnp.where(same, gc * xpad[pl.ds(base + 8 - k, CHUNK), :], 0.0)))
            after = idpad[pl.ds(base + 8 + k, CHUNK), :] == own_ids
            grad_x = grad_x + taps[k:k + 1, :] * jnp.where(after, gcpad[pl.ds(base + k, CHUNK), :], 0.0)
        grad_branch[at, there, 0:BS] = grad_x.astype(bf16)
        return tuple(new)

    sums = lax.fori_loop(0, rows // CHUNK, finish, (zero8,) * KW, unroll=2)
    small[...] = jnp.zeros((8, BS), f32)
    for k in range(KW):
        small[k:k + 1, :] = jnp.sum(sums[k], axis=0, keepdims=True)
    small[KW:KW + 1, :] = jnp.sum(decay_sum, axis=0, keepdims=True) * slope_row


def mixing_forward(me, branch, ids, taps, gates, rate):
    rows = LEN
    blocks = branch.shape[2] // (2 * BS)
    channels = blocks * BS
    flat = lambda n, me: (0, n)
    return pl.pallas_call(
        mixing_forward_kernel,
        grid_spec=pltpu.PrefetchScalarGridSpec(
            num_scalar_prefetch=1,
            grid=(blocks,),
            in_specs=[
                pl.BlockSpec((4, rows // 4, 2 * BS), lambda n, me: (0, 0, n)),
                pl.BlockSpec((rows, BS), lambda n, me: (0, 0)),
                pl.BlockSpec((8, BS), flat),
                pl.BlockSpec((BS, BS), flat),
                pl.BlockSpec((BS, BS), lambda n, me: (0, blocks + n)),
                pl.BlockSpec((8, BS), flat),
            ],
            out_specs=[
                pl.BlockSpec((4, rows // 4, BS), lambda n, me: (0, 0, n)),
                pl.BlockSpec((rows, BS), flat),
                pl.BlockSpec((rows, BS), flat),
                pl.BlockSpec((rows, BS), flat),
                pl.BlockSpec((rows, BS), flat),
            ],
            scratch_shapes=[
                pltpu.VMEM((rows + 8, BS), f32),
                pltpu.VMEM((rows + 8, BS), jnp.int32),
                pltpu.VMEM((rows, 2 * BS), f32),
                pltpu.VMEM((2 * BS, BS), bf16),
            ],
        ),
        out_shape=[
            jax.ShapeDtypeStruct((4, rows // 4, channels), bf16),
            hbm_out((rows, channels), f32),
            hbm_out((rows, channels), bf16),
            hbm_out((rows, channels), f32),
            hbm_out((rows, channels), f32),
        ],
        compiler_params=vmem(16),
        name="mixing_forward",
    )(me, in_hbm(branch), ids, taps, gates, gates, rate)


def mixing_backward(me, grad_gated, branch, states, conv, sig_r, sig_i, ids, taps, gates, rate, slope):
    rows = LEN
    blocks = branch.shape[2] // (2 * BS)
    channels = blocks * BS
    flat = lambda n, me: (0, n)
    cube = lambda n, me: (0, 0, n)
    return pl.pallas_call(
        mixing_backward_kernel,
        grid_spec=pltpu.PrefetchScalarGridSpec(
            num_scalar_prefetch=1,
            grid=(blocks,),
            in_specs=[
                pl.BlockSpec((4, rows // 4, BS), cube),
                pl.BlockSpec((4, rows // 4, 2 * BS), cube),
                pl.BlockSpec((rows, BS), flat),
                pl.BlockSpec((rows, BS), flat),
                pl.BlockSpec((rows, BS), flat),
                pl.BlockSpec((rows, BS), flat),
                pl.BlockSpec((rows, BS), lambda n, me: (0, 0)),
                pl.BlockSpec((8, BS), flat),
                pl.BlockSpec((BS, BS), flat),
                pl.BlockSpec((BS, BS), lambda n, me: (0, blocks + n)),
                pl.BlockSpec((8, BS), flat),
                pl.BlockSpec((8, BS), flat),
            ],
            out_specs=[
                pl.BlockSpec((4, rows // 4, 2 * BS), cube),
                pl.BlockSpec((2, BS, BS), cube),
                pl.BlockSpec((8, BS), flat),
            ],
            scratch_shapes=[
                pltpu.VMEM((rows + 8, BS), f32),
                pltpu.VMEM((rows + 16, BS), jnp.int32),
                pltpu.VMEM((rows + 8, BS), f32),
                pltpu.VMEM((rows, 2 * BS), bf16),
                pltpu.VMEM((rows + 8, BS), f32),
                pltpu.VMEM((rows, BS), f32),
                pltpu.VMEM((2 * BS, BS), bf16),
            ],
        ),
        out_shape=[
            jax.ShapeDtypeStruct((4, rows // 4, 2 * channels), bf16),
            jax.ShapeDtypeStruct((2, BS, channels), f32),
            jax.ShapeDtypeStruct((8, channels), f32),
        ],
        compiler_params=vmem(24),
        name="mixing_backward",
    )(me, grad_gated, *(in_hbm(v) for v in (branch, states, conv, sig_r, sig_i)), ids, taps, gates, gates, rate, slope)


def folded(count):
    return list(range(0, 1)) + list(range(1, count, 2)) + list(range((count - 1) // 2 * 2, 0, -2))


class Links:
    def __init__(self, dp, mp):
        assert mp == 4 and dp % 2 == 0
        self.dp, self.mp = dp, mp
        self.line = dp // 2
        self.order = folded(self.line)
        self.place = {a: k for k, a in enumerate(self.order)}
        self.ring = [
            (2 * a + b, 2 * self.order[(self.place[a] + 1) % self.line] + b)
            for a in range(self.line)
            for b in range(2)
        ]

    def to_core(self, v):
        return lax.ppermute(v, "mp", [(i, i ^ 1) for i in range(self.mp)])

    def to_x(self, v):
        return lax.ppermute(v, "mp", [(i, i ^ 2) for i in range(self.mp)])

    def to_pair(self, v):
        return lax.ppermute(v, "dp", [(i, i ^ 1) for i in range(self.dp)])

    def along(self, v):
        return lax.ppermute(v, "dp", self.ring)

    def behind(self, me, steps):
        at = lax.shift_right_logical(me, 1)
        place = jnp.int32(0)
        for a in range(self.line):
            place = jnp.where(at == a, self.order[(self.place[a] - steps) % self.line], place)
        return place.astype(jnp.int32)


def in_hbm(v):
    return pltpu.with_memory_space_constraint(v, pltpu.HBM)


def hbm_out(shape, dtype):
    return pltpu.HBM(shape, dtype)


def vmem(mib):
    return pltpu.CompilerParams(vmem_limit_bytes=mib * 1024 * 1024)


UNIT = 384


def assemble(pieces, whole):
    @pl.when(pl.program_id(0) == 0)
    def _():
        rows = pieces[0].shape[0]
        for k, piece in enumerate(pieces):
            whole[k * rows:(k + 1) * rows, :] = piece[...]


def rows_call(kernel, pieces, more, more_specs, outs, out_specs, grid, flops, name, mib, scratch=(), streamed=False):
    own, width = pieces[0].shape
    count = len(pieces)
    whole = pl.BlockSpec((count * own, width), lambda n: (0, 0))
    joined = count > 1

    def run(*refs):
        x, others = refs[0], refs[count:]
        if joined:
            x = refs[count + len(more)]
            assemble(refs[:count], x)
            others = refs[count:count + len(more)] + refs[count + len(more) + 1:]
        kernel(x, *others)

    moved = sum(2 * v.size * v.dtype.itemsize for v in (*pieces, *more))
    if streamed:
        pieces, more = [in_hbm(v) for v in pieces], [in_hbm(v) for v in more]
        outs = [hbm_out(v.shape, v.dtype) for v in outs]
    return pl.pallas_call(
        run,
        grid=(grid,),
        in_specs=[pl.BlockSpec((own, width), lambda n: (0, 0))] * count + more_specs,
        out_specs=[whole] * joined + out_specs,
        out_shape=[jax.ShapeDtypeStruct((count * own, width), bf16)] * joined + outs,
        scratch_shapes=list(scratch),
        compiler_params=vmem(mib),
        name=name,
    )(*pieces, *more)


def against_kernel(x, w, send, keep):
    half = send.shape[0]
    result = lax.dot_general(x[...], w[...], (((1,), (1,)), ((), ())), preferred_element_type=f32).astype(bf16)
    send[...] = result[:half]
    keep[...] = result[half:]


def against_rows(x, w, name):
    rows, depth = x.shape
    width = w.shape[0]
    tile = 256
    half = pl.BlockSpec((rows // 2, tile), lambda n: (0, n))
    return rows_call(
        against_kernel, [x], [w], [pl.BlockSpec((tile, depth), lambda n: (n, 0))],
        [jax.ShapeDtypeStruct((rows // 2, width), bf16)] * 2, [half] * 2, width // tile,
        2 * rows * width * depth, name, 20)


def project_kernel(x, w, out):
    out[...] = jnp.dot(x[...], w[...], preferred_element_type=f32)


def project_rows(pieces, w, tile, name, out=jax.ShapeDtypeStruct):
    own, width = pieces[0].shape
    columns = w.shape[1]
    return rows_call(
        project_kernel, pieces, [w], [pl.BlockSpec((width, tile), lambda n: (0, n))],
        [out((4 * own, columns), f32)], [pl.BlockSpec((4 * own, tile), lambda n: (0, n))],
        columns // tile, 8 * own * width * columns, name, 24)


def ffn_forward_kernel(x, w, hidden, by_gate, by_up):
    both = jnp.dot(x[...], w[...], preferred_element_type=f32)
    up = both[:, UNIT:]
    value, slope = gelu_parts(both[:, :UNIT])
    hidden[...] = (value * up).astype(bf16)
    by_gate[...] = (up * slope).astype(bf16)
    by_up[...] = value.astype(bf16)


def ffn_forward(pieces, w):
    own, width = pieces[0].shape
    units = w.shape[1] // 2
    tile = pl.BlockSpec((4 * own, UNIT), lambda n: (0, n))
    return rows_call(
        ffn_forward_kernel, pieces, [w], [pl.BlockSpec((width, 2 * UNIT), lambda n: (0, n))],
        [jax.ShapeDtypeStruct((4 * own, units), bf16)] * 3, [tile] * 3,
        units // UNIT, 16 * own * width * units, "ffn_forward", 34, streamed=True)


def ffn_backward_kernel(x, w, by_gate, by_up, w_up, out, send, keep, total):
    grad = jnp.dot(x[...], w[...], preferred_element_type=f32)
    out[:, :UNIT] = (grad * by_gate[...].astype(f32)).astype(bf16)
    out[:, UNIT:] = (grad * by_up[...].astype(f32)).astype(bf16)
    more = lax.dot_general(out[...], w_up[...], (((1,), (1,)), ((), ())), preferred_element_type=f32)
    at, last = pl.program_id(0), pl.num_programs(0) - 1

    @pl.when(at == 0)
    def _():
        total[...] = more

    @pl.when(jnp.logical_and(at > 0, at < last))
    def _():
        total[...] += more

    @pl.when(at == last)
    def _():
        half = send.shape[0]
        result = (total[...] + more).astype(bf16)
        send[...] = result[:half]
        keep[...] = result[half:]


def ffn_backward(x, w, by_gate, by_up, w_up):
    rows, width = x.shape
    units = w.shape[1]
    assert units // UNIT > 1
    tile = pl.BlockSpec((rows, UNIT), lambda n: (0, n))
    half = pl.BlockSpec((rows // 2, width), lambda n: (0, 0))
    return rows_call(
        ffn_backward_kernel, [x], [w, by_gate, by_up, w_up],
        [pl.BlockSpec((width, UNIT), lambda n: (0, n)), tile, tile,
         pl.BlockSpec((width, 2 * UNIT), lambda n: (0, n))],
        [jax.ShapeDtypeStruct((rows, 2 * units), bf16)] + [jax.ShapeDtypeStruct((rows // 2, width), bf16)] * 2,
        [pl.BlockSpec((rows, 2 * UNIT), lambda n: (0, n)), half, half],
        units // UNIT, 6 * rows * width * units, "ffn_backward", 46, [pltpu.VMEM((rows, width), f32)],
        streamed=True)


def pack_kernel(x, y, out, recur, inp, packed):
    rows, channels = x.shape
    columns = recur.shape[1]
    for n in range(channels // BS):
        block = slice(n * BS, (n + 1) * BS)
        packed[0:rows, 2 * n * BS:(2 * n + 1) * BS] = x[:, block]
        packed[0:rows, (2 * n + 1) * BS:(2 * n + 2) * BS] = y[:, block]
        packed[rows:rows + columns, block] = recur[n]
        packed[rows:rows + columns, channels + n * BS:channels + (n + 1) * BS] = inp[n]
    packed[0:rows, 2 * channels:3 * channels] = out[...]
    packed[rows:rows + columns, 2 * channels:3 * channels] = jnp.zeros((columns, channels), bf16)


def pack(x, y, out, recur, inp):
    rows, channels = x.shape
    return pl.pallas_call(
        pack_kernel,
        out_shape=jax.ShapeDtypeStruct((rows + recur.shape[1], 3 * channels), bf16),
        name="pack",
    )(x, y, out, recur, inp)


def weight_grad_kernel(line, shard, extra, groups, table, *refs):
    if extra:
        left_a, right_a, left_b, right_b, extra_a, extra_b, *sent, kept, total = refs
    else:
        left_a, right_a, left_b, right_b, *sent, kept, total = refs
    dims = (((0,), (0,)), ((), ()))
    total[...] = lax.dot_general(
        left_a[...], right_a[...], dims, preferred_element_type=f32
    ) + lax.dot_general(left_b[...], right_b[...], dims, preferred_element_type=f32)
    bit = table[line]
    size = line // groups
    for k in range(line):
        at = 2 * table[k]
        out = sent[k // size]
        mine = pl.ds(pl.multiple_of((at + bit) * shard, 16), shard)
        other = pl.ds(pl.multiple_of((at + 1 - bit) * shard, 16), shard)
        kept[k, 0:shard, :] = total[mine, :]
        out[k % size, 0:shard, :] = total[other, :].astype(bf16)
        if extra:
            kept[k, shard:shard + extra, :] = extra_a[0, at + bit] + extra_b[0, at + bit]
            out[k % size, shard:shard + extra, :] = (
                extra_a[0, at + 1 - bit] + extra_b[0, at + 1 - bit]).astype(bf16)


def weight_grad(table, left, right, tile, groups, extras=None):
    line = table.shape[0] - 1
    rows, width = left[0].shape
    columns = right[0].shape[1]
    shard = width // (2 * line)
    extra = extras[0].shape[2] if extras else 0
    lefts = pl.BlockSpec((rows, width), lambda n, t: (0, 0))
    rights = pl.BlockSpec((rows, tile), lambda n, t: (0, n))
    more = [pl.BlockSpec((1, 2 * line, extra, tile), lambda n, t: (n, 0, 0, 0))] * 2 if extra else []
    parts = lambda count: pl.BlockSpec((count, shard + extra, tile), lambda n, t: (0, 0, n))
    size = line // groups
    *sent, kept = pl.pallas_call(
        functools.partial(weight_grad_kernel, line, shard, extra, groups),
        grid_spec=pltpu.PrefetchScalarGridSpec(
            num_scalar_prefetch=1,
            grid=(columns // tile,),
            in_specs=[lefts, rights, lefts, rights] + more,
            out_specs=[parts(size)] * groups + [parts(line)],
            scratch_shapes=[pltpu.VMEM((width, tile), f32)],
        ),
        out_shape=[jax.ShapeDtypeStruct((size, shard + extra, columns), bf16)] * groups
        + [jax.ShapeDtypeStruct((line, shard + extra, columns), f32)],
        compiler_params=vmem(44),
        name="weight_grad",
    )(table, in_hbm(left[0]), in_hbm(right[0]), in_hbm(left[1]), in_hbm(right[1]), *(extras or ()))
    return sent, kept


def last_sum(write, held, at, outs, name):
    kept, sent, moving = held["kept"], held["sent"][at // held["size"]], held["moving"]
    shape = (1,) + kept.shape[1:]
    inside = at % held["size"]

    def kernel(kept, sent, moving, *outs):
        write(kept[0] + sent[0].astype(f32) + moving[...].astype(f32), *outs)

    return pl.pallas_call(
        kernel,
        grid=(1,),
        in_specs=[pl.BlockSpec(shape, lambda n: (at, 0, 0)), pl.BlockSpec(shape, lambda n: (inside, 0, 0)),
                  pl.BlockSpec(shape[1:], lambda n: (0, 0))],
        out_specs=[pl.BlockSpec(out, lambda n, rank=len(out): (0,) * rank) for out in outs],
        out_shape=[jax.ShapeDtypeStruct(out, f32) for out in outs],
        compiler_params=vmem(16),
        name=name,
    )(kept, sent, moving)


def write_plain(total, out):
    out[...] = total


def write_gate_up(total, gate, up):
    for k in range(gate.shape[1] // UNIT):
        gate[:, k * UNIT:(k + 1) * UNIT] = total[:, 2 * k * UNIT:(2 * k + 1) * UNIT]
        up[:, k * UNIT:(k + 1) * UNIT] = total[:, (2 * k + 1) * UNIT:(2 * k + 2) * UNIT]


def write_first(total, x, y, recur, inp):
    rows, channels = x.shape
    for n in range(channels // BS):
        block = slice(n * BS, (n + 1) * BS)
        x[:, block] = total[:rows, 2 * n * BS:(2 * n + 1) * BS]
        y[:, block] = total[:rows, (2 * n + 1) * BS:(2 * n + 2) * BS]
        recur[n] = total[rows:, block]
        inp[n] = total[rows:, channels + n * BS:channels + (n + 1) * BS]


class Bag(dict):
    def fence(self):
        values, tree = jax.tree.flatten(dict(self))
        values = lax.optimization_barrier(values)
        self.update(jax.tree.unflatten(tree, values))

    def take(self, *names):
        out = [self.pop(name) for name in names]
        return out if len(out) > 1 else out[0]


class Gather:
    def __init__(self, links, me, bag, name, shard, parts=None):
        self.links, self.me, self.bag, self.name = links, me, bag, name
        self.along_steps, self.pair_steps, self.placed, self.other_placed = 0, 0, 0, 0
        self.parts = parts or [(slice(0, shard.shape[0]), slice(0, shard.shape[1]))]
        bag[name] = {"z": [shard], "y": [], "whole": None}

    def along(self, steps=1):
        z = self.bag[self.name]["z"]
        for _ in range(steps):
            if self.along_steps < self.links.line - 1:
                z.append(self.links.along(z[self.along_steps]))
                self.along_steps += 1

    def pair(self, steps=1):
        held = self.bag[self.name]
        for _ in range(steps):
            if self.pair_steps <= self.along_steps and self.pair_steps < self.links.line:
                held["y"].append(self.links.to_pair(held["z"][self.pair_steps]))
                self.pair_steps += 1

    def put(self, pieces, at, bit):
        held = self.bag[self.name]
        base = 2 * self.links.behind(self.me, at)
        wholes = []
        for k, (rows, columns) in enumerate(self.parts):
            piece = pieces[at][rows, columns][None]
            whole = jnp.zeros((self.links.dp,) + piece.shape[1:], bf16) if held["whole"] is None else held["whole"][k]
            wholes.append(lax.dynamic_update_slice(whole, piece, (base + bit, 0, 0)))
        held["whole"] = wholes

    def place(self, z=0, y=0):
        held = self.bag[self.name]
        bit = lax.bitwise_and(self.me, 1)
        for _ in range(z):
            if self.placed <= self.along_steps:
                self.put(held["z"], self.placed, bit)
                self.placed += 1
        for _ in range(y):
            if self.other_placed < self.pair_steps:
                self.put(held["y"], self.other_placed, 1 - bit)
                self.other_placed += 1
        for k in range(min(self.placed, self.pair_steps, self.along_steps)):
            held["z"][k] = None
        for k in range(self.other_placed):
            held["y"][k] = None

    def finish(self):
        line = self.links.line
        while self.pair_steps < line:
            self.along()
            self.pair()
        self.place(line, line)
        return self.bag.pop(self.name)["whole"]


class Scatter:
    def __init__(self, links, bag, name, sent, kept):
        self.links, self.bag, self.name = links, bag, name
        self.pair_steps, self.along_steps = 0, 0
        self.size = links.line // len(sent)
        bag[name] = {"sent": list(sent), "kept": kept, "moving": None}

    def pair(self):
        sent = self.bag[self.name]["sent"]
        if self.pair_steps < len(sent):
            sent[self.pair_steps] = self.links.to_pair(sent[self.pair_steps])
            self.pair_steps += 1

    def along(self):
        held = self.bag[self.name]
        at = self.along_steps
        if at < self.links.line - 1 and at // self.size < self.pair_steps:
            held["moving"] = self.links.along(self.sum_here().astype(bf16))
            self.along_steps += 1

    def sum_here(self):
        held = self.bag[self.name]
        at = self.along_steps
        total = held["kept"][at] + held["sent"][at // self.size][at % self.size].astype(f32)
        if held["moving"] is not None:
            total = total + held["moving"].astype(f32)
        return total

    def finish(self, write, *outs):
        while self.pair_steps < len(self.bag[self.name]["sent"]):
            self.pair()
        while self.along_steps < self.links.line - 1:
            self.along()
        held = self.bag.pop(self.name)
        return last_sum(write, {**held, "size": self.size}, self.along_steps, outs, self.name)


class AllSum:
    def __init__(self, bag, name, value, axes):
        self.bag, self.name = bag, name
        self.steps = [(axis, count, 1 << k) for axis, count in axes for k in range(count.bit_length() - 1)]
        assert all(count & (count - 1) == 0 for _, count in axes)
        bag[name] = value

    def step(self):
        if self.steps:
            axis, count, bit = self.steps.pop(0)
            value = self.bag[self.name]
            self.bag[self.name] = value + lax.ppermute(value, axis, [(i, i ^ bit) for i in range(count)])

    def finish(self):
        while self.steps:
            self.step()
        return self.bag.pop(self.name)


def body(links, block_in, doc_ids, mix_gain, proj_x, proj_y, conv_taps, recur_gate, input_gate, decay_param,
         proj_out, ffn_gain, ffn_gate, ffn_up, ffn_down, out_grad):
    micro_count, own_rows, width = block_in.shape
    group_rows = doc_ids.shape[1]
    assert group_rows == LEN and own_rows * 4 == group_rows and micro_count == 2
    d_rows, channels = proj_x.shape
    blocks = channels // BS
    hidden_units = ffn_gate.shape[1]
    assert hidden_units % UNIT == 0
    gate_columns = recur_gate.shape[2]
    dp_me = lax.axis_index("dp")
    me = lax.axis_index("mp").astype(jnp.int32).reshape(1)
    gain_one = mix_gain.astype(f32)
    gain_two = ffn_gain.astype(f32)
    to_core, to_x = links.to_core, links.to_x
    bag = Bag()

    def exchange(name):
        send, keep = bag.pop(name + "_send"), bag.pop(name + "_keep")
        own_rows_of = lambda v, k: v[k * own_rows:(k + 1) * own_rows].astype(f32)
        sent = to_core(send)
        bag[name + "_own"] = (keep, sent)
        bag[name + "_x"] = (own_rows_of(keep, 1) + own_rows_of(sent, 1)).astype(bf16)

    def summed(name):
        keep, sent = bag.pop(name + "_own")
        return (keep[:own_rows].astype(f32) + sent[:own_rows].astype(f32)) + bag.pop(name + "_x").astype(f32)

    def across(name):
        bag[name + "_x"] = to_x(bag[name + "_x"])

    def rows_of(name):
        own, core, x, diagonal = bag.take(name, name + "_core", name + "_x", name + "_diagonal")
        return core, diagonal, own, x

    packed = pack(proj_x, proj_y, proj_out.T, jnp.swapaxes(recur_gate, 1, 2), jnp.swapaxes(input_gate, 1, 2))
    inner_rows, outer_rows = slice(0, d_rows), slice(d_rows, d_rows + gate_columns)
    wide, narrow = slice(0, 2 * channels), slice(2 * channels, 3 * channels)
    first = Gather(links, dp_me, bag, "first", packed, [(inner_rows, wide), (inner_rows, narrow), (outer_rows, wide)])
    bag.fence()

    bag["cot0"], bag["cot1"] = out_grad[0], out_grad[1]
    first.along()
    first.pair()
    for micro in range(2):
        xin = block_in[micro].astype(f32)
        inverse = lax.rsqrt(jnp.mean(xin * xin, axis=-1, keepdims=True) + norm_eps)
        bag[f"inverse_one{micro}"] = inverse
        bag[f"normed{micro}"] = (xin * inverse * gain_one).astype(bf16)
    bag.fence()

    first.along()
    first.pair()
    bag["normed0_x"] = to_x(bag["normed0"])
    bag["normed0_core"] = to_core(bag["normed0"])
    first.place(2, 1)
    decay_values = decay_param.astype(f32)
    bag["rate"] = jnp.broadcast_to((-decay_scale * jax.nn.softplus(-decay_values))[None], (8, channels))
    bag["slope"] = jnp.broadcast_to((decay_scale * jax.nn.sigmoid(-decay_values))[None], (8, channels))
    bag["taps"] = jnp.concatenate([conv_taps.astype(f32), jnp.zeros((8 - KW, channels), f32)])
    bag["table"] = jnp.stack(
        [links.behind(dp_me, step + 1) for step in range(links.line)] + [lax.bitwise_and(dp_me, 1).astype(jnp.int32)])
    bag.fence()

    first.along()
    first.pair()
    bag["normed1_x"] = to_x(bag["normed1"])
    bag["normed0_diagonal"] = to_core(bag["normed0_x"])
    first.place(1, 1)
    gate_up = jnp.stack([ffn_gate.reshape(d_rows, -1, UNIT), ffn_up.reshape(d_rows, -1, UNIT)], axis=2)
    second = Gather(links, dp_me, bag, "second", gate_up.reshape(d_rows, 2 * hidden_units))
    third = Gather(links, dp_me, bag, "third", ffn_down.T)
    for micro in range(2):
        bag[f"ids{micro}"] = jnp.broadcast_to(doc_ids[micro][:, None], (group_rows, BS))
    bag.fence()

    first.pair()
    third.along()
    third.pair()
    bag["cot0_x"] = to_x(bag["cot0"])
    first.place(1, 1)
    bag.fence()

    def mix(micro):
        bag[f"normed_all{micro}"], branch = project_rows(rows_of(f"normed{micro}"), bag["w_branch"], 256, "branch", hbm_out)
        branch = branch.reshape(4, own_rows, 2 * channels)
        gated, *rest = mixing_forward(me, branch, bag[f"ids{micro}"], bag["taps"], bag["gates"], bag["rate"])
        bag[f"mixed{micro}"] = [branch] + rest
        bag[f"gated{micro}"] = gated.reshape(group_rows, channels)

    def against_of(name, left, weight):
        bag[name + "_send"], bag[name + "_keep"] = against_rows(bag[left], bag[weight], weight + "_turned")

    def middle_of(micro):
        middle = block_in[micro].astype(f32) + summed(f"first{micro}")
        inverse = lax.rsqrt(jnp.mean(middle * middle, axis=-1, keepdims=True) + norm_eps)
        bag[f"middle{micro}"], bag[f"inverse_two{micro}"] = middle, inverse
        bag[f"two{micro}"] = (middle * inverse * gain_two).astype(bf16)

    second.along()
    third.along()
    second.pair()
    third.pair()
    w_branch, w_out, gates = first.finish()
    bag["w_branch"] = w_branch.reshape(width, 2 * channels)
    bag["gates"] = gates.reshape(BS, 2 * channels)
    bag["w_out"] = w_out.reshape(width, channels)
    mix(0)
    against_of("first0", "gated0", "w_out")
    bag.fence()

    bag["normed1_core"] = to_core(bag["normed1"])
    bag["normed1_diagonal"] = to_core(bag["normed1_x"])
    exchange("first0")
    second.place(1)
    bag.fence()

    second.along()
    third.along()
    second.pair()
    across("first0")
    second.place(1)
    mix(1)
    bag.fence()

    bag["cot0_core"] = to_core(bag["cot0"])
    middle_of(0)
    against_of("first1", "gated1", "w_out")
    bag.fence()

    second.along()
    second.pair()
    bag["two0_x"] = to_x(bag["two0"])
    bag["two0_core"] = to_core(bag["two0"])
    exchange("first1")
    second.place(2, 2)
    third.place(3, 2)
    bag.fence()

    def forward(micro):
        bag[f"two_all{micro}"], bag[f"hidden{micro}"], *bag[f"by{micro}"] = ffn_forward(
            rows_of(f"two{micro}"), bag["w_up"])

    second.pair()
    across("first1")
    bag["two0_diagonal"] = to_core(bag["two0_x"])
    second.place(1, 1)
    third.place(1)
    bag.fence()

    middle_of(1)
    bag.fence()

    third.pair(2)
    bag["two1_x"] = to_x(bag["two1"])
    bag["cot0_diagonal"] = to_core(bag["cot0_x"])
    bag["w_up"] = second.finish()[0].reshape(width, 2 * hidden_units)
    third.place(2)
    forward(0)
    bag.fence()

    def back(micro):
        name = f"second{micro}"
        bag[f"grad_pre{micro}"], bag[name + "_send"], bag[name + "_keep"] = ffn_backward(
            bag[f"cot_all{micro}"], bag["w_down"], *bag.pop(f"by{micro}"), bag["w_up"])

    def grad_middle_of(micro):
        grad = summed(f"second{micro}")
        inverse, middle = bag[f"inverse_two{micro}"], bag[f"middle{micro}"]
        unit = middle * inverse
        total = out_grad[micro].astype(f32) + norm_back(grad, unit, inverse, gain_two)
        bag[f"grad_middle{micro}"] = total
        bag[f"gain_two{micro}"] = jnp.sum(grad * unit, axis=0)
        bag[f"low{micro}"] = total.astype(bf16)

    bag["cot1_x"] = to_x(bag["cot1"])
    bag["two1_core"] = to_core(bag["two1"])
    bag["two1_diagonal"] = to_core(bag["two1_x"])
    bag["cot_all0"] = jnp.concatenate(rows_of("cot0"))
    bag["w_down"] = third.finish()[0].reshape(width, hidden_units)
    back(0)
    bag.fence()

    bag["cot1_core"] = to_core(bag["cot1"])
    bag["cot1_diagonal"] = to_core(bag["cot1_x"])
    exchange("second0")
    bag["cot_all1"] = jnp.concatenate(rows_of("cot1"))
    forward(1)
    against_of("down0", "hidden0", "w_down")
    bag.fence()

    across("second0")
    exchange("down0")
    down_grad = Scatter(links, bag, "down_grad", *weight_grad(
        bag["table"], [bag["cot_all0"], bag["cot_all1"]], [bag["hidden0"], bag["hidden1"]], UNIT, 2))
    bag.fence()

    across("down0")
    down_grad.pair()
    back(1)
    bag.fence()

    exchange("second1")
    grad_middle_of(0)
    bag.fence()

    across("second1")
    down_grad.pair()
    bag["low0_core"] = to_core(bag["low0"])
    up_grad = Scatter(links, bag, "up_grad", *weight_grad(
        bag["table"], bag.take("two_all0", "two_all1"), bag.take("grad_pre0", "grad_pre1"), 2 * UNIT, 4))
    bag.fence()

    def output_of(micro):
        bag[f"output{micro}"] = (bag[f"middle{micro}"] + summed(f"down{micro}")).astype(bf16)

    bag["low0_x"] = to_x(bag["low0"])
    up_grad.pair()
    down_grad.along()
    grad_middle_of(1)
    against_of("down1", "hidden1", "w_down")
    bag.fence()

    def into_mix(micro):
        bag[f"low_all{micro}"], bag[f"grad_gated{micro}"] = project_rows(
            rows_of(f"low{micro}"), bag["w_out"], 256, "grad_gated")

    def mix_back(micro):
        grad, bag[f"gates_grad{micro}"], bag[f"small{micro}"] = mixing_backward(
            me, bag.pop(f"grad_gated{micro}").reshape(4, own_rows, channels), *bag.pop(f"mixed{micro}"),
            bag[f"ids{micro}"], bag["taps"], bag["gates"], bag["rate"], bag["slope"])
        bag[f"grad_branch{micro}"] = grad.reshape(group_rows, 2 * channels)
        against_of(f"third{micro}", f"grad_branch{micro}", "w_branch")

    bag["low1_x"] = to_x(bag["low1"])
    bag["low0_diagonal"] = to_core(bag["low0_x"])
    up_grad.pair()
    up_grad.along()
    exchange("down1")
    into_mix(0)
    mix_back(0)
    bag.fence()

    across("down1")
    bag["low1_core"] = to_core(bag["low1"])
    bag["low1_diagonal"] = to_core(bag["low1_x"])
    exchange("third0")
    up_grad.pair()
    up_grad.along()
    into_mix(1)
    out_grad_w = Scatter(links, bag, "out_grad", *weight_grad(
        bag["table"], bag.take("low_all0", "low_all1"), bag.take("gated0", "gated1"), 512, 1))
    bag.fence()

    across("third0")
    up_grad.pair()
    up_grad.along()
    down_grad.along()
    mix_back(1)
    bag.fence()

    exchange("third1")
    bag.fence()

    def leave(micro):
        grad = summed(f"third{micro}")
        inverse = bag[f"inverse_one{micro}"]
        unit = block_in[micro].astype(f32) * inverse
        bag[f"input_grad{micro}"] = bag[f"grad_middle{micro}"] + norm_back(grad, unit, inverse, gain_one)
        bag[f"gain_one{micro}"] = jnp.sum(grad * unit, axis=0)

    across("third1")
    out_grad_w.pair()
    down_grad.along()
    gates_grads = [bag.pop(f"gates_grad{micro}").reshape(2, links.dp, gate_columns, channels) for micro in range(2)]
    first_grad = Scatter(links, bag, "first_grad", *weight_grad(
        bag["table"], bag.take("normed_all0", "normed_all1"), bag.take("grad_branch0", "grad_branch1"), channels, 4,
        gates_grads))
    leave(0)
    bag.fence()

    first_grad.pair()
    out_grad_w.along()
    leave(1)
    gains = jnp.stack([bag.pop("gain_one0") + bag.pop("gain_one1"), bag.pop("gain_two0") + bag.pop("gain_two1")])
    bag["sums"] = gains.reshape(-1, 128)
    gain_rows = bag["sums"].shape[0]
    bag.fence()

    first_grad.pair()
    first_grad.along()
    sums = AllSum(bag, "gains", bag.pop("sums"), [("mp", links.mp)])
    small = (bag.pop("small0") + bag.pop("small1")).reshape(-1, 128)
    sums = AllSum(bag, "sums", jnp.concatenate([sums.finish(), small]), [("dp", links.dp)])
    output_of(0)
    bag["up_total"] = up_grad.finish(write_gate_up, (d_rows, hidden_units), (d_rows, hidden_units))
    bag.fence()

    first_grad.pair()
    first_grad.along()
    out_grad_w.along()
    sums.step()
    output_of(1)
    bag["down_total"] = down_grad.finish(write_plain, (d_rows, hidden_units))
    bag.fence()

    first_grad.pair()
    first_grad.along()
    out_grad_w.along()
    sums.step()
    bag["outputs"] = jnp.stack(bag.take("output0", "output1"))
    bag["input_grads"] = jnp.stack([bag.pop("input_grad0"), bag.pop("input_grad1")])
    bag.fence()

    bag["out_total"] = out_grad_w.finish(write_plain, (d_rows, channels))
    x_grad, y_grad, recur, inp = first_grad.finish(
        write_first, (d_rows, channels), (d_rows, channels), (blocks, gate_columns, BS), (blocks, gate_columns, BS))
    sums = sums.finish()
    gains = sums[:gain_rows].reshape(2, width)
    small = sums[gain_rows:].reshape(8, channels)
    return (
        bag["outputs"],
        bag["input_grads"],
        gains[0],
        x_grad,
        y_grad,
        small[0:KW],
        jnp.swapaxes(recur, 1, 2),
        jnp.swapaxes(inp, 1, 2),
        small[KW],
        bag["out_total"][0].T,
        gains[1],
        *bag["up_total"],
        bag["down_total"][0].T,
    )


def solution(mesh):
    links = Links(mesh.shape["dp"], mesh.shape["mp"])
    tokens = P(None, ("dp", "mp"), None)
    rows, columns, gate = P("dp", "mp"), P("mp", "dp"), P("mp", None, "dp")
    return jax.shard_map(
        functools.partial(body, links),
        mesh=mesh,
        in_specs=(tokens, P(None, "dp"), P(), rows, rows, P(None, "mp"), gate, gate, P("mp"), columns, P(), rows,
                  rows, columns, tokens),
        out_specs=(tokens, tokens, P(), rows, rows, P(None, "mp"), gate, gate, P("mp"), columns, P(), rows, rows,
                   columns),
        check_vma=False,
    )
```

```python
import functools

import jax
import jax.numpy as jnp
import numpy as np
from jax import lax
from jax.experimental import pallas as pl
from jax.experimental.pallas import tpu as pltpu
from jax.sharding import PartitionSpec as P

LEN = 1024
BS = 128
KW = 4

norm_eps = 1e-06
root_floor = 0.01
decay_scale = 8.0
gelu_a = 0.7978845608028654
gelu_b = 0.044715

f32 = jnp.float32
bf16 = jnp.bfloat16


BLOCK_AT = (2, 0, 3, 1)


def project(left, right):
    return jnp.dot(left, right, preferred_element_type=f32)


def inner(left, right):
    return lax.dot_general(left, right, (((0,), (0,)), ((), ())), preferred_element_type=f32)


def against(left, right):
    return lax.dot_general(left, right, (((1,), (1,)), ((), ())), preferred_element_type=f32)


def norm_back(grad_normed, unit_rows, inverse, gain):
    scaled = grad_normed * gain
    return inverse * (scaled - unit_rows * jnp.mean(scaled * unit_rows, axis=-1, keepdims=True))


def gelu_parts(v):
    squared = v * v
    inside = gelu_a * v * (1.0 + gelu_b * squared)
    t = jnp.tanh(inside)
    half = 0.5 * (1.0 + t)
    value = v * half
    slope = half + 0.5 * v * (1.0 - t * t) * (gelu_a * (1.0 + 3.0 * gelu_b * squared))
    return value, slope


def gelu_value(v):
    return 0.5 * v * (1.0 + jnp.tanh(gelu_a * v * (1.0 + gelu_b * v * v)))


def place_of(me, block):
    differ = lax.bitwise_xor(me, block)
    low = lax.bitwise_and(differ, 1)
    high = lax.shift_right_logical(differ, 1)
    return 2 * (1 - low) + high


CHUNK = 64
STEP = 32


def tile_scan(a, b, row):
    for d in (1, 2, 4):
        use = row >= d
        b = b + a * jnp.where(use, pltpu.roll(b, d, 0), 0.0)
        a = a * jnp.where(use, pltpu.roll(a, d, 0), 1.0)
    return a, b


def tile_scan_back(a, b, row):
    for d in (1, 2, 4):
        use = row < 8 - d
        b = b + a * jnp.where(use, pltpu.roll(b, 8 - d, 0), 0.0)
        a = a * jnp.where(use, pltpu.roll(a, 8 - d, 0), 1.0)
    return a, b


def spread(row):
    return jnp.broadcast_to(row, (8, BS))


def mixing_forward_kernel(me_ref, branch, ids, taps, gate_r, gate_i, rate, gated, states, conv, sig_r, sig_i,
                          xpad, idpad, logits, gates):
    gates[0:BS, :] = gate_r[...]
    gates[BS:2 * BS, :] = gate_i[...]
    rows = LEN
    quarter = rows // 4
    me = me_ref[0]
    xpad[0:8, :] = jnp.zeros((8, BS), f32)
    idpad[0:8, :] = jnp.full((8, BS), -1, jnp.int32)
    idpad[8:8 + rows, :] = ids[...]
    for block in range(4):
        at = place_of(me, block)
        xpad[8 + block * quarter: 8 + (block + 1) * quarter, :] = branch[at, :, 0:BS]
    rate_row = rate[0:1, :]

    def convolve(step, _):
        base = pl.multiple_of(step * CHUNK, CHUNK)
        own_ids = idpad[pl.ds(base + 8, CHUNK), :]
        total = taps[0:1, :] * xpad[pl.ds(base + 8, CHUNK), :]
        for k in range(1, KW):
            same = idpad[pl.ds(base + 8 - k, CHUNK), :] == own_ids
            total = total + taps[k:k + 1, :] * jnp.where(same, xpad[pl.ds(base + 8 - k, CHUNK), :], 0.0)
        conv[pl.ds(base, CHUNK), :] = total.astype(bf16)
        return 0

    lax.fori_loop(0, rows // CHUNK, convolve, 0, unroll=2)
    logits[...] = lax.dot_general(conv[...], gates[...], (((1,), (1,)), ((), ())), preferred_element_type=f32)
    row = lax.broadcasted_iota(jnp.int32, (8, BS), 0)

    def advance(step, carry):
        base = pl.multiple_of(step * STEP, STEP)
        here = pl.ds(base, STEP)
        block = lax.div(step, quarter // STEP)
        at = place_of(me, block)
        there = pl.ds(pl.multiple_of(base - block * quarter, STEP), STEP)
        sr = jax.nn.sigmoid(logits[here, 0:BS])
        si = jax.nn.sigmoid(logits[here, BS:2 * BS])
        sig_r[here, :] = sr
        sig_i[here, :] = si
        same = idpad[pl.ds(base + 7, STEP), :] == idpad[pl.ds(base + 8, STEP), :]
        a = jnp.where(same, jnp.exp(rate_row * sr), 0.0)
        margin = jnp.maximum(1.0 - a * a, root_floor)
        b = conv[here, :].astype(f32) * si * (margin * lax.rsqrt(margin))
        tiles = []
        for k in range(STEP // 8):
            part = slice(8 * k, 8 * k + 8)
            product, local = tile_scan(a[part], b[part], row)
            tiles.append(local + product * carry)
            carry = spread(local[7:8]) + spread(product[7:8]) * carry
        state = jnp.concatenate(tiles, axis=0)
        states[here, :] = state
        gated[at, there, :] = (state * gelu_value(branch[at, there, BS:2 * BS])).astype(bf16)
        return carry

    lax.fori_loop(0, rows // STEP, advance, jnp.zeros((8, BS), f32), unroll=2)


def mixing_backward_kernel(me_ref, grad_gated, branch, states, conv, sig_r, sig_i, ids, taps, gate_r, gate_i, rate,
                           slope, grad_branch, grad_gates, small,
                           xpad, idpad, spad, low, gcpad, through, gates):
    gates[0:BS, :] = gate_r[...]
    gates[BS:2 * BS, :] = gate_i[...]
    rows = LEN
    quarter = rows // 4
    me = me_ref[0]
    zero8 = jnp.zeros((8, BS), f32)
    xpad[0:8, :] = zero8
    spad[0:8, :] = zero8
    spad[8:8 + rows, :] = states[...]
    idpad[0:8, :] = jnp.full((8, BS), -1, jnp.int32)
    idpad[8:8 + rows, :] = ids[...]
    idpad[8 + rows:16 + rows, :] = jnp.full((8, BS), -1, jnp.int32)
    gcpad[rows:rows + 8, :] = zero8
    rate_row = rate[0:1, :]
    slope_row = slope[0:1, :]
    for block in range(4):
        at = place_of(me, block)
        xpad[8 + block * quarter: 8 + (block + 1) * quarter, :] = branch[at, :, 0:BS]
    row = lax.broadcasted_iota(jnp.int32, (8, BS), 0)
    fold = lambda v: jnp.sum(v.reshape(v.shape[0] // 8, 8, BS), axis=0)
    steps = rows // STEP

    def retreat(count, held):
        carry, decay_sum = held
        step = steps - 1 - count
        base = pl.multiple_of(step * STEP, STEP)
        here = pl.ds(base, STEP)
        block = lax.div(step, quarter // STEP)
        at = place_of(me, block)
        there = pl.ds(pl.multiple_of(base - block * quarter, STEP), STEP)
        value, gradient = gelu_parts(branch[at, there, BS:2 * BS])
        incoming = grad_gated[at, there, :]
        grad_states = incoming * value
        grad_branch[at, there, BS:2 * BS] = (gradient * states[here, :] * incoming).astype(bf16)
        same = idpad[pl.ds(base + 7, STEP), :] == idpad[pl.ds(base + 8, STEP), :]
        sr = sig_r[here, :]
        si = sig_i[here, :]
        a = jnp.where(same, jnp.exp(rate_row * sr), 0.0)
        pushed = a * grad_states
        us, gs = [], []
        for k in reversed(range(STEP // 8)):
            part = slice(8 * k, 8 * k + 8)
            product, local = tile_scan_back(a[part], pushed[part], row)
            u = local + product * carry
            us.insert(0, u)
            gs.insert(0, grad_states[part] + jnp.where(row == 7, carry, pltpu.roll(u, 7, 0)))
            carry = spread(local[0:1]) + spread(product[0:1]) * carry
        u = jnp.concatenate(us, axis=0)
        g = jnp.concatenate(gs, axis=0)
        square = a * a
        inside = 1.0 - square
        margin = jnp.maximum(inside, root_floor)
        inverse = lax.rsqrt(margin)
        multiplier = margin * inverse
        gsi = g * si
        gcsi = gsi * conv[here, :].astype(f32)
        grad_log = u * spad[pl.ds(base + 7, STEP), :] - jnp.where(inside > root_floor, gcsi * square * inverse, 0.0)
        gcpad[here, :] = gsi * multiplier
        weighted = grad_log * sr
        low[here, 0:BS] = (weighted * (1.0 - sr) * rate_row).astype(bf16)
        low[here, BS:2 * BS] = (gcsi * multiplier * (1.0 - si)).astype(bf16)
        return carry, decay_sum + fold(weighted)

    _, decay_sum = lax.fori_loop(0, steps, retreat, (zero8, zero8), unroll=2)

    both_gates = lax.dot_general(low[...], conv[...], (((0,), (0,)), ((), ())), preferred_element_type=f32)
    grad_gates[0] = both_gates[0:BS]
    grad_gates[1] = both_gates[BS:2 * BS]
    through[...] = lax.dot_general(low[...], gates[...], (((1,), (0,)), ((), ())), preferred_element_type=f32)

    def add_gates(step, _):
        here = pl.ds(pl.multiple_of(step * CHUNK, CHUNK), CHUNK)
        gcpad[here, :] = gcpad[here, :] + through[here, :]
        return 0

    lax.fori_loop(0, rows // CHUNK, add_gates, 0, unroll=4)

    def finish(step, sums):
        base = pl.multiple_of(step * CHUNK, CHUNK)
        block = lax.div(step, quarter // CHUNK)
        at = place_of(me, block)
        there = pl.ds(pl.multiple_of(base - block * quarter, CHUNK), CHUNK)
        gc = gcpad[pl.ds(base, CHUNK), :]
        own_ids = idpad[pl.ds(base + 8, CHUNK), :]
        new = [sums[0] + fold(gc * xpad[pl.ds(base + 8, CHUNK), :])]
        grad_x = taps[0:1, :] * gc
        for k in range(1, KW):
            same = idpad[pl.ds(base + 8 - k, CHUNK), :] == own_ids
            new.append(sums[k] + fold(jnp.where(same, gc * xpad[pl.ds(base + 8 - k, CHUNK), :], 0.0)))
            after = idpad[pl.ds(base + 8 + k, CHUNK), :] == own_ids
            grad_x = grad_x + taps[k:k + 1, :] * jnp.where(after, gcpad[pl.ds(base + k, CHUNK), :], 0.0)
        grad_branch[at, there, 0:BS] = grad_x.astype(bf16)
        return tuple(new)

    sums = lax.fori_loop(0, rows // CHUNK, finish, (zero8,) * KW, unroll=2)
    small[...] = jnp.zeros((8, BS), f32)
    for k in range(KW):
        small[k:k + 1, :] = jnp.sum(sums[k], axis=0, keepdims=True)
    small[KW:KW + 1, :] = jnp.sum(decay_sum, axis=0, keepdims=True) * slope_row


def mixing_forward(me, branch, ids, taps, gates, rate):
    rows = LEN
    blocks = branch.shape[2] // (2 * BS)
    channels = blocks * BS
    flat = lambda n, me: (0, n)
    return pl.pallas_call(
        mixing_forward_kernel,
        grid_spec=pltpu.PrefetchScalarGridSpec(
            num_scalar_prefetch=1,
            grid=(blocks,),
            in_specs=[
                pl.BlockSpec((4, rows // 4, 2 * BS), lambda n, me: (0, 0, n)),
                pl.BlockSpec((rows, BS), lambda n, me: (0, 0)),
                pl.BlockSpec((8, BS), flat),
                pl.BlockSpec((BS, BS), flat),
                pl.BlockSpec((BS, BS), lambda n, me: (0, blocks + n)),
                pl.BlockSpec((8, BS), flat),
            ],
            out_specs=[
                pl.BlockSpec((4, rows // 4, BS), lambda n, me: (0, 0, n)),
                pl.BlockSpec((rows, BS), flat),
                pl.BlockSpec((rows, BS), flat),
                pl.BlockSpec((rows, BS), flat),
                pl.BlockSpec((rows, BS), flat),
            ],
            scratch_shapes=[
                pltpu.VMEM((rows + 8, BS), f32),
                pltpu.VMEM((rows + 8, BS), jnp.int32),
                pltpu.VMEM((rows, 2 * BS), f32),
                pltpu.VMEM((2 * BS, BS), bf16),
            ],
        ),
        out_shape=[
            jax.ShapeDtypeStruct((4, rows // 4, channels), bf16),
            hbm_out((rows, channels), f32),
            hbm_out((rows, channels), bf16),
            hbm_out((rows, channels), f32),
            hbm_out((rows, channels), f32),
        ],
        compiler_params=vmem(16),
        name="mixing_forward",
    )(me, in_hbm(branch), ids, taps, gates, gates, rate)


def mixing_backward(me, grad_gated, branch, states, conv, sig_r, sig_i, ids, taps, gates, rate, slope):
    rows = LEN
    blocks = branch.shape[2] // (2 * BS)
    channels = blocks * BS
    flat = lambda n, me: (0, n)
    cube = lambda n, me: (0, 0, n)
    return pl.pallas_call(
        mixing_backward_kernel,
        grid_spec=pltpu.PrefetchScalarGridSpec(
            num_scalar_prefetch=1,
            grid=(blocks,),
            in_specs=[
                pl.BlockSpec((4, rows // 4, BS), cube),
                pl.BlockSpec((4, rows // 4, 2 * BS), cube),
                pl.BlockSpec((rows, BS), flat),
                pl.BlockSpec((rows, BS), flat),
                pl.BlockSpec((rows, BS), flat),
                pl.BlockSpec((rows, BS), flat),
                pl.BlockSpec((rows, BS), lambda n, me: (0, 0)),
                pl.BlockSpec((8, BS), flat),
                pl.BlockSpec((BS, BS), flat),
                pl.BlockSpec((BS, BS), lambda n, me: (0, blocks + n)),
                pl.BlockSpec((8, BS), flat),
                pl.BlockSpec((8, BS), flat),
            ],
            out_specs=[
                pl.BlockSpec((4, rows // 4, 2 * BS), cube),
                pl.BlockSpec((2, BS, BS), cube),
                pl.BlockSpec((8, BS), flat),
            ],
            scratch_shapes=[
                pltpu.VMEM((rows + 8, BS), f32),
                pltpu.VMEM((rows + 16, BS), jnp.int32),
                pltpu.VMEM((rows + 8, BS), f32),
                pltpu.VMEM((rows, 2 * BS), bf16),
                pltpu.VMEM((rows + 8, BS), f32),
                pltpu.VMEM((rows, BS), f32),
                pltpu.VMEM((2 * BS, BS), bf16),
            ],
        ),
        out_shape=[
            jax.ShapeDtypeStruct((4, rows // 4, 2 * channels), bf16),
            jax.ShapeDtypeStruct((2, BS, channels), f32),
            jax.ShapeDtypeStruct((8, channels), f32),
        ],
        compiler_params=vmem(24),
        name="mixing_backward",
    )(me, grad_gated, *(in_hbm(v) for v in (branch, states, conv, sig_r, sig_i)), ids, taps, gates, gates, rate, slope)


def folded(count):
    return list(range(0, 1)) + list(range(1, count, 2)) + list(range((count - 1) // 2 * 2, 0, -2))


class Links:
    def __init__(self, dp, mp):
        assert mp == 4 and dp % 2 == 0
        self.dp, self.mp = dp, mp
        self.line = dp // 2
        self.order = folded(self.line)
        self.place = {a: k for k, a in enumerate(self.order)}
        self.ring = [
            (2 * a + b, 2 * self.order[(self.place[a] + 1) % self.line] + b)
            for a in range(self.line)
            for b in range(2)
        ]

    def to_core(self, v):
        return lax.ppermute(v, "mp", [(i, i ^ 1) for i in range(self.mp)])

    def to_x(self, v):
        return lax.ppermute(v, "mp", [(i, i ^ 2) for i in range(self.mp)])

    def to_pair(self, v):
        return lax.ppermute(v, "dp", [(i, i ^ 1) for i in range(self.dp)])

    def along(self, v):
        return lax.ppermute(v, "dp", self.ring)

    def behind(self, me, steps):
        at = lax.shift_right_logical(me, 1)
        place = jnp.int32(0)
        for a in range(self.line):
            place = jnp.where(at == a, self.order[(self.place[a] - steps) % self.line], place)
        return place.astype(jnp.int32)


def in_hbm(v):
    return pltpu.with_memory_space_constraint(v, pltpu.HBM)


def hbm_out(shape, dtype):
    return pltpu.HBM(shape, dtype)


def vmem(mib):
    return pltpu.CompilerParams(vmem_limit_bytes=mib * 1024 * 1024)


UNIT = 384


def assemble(pieces, whole):
    @pl.when(pl.program_id(0) == 0)
    def _():
        rows = pieces[0].shape[0]
        for k, piece in enumerate(pieces):
            whole[k * rows:(k + 1) * rows, :] = piece[...]


def rows_call(kernel, pieces, more, more_specs, outs, out_specs, grid, name, mib, scratch=(), streamed=False):
    own, width = pieces[0].shape
    count = len(pieces)
    whole = pl.BlockSpec((count * own, width), lambda n: (0, 0))
    joined = count > 1

    def run(*refs):
        x, others = refs[0], refs[count:]
        if joined:
            x = refs[count + len(more)]
            assemble(refs[:count], x)
            others = refs[count:count + len(more)] + refs[count + len(more) + 1:]
        kernel(x, *others)

    if streamed:
        pieces, more = [in_hbm(v) for v in pieces], [in_hbm(v) for v in more]
        outs = [hbm_out(v.shape, v.dtype) for v in outs]
    return pl.pallas_call(
        run,
        grid=(grid,),
        in_specs=[pl.BlockSpec((own, width), lambda n: (0, 0))] * count + more_specs,
        out_specs=[whole] * joined + out_specs,
        out_shape=[jax.ShapeDtypeStruct((count * own, width), bf16)] * joined + outs,
        scratch_shapes=list(scratch),
        compiler_params=vmem(mib),
        name=name,
    )(*pieces, *more)


def against_kernel(x, w, send, keep):
    half = send.shape[0]
    result = lax.dot_general(x[...], w[...], (((1,), (1,)), ((), ())), preferred_element_type=f32).astype(bf16)
    send[...] = result[:half]
    keep[...] = result[half:]


def against_rows(x, w, name):
    rows, depth = x.shape
    width = w.shape[0]
    tile = 256
    half = pl.BlockSpec((rows // 2, tile), lambda n: (0, n))
    return rows_call(
        against_kernel, [x], [w], [pl.BlockSpec((tile, depth), lambda n: (n, 0))],
        [jax.ShapeDtypeStruct((rows // 2, width), bf16)] * 2, [half] * 2, width // tile,
        name, 20)


def project_kernel(x, w, out):
    out[...] = jnp.dot(x[...], w[...], preferred_element_type=f32)


def project_rows(pieces, w, tile, name, out=jax.ShapeDtypeStruct):
    own, width = pieces[0].shape
    columns = w.shape[1]
    return rows_call(
        project_kernel, pieces, [w], [pl.BlockSpec((width, tile), lambda n: (0, n))],
        [out((4 * own, columns), f32)], [pl.BlockSpec((4 * own, tile), lambda n: (0, n))],
        columns // tile, name, 24)


def ffn_forward_kernel(x, w, hidden, by_gate, by_up):
    both = jnp.dot(x[...], w[...], preferred_element_type=f32)
    up = both[:, UNIT:]
    value, slope = gelu_parts(both[:, :UNIT])
    hidden[...] = (value * up).astype(bf16)
    by_gate[...] = (up * slope).astype(bf16)
    by_up[...] = value.astype(bf16)


def ffn_forward(pieces, w):
    own, width = pieces[0].shape
    units = w.shape[1] // 2
    tile = pl.BlockSpec((4 * own, UNIT), lambda n: (0, n))
    return rows_call(
        ffn_forward_kernel, pieces, [w], [pl.BlockSpec((width, 2 * UNIT), lambda n: (0, n))],
        [jax.ShapeDtypeStruct((4 * own, units), bf16)] * 3, [tile] * 3,
        units // UNIT, "ffn_forward", 34, streamed=True)


def ffn_backward_kernel(tiles, x, w, by_gate, by_up, w_up, out, send, keep, whole):
    at = pl.program_id(0)

    @pl.when(at < tiles)
    def _():
        grad = jnp.dot(x[...], w[...], preferred_element_type=f32)
        out[:, :UNIT] = (grad * by_gate[...].astype(f32)).astype(bf16)
        out[:, UNIT:] = (grad * by_up[...].astype(f32)).astype(bf16)
        whole[at] = out[...]

    @pl.when(at >= tiles)
    def _():
        half = send.shape[0]
        result = sum(
            lax.dot_general(whole[k], w_up[:, 2 * k * UNIT:2 * (k + 1) * UNIT], (((1,), (1,)), ((), ())),
                            preferred_element_type=f32)
            for k in range(tiles))
        result = result.astype(bf16)
        send[...] = result[:half]
        keep[...] = result[half:]


def ffn_backward(x, w, by_gate, by_up, w_up):
    rows, width = x.shape
    units = w.shape[1]
    tiles = units // UNIT
    tile = 256
    first = lambda n: jnp.minimum(n, tiles - 1)
    then = lambda n: jnp.maximum(n - tiles, 0)
    half = pl.BlockSpec((rows // 2, tile), lambda n: (0, then(n)))
    return rows_call(
        functools.partial(ffn_backward_kernel, tiles), [x], [w, by_gate, by_up, w_up],
        [pl.BlockSpec((width, UNIT), lambda n: (0, first(n))), pl.BlockSpec((rows, UNIT), lambda n: (0, first(n))),
         pl.BlockSpec((rows, UNIT), lambda n: (0, first(n))),
         pl.BlockSpec((tile, 2 * units), lambda n: (then(n), 0))],
        [jax.ShapeDtypeStruct((rows, 2 * units), bf16)] + [jax.ShapeDtypeStruct((rows // 2, width), bf16)] * 2,
        [pl.BlockSpec((rows, 2 * UNIT), lambda n: (0, first(n))), half, half],
        tiles + width // tile, "ffn_backward", 46, [pltpu.VMEM((tiles, rows, 2 * UNIT), bf16)], streamed=True)


def pack_kernel(x, y, out, recur, inp, packed):
    rows, channels = x.shape
    columns = recur.shape[1]
    for n in range(channels // BS):
        block = slice(n * BS, (n + 1) * BS)
        packed[0:rows, 2 * n * BS:(2 * n + 1) * BS] = x[:, block]
        packed[0:rows, (2 * n + 1) * BS:(2 * n + 2) * BS] = y[:, block]
        packed[rows:rows + columns, block] = recur[n]
        packed[rows:rows + columns, channels + n * BS:channels + (n + 1) * BS] = inp[n]
    packed[0:rows, 2 * channels:3 * channels] = out[...]
    packed[rows:rows + columns, 2 * channels:3 * channels] = jnp.zeros((columns, channels), bf16)


def pack(x, y, out, recur, inp):
    rows, channels = x.shape
    return pl.pallas_call(
        pack_kernel,
        out_shape=jax.ShapeDtypeStruct((rows + recur.shape[1], 3 * channels), bf16),
        name="pack",
    )(x, y, out, recur, inp)


def weight_grad_kernel(line, shard, extra, groups, table, *refs):
    if extra:
        left_a, right_a, left_b, right_b, extra_a, extra_b, *sent, kept, total = refs
    else:
        left_a, right_a, left_b, right_b, *sent, kept, total = refs
    dims = (((0,), (0,)), ((), ()))
    total[...] = lax.dot_general(
        left_a[...], right_a[...], dims, preferred_element_type=f32
    ) + lax.dot_general(left_b[...], right_b[...], dims, preferred_element_type=f32)
    bit = table[line]
    size = line // groups
    for k in range(line):
        at = 2 * table[k]
        out = sent[k // size]
        mine = pl.ds(pl.multiple_of((at + bit) * shard, 16), shard)
        other = pl.ds(pl.multiple_of((at + 1 - bit) * shard, 16), shard)
        kept[k, 0:shard, :] = total[mine, :]
        out[k % size, 0:shard, :] = total[other, :].astype(bf16)
        if extra:
            kept[k, shard:shard + extra, :] = extra_a[0, at + bit] + extra_b[0, at + bit]
            out[k % size, shard:shard + extra, :] = (
                extra_a[0, at + 1 - bit] + extra_b[0, at + 1 - bit]).astype(bf16)


def weight_grad(table, left, right, tile, groups, extras=None):
    line = table.shape[0] - 1
    rows, width = left[0].shape
    columns = right[0].shape[1]
    shard = width // (2 * line)
    extra = extras[0].shape[2] if extras else 0
    lefts = pl.BlockSpec((rows, width), lambda n, t: (0, 0))
    rights = pl.BlockSpec((rows, tile), lambda n, t: (0, n))
    more = [pl.BlockSpec((1, 2 * line, extra, tile), lambda n, t: (n, 0, 0, 0))] * 2 if extra else []
    parts = lambda count: pl.BlockSpec((count, shard + extra, tile), lambda n, t: (0, 0, n))
    size = line // groups
    *sent, kept = pl.pallas_call(
        functools.partial(weight_grad_kernel, line, shard, extra, groups),
        grid_spec=pltpu.PrefetchScalarGridSpec(
            num_scalar_prefetch=1,
            grid=(columns // tile,),
            in_specs=[lefts, rights, lefts, rights] + more,
            out_specs=[parts(size)] * groups + [parts(line)],
            scratch_shapes=[pltpu.VMEM((width, tile), f32)],
        ),
        out_shape=[jax.ShapeDtypeStruct((size, shard + extra, columns), bf16)] * groups
        + [jax.ShapeDtypeStruct((line, shard + extra, columns), f32)],
        compiler_params=vmem(52 if tile > 1024 else 44),
        name="weight_grad",
    )(table, in_hbm(left[0]), in_hbm(right[0]), in_hbm(left[1]), in_hbm(right[1]), *(extras or ()))
    return sent, kept


def last_sum(write, held, at, outs, name):
    kept, sent, moving = held["kept"], held["sent"][at // held["size"]], held["moving"]
    shape = (1,) + kept.shape[1:]
    inside = at % held["size"]

    def kernel(kept, sent, moving, *outs):
        write(kept[0] + sent[0].astype(f32) + moving[...].astype(f32), *outs)

    return pl.pallas_call(
        kernel,
        grid=(1,),
        in_specs=[pl.BlockSpec(shape, lambda n: (at, 0, 0)), pl.BlockSpec(shape, lambda n: (inside, 0, 0)),
                  pl.BlockSpec(shape[1:], lambda n: (0, 0))],
        out_specs=[pl.BlockSpec(out, lambda n, rank=len(out): (0,) * rank) for out in outs],
        out_shape=[jax.ShapeDtypeStruct(out, f32) for out in outs],
        compiler_params=vmem(16),
        name=name,
    )(kept, sent, moving)


def write_plain(total, out):
    out[...] = total


def write_gate_up(total, gate, up):
    for k in range(gate.shape[1] // UNIT):
        gate[:, k * UNIT:(k + 1) * UNIT] = total[:, 2 * k * UNIT:(2 * k + 1) * UNIT]
        up[:, k * UNIT:(k + 1) * UNIT] = total[:, (2 * k + 1) * UNIT:(2 * k + 2) * UNIT]


def write_first(total, x, y, recur, inp):
    rows, channels = x.shape
    for n in range(channels // BS):
        block = slice(n * BS, (n + 1) * BS)
        x[:, block] = total[:rows, 2 * n * BS:(2 * n + 1) * BS]
        y[:, block] = total[:rows, (2 * n + 1) * BS:(2 * n + 2) * BS]
        recur[n] = total[rows:, block]
        inp[n] = total[rows:, channels + n * BS:channels + (n + 1) * BS]


class Bag(dict):
    def fence(self):
        values, tree = jax.tree.flatten(dict(self))
        values = lax.optimization_barrier(values)
        self.update(jax.tree.unflatten(tree, values))

    def take(self, *names):
        out = [self.pop(name) for name in names]
        return out if len(out) > 1 else out[0]


class Gather:
    def __init__(self, links, me, bag, name, shard, parts=None):
        self.links, self.me, self.bag, self.name = links, me, bag, name
        self.along_steps, self.pair_steps, self.placed, self.other_placed = 0, 0, 0, 0
        self.parts = parts or [(slice(0, shard.shape[0]), slice(0, shard.shape[1]))]
        bag[name] = {"z": [shard], "y": [], "whole": None}

    def along(self, steps=1):
        z = self.bag[self.name]["z"]
        for _ in range(steps):
            if self.along_steps < self.links.line - 1:
                z.append(self.links.along(z[self.along_steps]))
                self.along_steps += 1

    def pair(self, steps=1):
        held = self.bag[self.name]
        for _ in range(steps):
            if self.pair_steps <= self.along_steps and self.pair_steps < self.links.line:
                held["y"].append(self.links.to_pair(held["z"][self.pair_steps]))
                self.pair_steps += 1

    def put(self, pieces, at, bit):
        held = self.bag[self.name]
        base = 2 * self.links.behind(self.me, at)
        wholes = []
        for k, (rows, columns) in enumerate(self.parts):
            piece = pieces[at][rows, columns][None]
            whole = jnp.zeros((self.links.dp,) + piece.shape[1:], bf16) if held["whole"] is None else held["whole"][k]
            wholes.append(lax.dynamic_update_slice(whole, piece, (base + bit, 0, 0)))
        held["whole"] = wholes

    def place(self, z=0, y=0):
        held = self.bag[self.name]
        bit = lax.bitwise_and(self.me, 1)
        for _ in range(z):
            if self.placed <= self.along_steps:
                self.put(held["z"], self.placed, bit)
                self.placed += 1
        for _ in range(y):
            if self.other_placed < self.pair_steps:
                self.put(held["y"], self.other_placed, 1 - bit)
                self.other_placed += 1
        for k in range(min(self.placed, self.pair_steps, self.along_steps)):
            held["z"][k] = None
        for k in range(self.other_placed):
            held["y"][k] = None

    def finish(self):
        line = self.links.line
        while self.pair_steps < line:
            self.along()
            self.pair()
        self.place(line, line)
        return self.bag.pop(self.name)["whole"]


class Scatter:
    def __init__(self, links, bag, name, sent, kept):
        self.links, self.bag, self.name = links, bag, name
        self.pair_steps, self.along_steps = 0, 0
        self.size = links.line // len(sent)
        bag[name] = {"sent": list(sent), "kept": kept, "moving": None}

    def pair(self):
        sent = self.bag[self.name]["sent"]
        if self.pair_steps < len(sent):
            sent[self.pair_steps] = self.links.to_pair(sent[self.pair_steps])
            self.pair_steps += 1

    def along(self):
        held = self.bag[self.name]
        at = self.along_steps
        if at < self.links.line - 1 and at // self.size < self.pair_steps:
            held["moving"] = self.links.along(self.sum_here().astype(bf16))
            self.along_steps += 1

    def sum_here(self):
        held = self.bag[self.name]
        at = self.along_steps
        total = held["kept"][at] + held["sent"][at // self.size][at % self.size].astype(f32)
        if held["moving"] is not None:
            total = total + held["moving"].astype(f32)
        return total

    def finish(self, write, *outs):
        while self.pair_steps < len(self.bag[self.name]["sent"]):
            self.pair()
        while self.along_steps < self.links.line - 1:
            self.along()
        held = self.bag.pop(self.name)
        return last_sum(write, {**held, "size": self.size}, self.along_steps, outs, self.name)


class AllSum:
    def __init__(self, bag, name, value, axes):
        self.bag, self.name = bag, name
        self.steps = [(axis, count, 1 << k) for axis, count in axes for k in range(count.bit_length() - 1)]
        assert all(count & (count - 1) == 0 for _, count in axes)
        bag[name] = value

    def step(self):
        if self.steps:
            axis, count, bit = self.steps.pop(0)
            value = self.bag[self.name]
            self.bag[self.name] = value + lax.ppermute(value, axis, [(i, i ^ bit) for i in range(count)])

    def finish(self):
        while self.steps:
            self.step()
        return self.bag.pop(self.name)


def body(links, block_in, doc_ids, mix_gain, proj_x, proj_y, conv_taps, recur_gate, input_gate, decay_param,
         proj_out, ffn_gain, ffn_gate, ffn_up, ffn_down, out_grad):
    micro_count, own_rows, width = block_in.shape
    group_rows = doc_ids.shape[1]
    assert group_rows == LEN and own_rows * 4 == group_rows and micro_count == 2
    d_rows, channels = proj_x.shape
    blocks = channels // BS
    hidden_units = ffn_gate.shape[1]
    assert hidden_units % UNIT == 0
    gate_columns = recur_gate.shape[2]
    dp_me = lax.axis_index("dp")
    me = lax.axis_index("mp").astype(jnp.int32).reshape(1)
    gain_one = mix_gain.astype(f32)
    gain_two = ffn_gain.astype(f32)
    to_core, to_x = links.to_core, links.to_x
    bag = Bag()

    def exchange(name):
        send, keep = bag.pop(name + "_send"), bag.pop(name + "_keep")
        own_rows_of = lambda v, k: v[k * own_rows:(k + 1) * own_rows].astype(f32)
        sent = to_core(send)
        bag[name + "_own"] = (keep, sent)
        bag[name + "_x"] = (own_rows_of(keep, 1) + own_rows_of(sent, 1)).astype(bf16)

    def summed(name):
        keep, sent = bag.pop(name + "_own")
        return (keep[:own_rows].astype(f32) + sent[:own_rows].astype(f32)) + bag.pop(name + "_x").astype(f32)

    def across(name):
        bag[name + "_x"] = to_x(bag[name + "_x"])

    def rows_of(name):
        own, core, x, diagonal = bag.take(name, name + "_core", name + "_x", name + "_diagonal")
        return core, diagonal, own, x

    packed = pack(proj_x, proj_y, proj_out.T, jnp.swapaxes(recur_gate, 1, 2), jnp.swapaxes(input_gate, 1, 2))
    inner_rows, outer_rows = slice(0, d_rows), slice(d_rows, d_rows + gate_columns)
    wide, narrow = slice(0, 2 * channels), slice(2 * channels, 3 * channels)
    first = Gather(links, dp_me, bag, "first", packed, [(inner_rows, wide), (inner_rows, narrow), (outer_rows, wide)])
    bag.fence()

    bag["cot0"], bag["cot1"] = out_grad[0], out_grad[1]
    first.along()
    first.pair()
    for micro in range(2):
        xin = block_in[micro].astype(f32)
        inverse = lax.rsqrt(jnp.mean(xin * xin, axis=-1, keepdims=True) + norm_eps)
        bag[f"inverse_one{micro}"] = inverse
        bag[f"normed{micro}"] = (xin * inverse * gain_one).astype(bf16)
    bag.fence()

    first.along()
    first.pair()
    bag["normed0_x"] = to_x(bag["normed0"])
    bag["normed0_core"] = to_core(bag["normed0"])
    first.place(2, 1)
    decay_values = decay_param.astype(f32)
    bag["rate"] = jnp.broadcast_to((-decay_scale * jax.nn.softplus(-decay_values))[None], (8, channels))
    bag["slope"] = jnp.broadcast_to((decay_scale * jax.nn.sigmoid(-decay_values))[None], (8, channels))
    bag["taps"] = jnp.concatenate([conv_taps.astype(f32), jnp.zeros((8 - KW, channels), f32)])
    bag["table"] = jnp.stack(
        [links.behind(dp_me, step + 1) for step in range(links.line)] + [lax.bitwise_and(dp_me, 1).astype(jnp.int32)])
    bag.fence()

    first.along()
    first.pair()
    bag["normed1_x"] = to_x(bag["normed1"])
    bag["normed0_diagonal"] = to_core(bag["normed0_x"])
    first.place(1, 1)
    gate_up = jnp.stack([ffn_gate.reshape(d_rows, -1, UNIT), ffn_up.reshape(d_rows, -1, UNIT)], axis=2)
    second = Gather(links, dp_me, bag, "second", gate_up.reshape(d_rows, 2 * hidden_units))
    third = Gather(links, dp_me, bag, "third", ffn_down.T)
    for micro in range(2):
        bag[f"ids{micro}"] = jnp.broadcast_to(doc_ids[micro][:, None], (group_rows, BS))
    bag.fence()

    first.pair()
    third.along(2)
    third.pair()
    bag["cot0_x"] = to_x(bag["cot0"])
    first.place(1, 1)
    bag.fence()

    def mix(micro):
        bag[f"normed_all{micro}"], branch = project_rows(rows_of(f"normed{micro}"), bag["w_branch"], 256, "branch", hbm_out)
        branch = branch.reshape(4, own_rows, 2 * channels)
        gated, *rest = mixing_forward(me, branch, bag[f"ids{micro}"], bag["taps"], bag["gates"], bag["rate"])
        bag[f"mixed{micro}"] = [branch] + rest
        bag[f"gated{micro}"] = gated.reshape(group_rows, channels)

    def against_of(name, left, weight):
        bag[name + "_send"], bag[name + "_keep"] = against_rows(bag[left], bag[weight], weight + "_turned")

    def middle_of(micro):
        middle = block_in[micro].astype(f32) + summed(f"first{micro}")
        inverse = lax.rsqrt(jnp.mean(middle * middle, axis=-1, keepdims=True) + norm_eps)
        bag[f"middle{micro}"], bag[f"inverse_two{micro}"] = middle, inverse
        bag[f"two{micro}"] = (middle * inverse * gain_two).astype(bf16)

    second.along()
    second.pair()
    third.pair()
    bag["cot1_x"] = to_x(bag["cot1"])
    w_branch, w_out, gates = first.finish()
    bag["w_branch"] = w_branch.reshape(width, 2 * channels)
    bag["gates"] = gates.reshape(BS, 2 * channels)
    bag["w_out"] = w_out.reshape(width, channels)
    mix(0)
    against_of("first0", "gated0", "w_out")
    bag.fence()

    bag["normed1_core"] = to_core(bag["normed1"])
    bag["normed1_diagonal"] = to_core(bag["normed1_x"])
    exchange("first0")
    second.place(1)
    bag.fence()

    second.along()
    second.pair()
    across("first0")
    second.place(1)
    mix(1)
    bag.fence()

    bag["cot0_core"] = to_core(bag["cot0"])
    bag["cot0_diagonal"] = to_core(bag["cot0_x"])
    middle_of(0)
    against_of("first1", "gated1", "w_out")
    bag.fence()

    second.along()
    second.pair()
    bag["two0_x"] = to_x(bag["two0"])
    bag["two0_core"] = to_core(bag["two0"])
    exchange("first1")
    bag["cot_all0"] = jnp.concatenate(rows_of("cot0"))
    second.place(2, 2)
    third.place(3, 2)
    bag.fence()

    def forward(micro):
        bag[f"two_all{micro}"], bag[f"hidden{micro}"], *bag[f"by{micro}"] = ffn_forward(
            rows_of(f"two{micro}"), bag["w_up"])

    third.along()
    second.pair()
    across("first1")
    bag["two0_diagonal"] = to_core(bag["two0_x"])
    bag["cot1_core"] = to_core(bag["cot1"])
    bag["cot1_diagonal"] = to_core(bag["cot1_x"])
    bag["cot_all1"] = jnp.concatenate(rows_of("cot1"))
    second.place(1, 1)
    bag.fence()

    middle_of(1)
    bag.fence()

    third.pair(2)
    bag["two1_x"] = to_x(bag["two1"])
    bag["w_up"] = second.finish()[0].reshape(width, 2 * hidden_units)
    third.place(2)
    forward(0)
    bag.fence()

    def back(micro):
        name = f"second{micro}"
        bag[f"grad_pre{micro}"], bag[name + "_send"], bag[name + "_keep"] = ffn_backward(
            bag[f"cot_all{micro}"], bag["w_down"], *bag.pop(f"by{micro}"), bag["w_up"])

    def grad_middle_of(micro):
        grad = summed(f"second{micro}")
        inverse, middle = bag[f"inverse_two{micro}"], bag[f"middle{micro}"]
        unit = middle * inverse
        total = out_grad[micro].astype(f32) + norm_back(grad, unit, inverse, gain_two)
        bag[f"grad_middle{micro}"] = total
        bag[f"gain_two{micro}"] = jnp.sum(grad * unit, axis=0)
        bag[f"low{micro}"] = total.astype(bf16)

    bag["two1_core"] = to_core(bag["two1"])
    bag["two1_diagonal"] = to_core(bag["two1_x"])
    bag["w_down"] = third.finish()[0].reshape(width, hidden_units)
    back(0)
    bag.fence()

    exchange("second0")
    forward(1)
    bag.fence()

    across("second0")
    down_grad = Scatter(links, bag, "down_grad", *weight_grad(
        bag["table"], [bag["cot_all0"], bag["cot_all1"]], [bag["hidden0"], bag["hidden1"]], hidden_units, 2))
    bag.fence()

    down_grad.pair()
    back(1)
    bag.fence()

    exchange("second1")
    grad_middle_of(0)
    bag.fence()

    across("second1")
    down_grad.pair()
    bag["low0_core"] = to_core(bag["low0"])
    up_grad = Scatter(links, bag, "up_grad", *weight_grad(
        bag["table"], bag.take("two_all0", "two_all1"), bag.take("grad_pre0", "grad_pre1"), 2 * UNIT, 4))
    bag.fence()

    def output_of(micro):
        bag[f"output{micro}"] = (bag[f"middle{micro}"] + summed(f"down{micro}")).astype(bf16)

    bag["low0_x"] = to_x(bag["low0"])
    up_grad.pair()
    down_grad.along()
    grad_middle_of(1)
    against_of("down0", "hidden0", "w_down")
    bag.fence()

    def into_mix(micro):
        bag[f"low_all{micro}"], bag[f"grad_gated{micro}"] = project_rows(
            rows_of(f"low{micro}"), bag["w_out"], 256, "grad_gated")

    def mix_back(micro):
        grad, bag[f"gates_grad{micro}"], bag[f"small{micro}"] = mixing_backward(
            me, bag.pop(f"grad_gated{micro}").reshape(4, own_rows, channels), *bag.pop(f"mixed{micro}"),
            bag[f"ids{micro}"], bag["taps"], bag["gates"], bag["rate"], bag["slope"])
        bag[f"grad_branch{micro}"] = grad.reshape(group_rows, 2 * channels)
        against_of(f"third{micro}", f"grad_branch{micro}", "w_branch")

    bag["low1_x"] = to_x(bag["low1"])
    bag["low0_diagonal"] = to_core(bag["low0_x"])
    up_grad.pair()
    up_grad.along()
    exchange("down0")
    into_mix(0)
    mix_back(0)
    bag.fence()

    across("down0")
    bag["low1_core"] = to_core(bag["low1"])
    bag["low1_diagonal"] = to_core(bag["low1_x"])
    exchange("third0")
    up_grad.pair()
    up_grad.along()
    into_mix(1)
    out_grad_w = Scatter(links, bag, "out_grad", *weight_grad(
        bag["table"], bag.take("low_all0", "low_all1"), bag.take("gated0", "gated1"), 512, 1))
    bag.fence()

    across("third0")
    up_grad.pair()
    up_grad.along()
    down_grad.along()
    mix_back(1)
    bag.fence()

    exchange("third1")
    bag.fence()

    def leave(micro):
        grad = summed(f"third{micro}")
        inverse = bag[f"inverse_one{micro}"]
        unit = block_in[micro].astype(f32) * inverse
        bag[f"input_grad{micro}"] = bag[f"grad_middle{micro}"] + norm_back(grad, unit, inverse, gain_one)
        bag[f"gain_one{micro}"] = jnp.sum(grad * unit, axis=0)

    across("third1")
    out_grad_w.pair()
    down_grad.along()
    gates_grads = [bag.pop(f"gates_grad{micro}").reshape(2, links.dp, gate_columns, channels) for micro in range(2)]
    first_grad = Scatter(links, bag, "first_grad", *weight_grad(
        bag["table"], bag.take("normed_all0", "normed_all1"), bag.take("grad_branch0", "grad_branch1"), channels, 4,
        gates_grads))
    bag.fence()

    first_grad.pair()
    out_grad_w.along()
    leave(1)
    leave(0)
    against_of("down1", "hidden1", "w_down")
    gains = jnp.stack([bag.pop("gain_one0") + bag.pop("gain_one1"), bag.pop("gain_two0") + bag.pop("gain_two1")])
    bag["sums"] = gains.reshape(-1, 128)
    gain_rows = bag["sums"].shape[0]
    bag.fence()

    first_grad.pair()
    first_grad.along()
    sums = AllSum(bag, "gains", bag.pop("sums"), [("mp", links.mp)])
    small = (bag.pop("small0") + bag.pop("small1")).reshape(-1, 128)
    sums = AllSum(bag, "sums", jnp.concatenate([sums.finish(), small]), [("dp", links.dp)])
    exchange("down1")
    output_of(0)
    bag["up_total"] = up_grad.finish(write_gate_up, (d_rows, hidden_units), (d_rows, hidden_units))
    bag.fence()

    first_grad.pair()
    first_grad.along()
    out_grad_w.along()
    sums.step()
    bag["down1_xa"] = to_x(bag["down1_x"][:own_rows // 2])
    bag["down_total"] = down_grad.finish(write_plain, (d_rows, hidden_units))
    bag.fence()

    first_grad.pair()
    first_grad.along()
    out_grad_w.along()
    sums.step()
    bag["down1_xb"] = to_x(bag["down1_x"][own_rows // 2:])
    bag["input_grads"] = jnp.stack([bag.pop("input_grad0"), bag.pop("input_grad1")])
    bag.fence()

    bag["down1_x"] = jnp.concatenate(bag.take("down1_xa", "down1_xb"))
    output_of(1)
    bag["outputs"] = jnp.stack(bag.take("output0", "output1"))
    bag["out_total"] = out_grad_w.finish(write_plain, (d_rows, channels))
    x_grad, y_grad, recur, inp = first_grad.finish(
        write_first, (d_rows, channels), (d_rows, channels), (blocks, gate_columns, BS), (blocks, gate_columns, BS))
    sums = sums.finish()
    gains = sums[:gain_rows].reshape(2, width)
    small = sums[gain_rows:].reshape(8, channels)
    return (
        bag["outputs"],
        bag["input_grads"],
        gains[0],
        x_grad,
        y_grad,
        small[0:KW],
        jnp.swapaxes(recur, 1, 2),
        jnp.swapaxes(inp, 1, 2),
        small[KW],
        bag["out_total"][0].T,
        gains[1],
        *bag["up_total"],
        bag["down_total"][0].T,
    )


def solution(mesh):
    links = Links(mesh.shape["dp"], mesh.shape["mp"])
    tokens = P(None, ("dp", "mp"), None)
    rows, columns, gate = P("dp", "mp"), P("mp", "dp"), P("mp", None, "dp")
    return jax.shard_map(
        functools.partial(body, links),
        mesh=mesh,
        in_specs=(tokens, P(None, "dp"), P(), rows, rows, P(None, "mp"), gate, gate, P("mp"), columns, P(), rows,
                  rows, columns, tokens),
        out_specs=(tokens, tokens, P(), rows, rows, P(None, "mp"), gate, gate, P("mp"), columns, P(), rows, rows,
                   columns),
        check_vma=False,
    )
```

```python
import functools

import jax
import jax.numpy as jnp
import numpy as np
from jax import lax
from jax.experimental import pallas as pl
from jax.experimental.pallas import tpu as pltpu
from jax.sharding import PartitionSpec as P

LEN = 1024
BS = 128
KW = 4

norm_eps = 1e-06
root_floor = 0.01
decay_scale = 8.0
gelu_a = 0.7978845608028654
gelu_b = 0.044715

f32 = jnp.float32
bf16 = jnp.bfloat16


BLOCK_AT = (2, 0, 3, 1)


def project(left, right):
    return jnp.dot(left, right, preferred_element_type=f32)


def inner(left, right):
    return lax.dot_general(left, right, (((0,), (0,)), ((), ())), preferred_element_type=f32)


def against(left, right):
    return lax.dot_general(left, right, (((1,), (1,)), ((), ())), preferred_element_type=f32)


def norm_back(grad_normed, unit_rows, inverse, gain):
    scaled = grad_normed * gain
    return inverse * (scaled - unit_rows * jnp.mean(scaled * unit_rows, axis=-1, keepdims=True))


def gelu_parts(v):
    squared = v * v
    inside = gelu_a * v * (1.0 + gelu_b * squared)
    t = jnp.tanh(inside)
    half = 0.5 * (1.0 + t)
    value = v * half
    slope = half + 0.5 * v * (1.0 - t * t) * (gelu_a * (1.0 + 3.0 * gelu_b * squared))
    return value, slope


def gelu_value(v):
    return 0.5 * v * (1.0 + jnp.tanh(gelu_a * v * (1.0 + gelu_b * v * v)))


def place_of(me, block):
    differ = lax.bitwise_xor(me, block)
    low = lax.bitwise_and(differ, 1)
    high = lax.shift_right_logical(differ, 1)
    return 2 * (1 - low) + high


CHUNK = 64
STEP = 32


def tile_scan(a, b, row):
    for d in (1, 2, 4):
        use = row >= d
        b = b + a * jnp.where(use, pltpu.roll(b, d, 0), 0.0)
        a = a * jnp.where(use, pltpu.roll(a, d, 0), 1.0)
    return a, b


def tile_scan_back(a, b, row):
    for d in (1, 2, 4):
        use = row < 8 - d
        b = b + a * jnp.where(use, pltpu.roll(b, 8 - d, 0), 0.0)
        a = a * jnp.where(use, pltpu.roll(a, 8 - d, 0), 1.0)
    return a, b


def spread(row):
    return jnp.broadcast_to(row, (8, BS))


def mixing_forward_kernel(me_ref, branch, ids, taps, gate_r, gate_i, rate, gated, states, conv, sig_r, sig_i,
                          xpad, idpad, logits, gates):
    gates[0:BS, :] = gate_r[...]
    gates[BS:2 * BS, :] = gate_i[...]
    rows = LEN
    quarter = rows // 4
    me = me_ref[0]
    xpad[0:8, :] = jnp.zeros((8, BS), f32)
    idpad[0:8, :] = jnp.full((8, BS), -1, jnp.int32)
    idpad[8:8 + rows, :] = ids[...]
    for block in range(4):
        at = place_of(me, block)
        xpad[8 + block * quarter: 8 + (block + 1) * quarter, :] = branch[at, :, 0:BS]
    rate_row = rate[0:1, :]

    def convolve(step, _):
        base = pl.multiple_of(step * CHUNK, CHUNK)
        own_ids = idpad[pl.ds(base + 8, CHUNK), :]
        total = taps[0:1, :] * xpad[pl.ds(base + 8, CHUNK), :]
        for k in range(1, KW):
            same = idpad[pl.ds(base + 8 - k, CHUNK), :] == own_ids
            total = total + taps[k:k + 1, :] * jnp.where(same, xpad[pl.ds(base + 8 - k, CHUNK), :], 0.0)
        conv[pl.ds(base, CHUNK), :] = total.astype(bf16)
        return 0

    lax.fori_loop(0, rows // CHUNK, convolve, 0, unroll=2)
    logits[...] = lax.dot_general(conv[...], gates[...], (((1,), (1,)), ((), ())), preferred_element_type=f32)
    row = lax.broadcasted_iota(jnp.int32, (8, BS), 0)

    def advance(step, carry):
        base = pl.multiple_of(step * STEP, STEP)
        here = pl.ds(base, STEP)
        block = lax.div(step, quarter // STEP)
        at = place_of(me, block)
        there = pl.ds(pl.multiple_of(base - block * quarter, STEP), STEP)
        sr = jax.nn.sigmoid(logits[here, 0:BS])
        si = jax.nn.sigmoid(logits[here, BS:2 * BS])
        sig_r[here, :] = sr
        sig_i[here, :] = si
        same = idpad[pl.ds(base + 7, STEP), :] == idpad[pl.ds(base + 8, STEP), :]
        a = jnp.where(same, jnp.exp(rate_row * sr), 0.0)
        margin = jnp.maximum(1.0 - a * a, root_floor)
        b = conv[here, :].astype(f32) * si * (margin * lax.rsqrt(margin))
        tiles = []
        for k in range(STEP // 8):
            part = slice(8 * k, 8 * k + 8)
            product, local = tile_scan(a[part], b[part], row)
            tiles.append(local + product * carry)
            carry = spread(local[7:8]) + spread(product[7:8]) * carry
        state = jnp.concatenate(tiles, axis=0)
        states[here, :] = state
        gated[at, there, :] = (state * gelu_value(branch[at, there, BS:2 * BS])).astype(bf16)
        return carry

    lax.fori_loop(0, rows // STEP, advance, jnp.zeros((8, BS), f32), unroll=2)


def mixing_backward_kernel(me_ref, grad_gated, branch, states, conv, sig_r, sig_i, ids, taps, gate_r, gate_i, rate,
                           slope, grad_branch, grad_gates, small,
                           xpad, idpad, spad, low, gcpad, through, gates):
    gates[0:BS, :] = gate_r[...]
    gates[BS:2 * BS, :] = gate_i[...]
    rows = LEN
    quarter = rows // 4
    me = me_ref[0]
    zero8 = jnp.zeros((8, BS), f32)
    xpad[0:8, :] = zero8
    spad[0:8, :] = zero8
    spad[8:8 + rows, :] = states[...]
    idpad[0:8, :] = jnp.full((8, BS), -1, jnp.int32)
    idpad[8:8 + rows, :] = ids[...]
    idpad[8 + rows:16 + rows, :] = jnp.full((8, BS), -1, jnp.int32)
    gcpad[rows:rows + 8, :] = zero8
    rate_row = rate[0:1, :]
    slope_row = slope[0:1, :]
    for block in range(4):
        at = place_of(me, block)
        xpad[8 + block * quarter: 8 + (block + 1) * quarter, :] = branch[at, :, 0:BS]
    row = lax.broadcasted_iota(jnp.int32, (8, BS), 0)
    fold = lambda v: jnp.sum(v.reshape(v.shape[0] // 8, 8, BS), axis=0)
    steps = rows // STEP

    def retreat(count, held):
        carry, decay_sum = held
        step = steps - 1 - count
        base = pl.multiple_of(step * STEP, STEP)
        here = pl.ds(base, STEP)
        block = lax.div(step, quarter // STEP)
        at = place_of(me, block)
        there = pl.ds(pl.multiple_of(base - block * quarter, STEP), STEP)
        value, gradient = gelu_parts(branch[at, there, BS:2 * BS])
        incoming = grad_gated[at, there, :]
        grad_states = incoming * value
        grad_branch[at, there, BS:2 * BS] = (gradient * states[here, :] * incoming).astype(bf16)
        same = idpad[pl.ds(base + 7, STEP), :] == idpad[pl.ds(base + 8, STEP), :]
        sr = sig_r[here, :]
        si = sig_i[here, :]
        a = jnp.where(same, jnp.exp(rate_row * sr), 0.0)
        pushed = a * grad_states
        us, gs = [], []
        for k in reversed(range(STEP // 8)):
            part = slice(8 * k, 8 * k + 8)
            product, local = tile_scan_back(a[part], pushed[part], row)
            u = local + product * carry
            us.insert(0, u)
            gs.insert(0, grad_states[part] + jnp.where(row == 7, carry, pltpu.roll(u, 7, 0)))
            carry = spread(local[0:1]) + spread(product[0:1]) * carry
        u = jnp.concatenate(us, axis=0)
        g = jnp.concatenate(gs, axis=0)
        square = a * a
        inside = 1.0 - square
        margin = jnp.maximum(inside, root_floor)
        inverse = lax.rsqrt(margin)
        multiplier = margin * inverse
        gsi = g * si
        gcsi = gsi * conv[here, :].astype(f32)
        grad_log = u * spad[pl.ds(base + 7, STEP), :] - jnp.where(inside > root_floor, gcsi * square * inverse, 0.0)
        gcpad[here, :] = gsi * multiplier
        weighted = grad_log * sr
        low[here, 0:BS] = (weighted * (1.0 - sr) * rate_row).astype(bf16)
        low[here, BS:2 * BS] = (gcsi * multiplier * (1.0 - si)).astype(bf16)
        return carry, decay_sum + fold(weighted)

    _, decay_sum = lax.fori_loop(0, steps, retreat, (zero8, zero8), unroll=2)

    both_gates = lax.dot_general(low[...], conv[...], (((0,), (0,)), ((), ())), preferred_element_type=f32)
    grad_gates[0] = both_gates[0:BS]
    grad_gates[1] = both_gates[BS:2 * BS]
    through[...] = lax.dot_general(low[...], gates[...], (((1,), (0,)), ((), ())), preferred_element_type=f32)

    def add_gates(step, _):
        here = pl.ds(pl.multiple_of(step * CHUNK, CHUNK), CHUNK)
        gcpad[here, :] = gcpad[here, :] + through[here, :]
        return 0

    lax.fori_loop(0, rows // CHUNK, add_gates, 0, unroll=4)

    def finish(step, sums):
        base = pl.multiple_of(step * CHUNK, CHUNK)
        block = lax.div(step, quarter // CHUNK)
        at = place_of(me, block)
        there = pl.ds(pl.multiple_of(base - block * quarter, CHUNK), CHUNK)
        gc = gcpad[pl.ds(base, CHUNK), :]
        own_ids = idpad[pl.ds(base + 8, CHUNK), :]
        new = [sums[0] + fold(gc * xpad[pl.ds(base + 8, CHUNK), :])]
        grad_x = taps[0:1, :] * gc
        for k in range(1, KW):
            same = idpad[pl.ds(base + 8 - k, CHUNK), :] == own_ids
            new.append(sums[k] + fold(jnp.where(same, gc * xpad[pl.ds(base + 8 - k, CHUNK), :], 0.0)))
            after = idpad[pl.ds(base + 8 + k, CHUNK), :] == own_ids
            grad_x = grad_x + taps[k:k + 1, :] * jnp.where(after, gcpad[pl.ds(base + k, CHUNK), :], 0.0)
        grad_branch[at, there, 0:BS] = grad_x.astype(bf16)
        return tuple(new)

    sums = lax.fori_loop(0, rows // CHUNK, finish, (zero8,) * KW, unroll=2)
    small[...] = jnp.zeros((8, BS), f32)
    for k in range(KW):
        small[k:k + 1, :] = jnp.sum(sums[k], axis=0, keepdims=True)
    small[KW:KW + 1, :] = jnp.sum(decay_sum, axis=0, keepdims=True) * slope_row


def mixing_forward(me, branch, ids, taps, gates, rate):
    rows = LEN
    blocks = branch.shape[2] // (2 * BS)
    channels = blocks * BS
    flat = lambda n, me: (0, n)
    return pl.pallas_call(
        mixing_forward_kernel,
        grid_spec=pltpu.PrefetchScalarGridSpec(
            num_scalar_prefetch=1,
            grid=(blocks,),
            in_specs=[
                pl.BlockSpec((4, rows // 4, 2 * BS), lambda n, me: (0, 0, n)),
                pl.BlockSpec((rows, BS), lambda n, me: (0, 0)),
                pl.BlockSpec((8, BS), flat),
                pl.BlockSpec((BS, BS), flat),
                pl.BlockSpec((BS, BS), lambda n, me: (0, blocks + n)),
                pl.BlockSpec((8, BS), flat),
            ],
            out_specs=[
                pl.BlockSpec((4, rows // 4, BS), lambda n, me: (0, 0, n)),
                pl.BlockSpec((rows, BS), flat),
                pl.BlockSpec((rows, BS), flat),
                pl.BlockSpec((rows, BS), flat),
                pl.BlockSpec((rows, BS), flat),
            ],
            scratch_shapes=[
                pltpu.VMEM((rows + 8, BS), f32),
                pltpu.VMEM((rows + 8, BS), jnp.int32),
                pltpu.VMEM((rows, 2 * BS), f32),
                pltpu.VMEM((2 * BS, BS), bf16),
            ],
        ),
        out_shape=[
            jax.ShapeDtypeStruct((4, rows // 4, channels), bf16),
            hbm_out((rows, channels), f32),
            hbm_out((rows, channels), bf16),
            hbm_out((rows, channels), f32),
            hbm_out((rows, channels), f32),
        ],
        compiler_params=vmem(16),
        name="mixing_forward",
    )(me, in_hbm(branch), ids, taps, gates, gates, rate)


def mixing_backward(me, grad_gated, branch, states, conv, sig_r, sig_i, ids, taps, gates, rate, slope):
    rows = LEN
    blocks = branch.shape[2] // (2 * BS)
    channels = blocks * BS
    flat = lambda n, me: (0, n)
    cube = lambda n, me: (0, 0, n)
    return pl.pallas_call(
        mixing_backward_kernel,
        grid_spec=pltpu.PrefetchScalarGridSpec(
            num_scalar_prefetch=1,
            grid=(blocks,),
            in_specs=[
                pl.BlockSpec((4, rows // 4, BS), cube),
                pl.BlockSpec((4, rows // 4, 2 * BS), cube),
                pl.BlockSpec((rows, BS), flat),
                pl.BlockSpec((rows, BS), flat),
                pl.BlockSpec((rows, BS), flat),
                pl.BlockSpec((rows, BS), flat),
                pl.BlockSpec((rows, BS), lambda n, me: (0, 0)),
                pl.BlockSpec((8, BS), flat),
                pl.BlockSpec((BS, BS), flat),
                pl.BlockSpec((BS, BS), lambda n, me: (0, blocks + n)),
                pl.BlockSpec((8, BS), flat),
                pl.BlockSpec((8, BS), flat),
            ],
            out_specs=[
                pl.BlockSpec((4, rows // 4, 2 * BS), cube),
                pl.BlockSpec((2, BS, BS), cube),
                pl.BlockSpec((8, BS), flat),
            ],
            scratch_shapes=[
                pltpu.VMEM((rows + 8, BS), f32),
                pltpu.VMEM((rows + 16, BS), jnp.int32),
                pltpu.VMEM((rows + 8, BS), f32),
                pltpu.VMEM((rows, 2 * BS), bf16),
                pltpu.VMEM((rows + 8, BS), f32),
                pltpu.VMEM((rows, BS), f32),
                pltpu.VMEM((2 * BS, BS), bf16),
            ],
        ),
        out_shape=[
            jax.ShapeDtypeStruct((4, rows // 4, 2 * channels), bf16),
            jax.ShapeDtypeStruct((2, BS, channels), f32),
            jax.ShapeDtypeStruct((8, channels), f32),
        ],
        compiler_params=vmem(24),
        name="mixing_backward",
    )(me, grad_gated, *(in_hbm(v) for v in (branch, states, conv, sig_r, sig_i)), ids, taps, gates, gates, rate, slope)


def folded(count):
    return list(range(0, 1)) + list(range(1, count, 2)) + list(range((count - 1) // 2 * 2, 0, -2))


class Links:
    def __init__(self, dp, mp):
        assert mp == 4 and dp % 2 == 0
        self.dp, self.mp = dp, mp
        self.line = dp // 2
        self.order = folded(self.line)
        self.place = {a: k for k, a in enumerate(self.order)}
        self.ring = [
            (2 * a + b, 2 * self.order[(self.place[a] + 1) % self.line] + b)
            for a in range(self.line)
            for b in range(2)
        ]

    def to_core(self, v):
        return lax.ppermute(v, "mp", [(i, i ^ 1) for i in range(self.mp)])

    def to_x(self, v):
        return lax.ppermute(v, "mp", [(i, i ^ 2) for i in range(self.mp)])

    def to_pair(self, v):
        return lax.ppermute(v, "dp", [(i, i ^ 1) for i in range(self.dp)])

    def along(self, v):
        return lax.ppermute(v, "dp", self.ring)

    def behind(self, me, steps):
        at = lax.shift_right_logical(me, 1)
        place = jnp.int32(0)
        for a in range(self.line):
            place = jnp.where(at == a, self.order[(self.place[a] - steps) % self.line], place)
        return place.astype(jnp.int32)


def in_hbm(v):
    return pltpu.with_memory_space_constraint(v, pltpu.HBM)


def hbm_out(shape, dtype):
    return pltpu.HBM(shape, dtype)


def vmem(mib):
    return pltpu.CompilerParams(vmem_limit_bytes=mib * 1024 * 1024)


UNIT = 384


def assemble(pieces, whole):
    @pl.when(pl.program_id(0) == 0)
    def _():
        rows = pieces[0].shape[0]
        for k, piece in enumerate(pieces):
            whole[k * rows:(k + 1) * rows, :] = piece[...]


def rows_call(kernel, pieces, more, more_specs, outs, out_specs, grid, name, mib, scratch=(), streamed=False):
    own, width = pieces[0].shape
    count = len(pieces)
    whole = pl.BlockSpec((count * own, width), lambda n: (0, 0))
    joined = count > 1

    def run(*refs):
        x, others = refs[0], refs[count:]
        if joined:
            x = refs[count + len(more)]
            assemble(refs[:count], x)
            others = refs[count:count + len(more)] + refs[count + len(more) + 1:]
        kernel(x, *others)

    if streamed:
        pieces, more = [in_hbm(v) for v in pieces], [in_hbm(v) for v in more]
        outs = [hbm_out(v.shape, v.dtype) for v in outs]
    return pl.pallas_call(
        run,
        grid=(grid,),
        in_specs=[pl.BlockSpec((own, width), lambda n: (0, 0))] * count + more_specs,
        out_specs=[whole] * joined + out_specs,
        out_shape=[jax.ShapeDtypeStruct((count * own, width), bf16)] * joined + outs,
        scratch_shapes=list(scratch),
        compiler_params=vmem(mib),
        name=name,
    )(*pieces, *more)


def against_kernel(x, w, send, keep):
    half = send.shape[0]
    result = lax.dot_general(x[...], w[...], (((1,), (1,)), ((), ())), preferred_element_type=f32).astype(bf16)
    send[...] = result[:half]
    keep[...] = result[half:]


def against_rows(x, w, name):
    rows, depth = x.shape
    width = w.shape[0]
    tile = 256
    half = pl.BlockSpec((rows // 2, tile), lambda n: (0, n))
    return rows_call(
        against_kernel, [x], [w], [pl.BlockSpec((tile, depth), lambda n: (n, 0))],
        [jax.ShapeDtypeStruct((rows // 2, width), bf16)] * 2, [half] * 2, width // tile,
        name, 20)


def project_kernel(x, w, out):
    out[...] = jnp.dot(x[...], w[...], preferred_element_type=f32)


def project_rows(pieces, w, tile, name, out=jax.ShapeDtypeStruct):
    own, width = pieces[0].shape
    columns = w.shape[1]
    return rows_call(
        project_kernel, pieces, [w], [pl.BlockSpec((width, tile), lambda n: (0, n))],
        [out((4 * own, columns), f32)], [pl.BlockSpec((4 * own, tile), lambda n: (0, n))],
        columns // tile, name, 24)


def ffn_forward_kernel(x, w, hidden, by_gate, by_up):
    both = jnp.dot(x[...], w[...], preferred_element_type=f32)
    up = both[:, UNIT:]
    value, slope = gelu_parts(both[:, :UNIT])
    hidden[...] = (value * up).astype(bf16)
    by_gate[...] = (up * slope).astype(bf16)
    by_up[...] = value.astype(bf16)


def ffn_forward(pieces, w):
    own, width = pieces[0].shape
    units = w.shape[1] // 2
    tile = pl.BlockSpec((4 * own, UNIT), lambda n: (0, n))
    return rows_call(
        ffn_forward_kernel, pieces, [w], [pl.BlockSpec((width, 2 * UNIT), lambda n: (0, n))],
        [jax.ShapeDtypeStruct((4 * own, units), bf16)] * 3, [tile] * 3,
        units // UNIT, "ffn_forward", 34, streamed=True)


def ffn_backward_kernel(tiles, x, w, by_gate, by_up, w_up, out, send, keep, whole):
    at = pl.program_id(0)

    @pl.when(at < tiles)
    def _():
        grad = jnp.dot(x[...], w[...], preferred_element_type=f32)
        out[:, :UNIT] = (grad * by_gate[...].astype(f32)).astype(bf16)
        out[:, UNIT:] = (grad * by_up[...].astype(f32)).astype(bf16)
        whole[at] = out[...]

    @pl.when(at >= tiles)
    def _():
        half = send.shape[0]
        result = sum(
            lax.dot_general(whole[k], w_up[:, 2 * k * UNIT:2 * (k + 1) * UNIT], (((1,), (1,)), ((), ())),
                            preferred_element_type=f32)
            for k in range(tiles))
        result = result.astype(bf16)
        send[...] = result[:half]
        keep[...] = result[half:]


def ffn_backward(x, w, by_gate, by_up, w_up):
    rows, width = x.shape
    units = w.shape[1]
    tiles = units // UNIT
    tile = 256
    first = lambda n: jnp.minimum(n, tiles - 1)
    then = lambda n: jnp.maximum(n - tiles, 0)
    half = pl.BlockSpec((rows // 2, tile), lambda n: (0, then(n)))
    return rows_call(
        functools.partial(ffn_backward_kernel, tiles), [x], [w, by_gate, by_up, w_up],
        [pl.BlockSpec((width, UNIT), lambda n: (0, first(n))), pl.BlockSpec((rows, UNIT), lambda n: (0, first(n))),
         pl.BlockSpec((rows, UNIT), lambda n: (0, first(n))),
         pl.BlockSpec((tile, 2 * units), lambda n: (then(n), 0))],
        [jax.ShapeDtypeStruct((rows, 2 * units), bf16)] + [jax.ShapeDtypeStruct((rows // 2, width), bf16)] * 2,
        [pl.BlockSpec((rows, 2 * UNIT), lambda n: (0, first(n))), half, half],
        tiles + width // tile, "ffn_backward", 46, [pltpu.VMEM((tiles, rows, 2 * UNIT), bf16)], streamed=True)


def pack_kernel(x, y, out, recur, inp, packed):
    rows, channels = x.shape
    columns = recur.shape[1]
    for n in range(channels // BS):
        block = slice(n * BS, (n + 1) * BS)
        packed[0:rows, 2 * n * BS:(2 * n + 1) * BS] = x[:, block]
        packed[0:rows, (2 * n + 1) * BS:(2 * n + 2) * BS] = y[:, block]
        packed[rows:rows + columns, block] = recur[n]
        packed[rows:rows + columns, channels + n * BS:channels + (n + 1) * BS] = inp[n]
    packed[0:rows, 2 * channels:3 * channels] = out[...]
    packed[rows:rows + columns, 2 * channels:3 * channels] = jnp.zeros((columns, channels), bf16)


def pack(x, y, out, recur, inp):
    rows, channels = x.shape
    return pl.pallas_call(
        pack_kernel,
        out_shape=jax.ShapeDtypeStruct((rows + recur.shape[1], 3 * channels), bf16),
        name="pack",
    )(x, y, out, recur, inp)


def weight_grad_kernel(line, shard, extra, groups, table, *refs):
    if extra:
        left_a, right_a, left_b, right_b, extra_a, extra_b, *sent, kept, total = refs
    else:
        left_a, right_a, left_b, right_b, *sent, kept, total = refs
    dims = (((0,), (0,)), ((), ()))
    total[...] = lax.dot_general(
        left_a[...], right_a[...], dims, preferred_element_type=f32
    ) + lax.dot_general(left_b[...], right_b[...], dims, preferred_element_type=f32)
    bit = table[line]
    size = line // groups
    for k in range(line):
        at = 2 * table[k]
        out = sent[k // size]
        mine = pl.ds(pl.multiple_of((at + bit) * shard, 16), shard)
        other = pl.ds(pl.multiple_of((at + 1 - bit) * shard, 16), shard)
        kept[k, 0:shard, :] = total[mine, :]
        out[k % size, 0:shard, :] = total[other, :].astype(bf16)
        if extra:
            kept[k, shard:shard + extra, :] = extra_a[0, at + bit] + extra_b[0, at + bit]
            out[k % size, shard:shard + extra, :] = (
                extra_a[0, at + 1 - bit] + extra_b[0, at + 1 - bit]).astype(bf16)


def weight_grad(table, left, right, tile, groups, extras=None):
    line = table.shape[0] - 1
    rows, width = left[0].shape
    columns = right[0].shape[1]
    shard = width // (2 * line)
    extra = extras[0].shape[2] if extras else 0
    lefts = pl.BlockSpec((rows, width), lambda n, t: (0, 0))
    rights = pl.BlockSpec((rows, tile), lambda n, t: (0, n))
    more = [pl.BlockSpec((1, 2 * line, extra, tile), lambda n, t: (n, 0, 0, 0))] * 2 if extra else []
    parts = lambda count: pl.BlockSpec((count, shard + extra, tile), lambda n, t: (0, 0, n))
    size = line // groups
    *sent, kept = pl.pallas_call(
        functools.partial(weight_grad_kernel, line, shard, extra, groups),
        grid_spec=pltpu.PrefetchScalarGridSpec(
            num_scalar_prefetch=1,
            grid=(columns // tile,),
            in_specs=[lefts, rights, lefts, rights] + more,
            out_specs=[parts(size)] * groups + [parts(line)],
            scratch_shapes=[pltpu.VMEM((width, tile), f32)],
        ),
        out_shape=[jax.ShapeDtypeStruct((size, shard + extra, columns), bf16)] * groups
        + [jax.ShapeDtypeStruct((line, shard + extra, columns), f32)],
        compiler_params=vmem(52 if tile > 1024 else 44),
        name="weight_grad",
    )(table, in_hbm(left[0]), in_hbm(right[0]), in_hbm(left[1]), in_hbm(right[1]), *(extras or ()))
    return sent, kept


def last_sum(write, held, at, outs, name):
    kept, sent, moving = held["kept"], held["sent"][at // held["size"]], held["moving"]
    shape = (1,) + kept.shape[1:]
    inside = at % held["size"]

    def kernel(kept, sent, moving, *outs):
        write(kept[0] + sent[0].astype(f32) + moving[...].astype(f32), *outs)

    return pl.pallas_call(
        kernel,
        grid=(1,),
        in_specs=[pl.BlockSpec(shape, lambda n: (at, 0, 0)), pl.BlockSpec(shape, lambda n: (inside, 0, 0)),
                  pl.BlockSpec(shape[1:], lambda n: (0, 0))],
        out_specs=[pl.BlockSpec(out, lambda n, rank=len(out): (0,) * rank) for out in outs],
        out_shape=[jax.ShapeDtypeStruct(out, f32) for out in outs],
        compiler_params=vmem(16),
        name=name,
    )(kept, sent, moving)


def write_plain(total, out):
    out[...] = total


def write_gate_up(total, gate, up):
    for k in range(gate.shape[1] // UNIT):
        gate[:, k * UNIT:(k + 1) * UNIT] = total[:, 2 * k * UNIT:(2 * k + 1) * UNIT]
        up[:, k * UNIT:(k + 1) * UNIT] = total[:, (2 * k + 1) * UNIT:(2 * k + 2) * UNIT]


def write_first(total, x, y, recur, inp):
    rows, channels = x.shape
    for n in range(channels // BS):
        block = slice(n * BS, (n + 1) * BS)
        x[:, block] = total[:rows, 2 * n * BS:(2 * n + 1) * BS]
        y[:, block] = total[:rows, (2 * n + 1) * BS:(2 * n + 2) * BS]
        recur[n] = total[rows:, block]
        inp[n] = total[rows:, channels + n * BS:channels + (n + 1) * BS]


class Bag(dict):
    def fence(self):
        values, tree = jax.tree.flatten(dict(self))
        values = lax.optimization_barrier(values)
        self.update(jax.tree.unflatten(tree, values))

    def take(self, *names):
        out = [self.pop(name) for name in names]
        return out if len(out) > 1 else out[0]


class Gather:
    def __init__(self, links, me, bag, name, shard, parts=None):
        self.links, self.me, self.bag, self.name = links, me, bag, name
        self.along_steps, self.pair_steps, self.placed, self.other_placed = 0, 0, 0, 0
        self.parts = parts or [(slice(0, shard.shape[0]), slice(0, shard.shape[1]))]
        bag[name] = {"z": [shard], "y": [], "whole": None}

    def along(self, steps=1):
        z = self.bag[self.name]["z"]
        for _ in range(steps):
            if self.along_steps < self.links.line - 1:
                z.append(self.links.along(z[self.along_steps]))
                self.along_steps += 1

    def pair(self, steps=1):
        held = self.bag[self.name]
        for _ in range(steps):
            if self.pair_steps <= self.along_steps and self.pair_steps < self.links.line:
                held["y"].append(self.links.to_pair(held["z"][self.pair_steps]))
                self.pair_steps += 1

    def put(self, pieces, at, bit):
        held = self.bag[self.name]
        base = 2 * self.links.behind(self.me, at)
        wholes = []
        for k, (rows, columns) in enumerate(self.parts):
            piece = pieces[at][rows, columns][None]
            whole = jnp.zeros((self.links.dp,) + piece.shape[1:], bf16) if held["whole"] is None else held["whole"][k]
            wholes.append(lax.dynamic_update_slice(whole, piece, (base + bit, 0, 0)))
        held["whole"] = wholes

    def place(self, z=0, y=0):
        held = self.bag[self.name]
        bit = lax.bitwise_and(self.me, 1)
        for _ in range(z):
            if self.placed <= self.along_steps:
                self.put(held["z"], self.placed, bit)
                self.placed += 1
        for _ in range(y):
            if self.other_placed < self.pair_steps:
                self.put(held["y"], self.other_placed, 1 - bit)
                self.other_placed += 1
        for k in range(min(self.placed, self.pair_steps, self.along_steps)):
            held["z"][k] = None
        for k in range(self.other_placed):
            held["y"][k] = None

    def finish(self):
        line = self.links.line
        while self.pair_steps < line:
            self.along()
            self.pair()
        self.place(line, line)
        return self.bag.pop(self.name)["whole"]


class PairGather:
    def __init__(self, links, me, bag, name, shard):
        self.links, self.me, self.bag, self.name = links, me, bag, name
        self.along_steps, self.placed = 0, 0
        bag[name] = {"own": shard, "other": None, "z": [], "whole": None}

    def pair(self):
        held = self.bag[self.name]
        held["other"] = self.links.to_pair(held["own"])

    def join(self):
        held = self.bag[self.name]
        bit = lax.bitwise_and(self.me, 1)
        both = jnp.zeros((2,) + held["own"].shape, bf16)
        both = lax.dynamic_update_slice(both, held["own"][None], (bit, 0, 0))
        held["z"].append(lax.dynamic_update_slice(both, held["other"][None], (1 - bit, 0, 0)))
        held["own"] = held["other"] = None

    def along(self):
        z = self.bag[self.name]["z"]
        if self.along_steps < self.links.line - 1:
            z.append(self.links.along(z[self.along_steps]))
            self.along_steps += 1

    def place(self, steps=1):
        held = self.bag[self.name]
        for _ in range(steps):
            if self.placed <= self.along_steps:
                piece = held["z"][self.placed][None]
                if held["whole"] is None:
                    held["whole"] = jnp.zeros((self.links.line,) + piece.shape[1:], bf16)
                at = self.links.behind(self.me, self.placed)
                held["whole"] = lax.dynamic_update_slice(held["whole"], piece, (at, 0, 0, 0))
                self.placed += 1
        for k in range(min(self.placed, self.along_steps)):
            held["z"][k] = None

    def finish(self):
        while self.along_steps < self.links.line - 1:
            self.along()
        self.place(self.links.line)
        return self.bag.pop(self.name)["whole"]


class Scatter:
    def __init__(self, links, bag, name, sent, kept):
        self.links, self.bag, self.name = links, bag, name
        self.pair_steps, self.along_steps = 0, 0
        self.size = links.line // len(sent)
        bag[name] = {"sent": list(sent), "kept": kept, "moving": None, "ready": None}

    def pair(self):
        sent = self.bag[self.name]["sent"]
        if self.pair_steps < len(sent):
            sent[self.pair_steps] = self.links.to_pair(sent[self.pair_steps])
            self.pair_steps += 1

    def ready(self):
        held = self.bag[self.name]
        at = self.along_steps
        if at < self.links.line - 1 and at // self.size < self.pair_steps and held["ready"] is None:
            held["ready"] = self.sum_here().astype(bf16)

    def along(self):
        held = self.bag[self.name]
        self.ready()
        if held["ready"] is not None:
            held["moving"], held["ready"] = self.links.along(held["ready"]), None
            self.along_steps += 1

    def sum_here(self):
        held = self.bag[self.name]
        at = self.along_steps
        total = held["kept"][at] + held["sent"][at // self.size][at % self.size].astype(f32)
        if held["moving"] is not None:
            total = total + held["moving"].astype(f32)
        return total

    def finish(self, write, *outs):
        while self.pair_steps < len(self.bag[self.name]["sent"]):
            self.pair()
        while self.along_steps < self.links.line - 1:
            self.along()
        held = self.bag.pop(self.name)
        held.pop("ready")
        return last_sum(write, {**held, "size": self.size}, self.along_steps, outs, self.name)


class AllSum:
    def __init__(self, bag, name, value, axes):
        self.bag, self.name = bag, name
        self.steps = [(axis, count, 1 << k) for axis, count in axes for k in range(count.bit_length() - 1)]
        assert all(count & (count - 1) == 0 for _, count in axes)
        bag[name] = value

    def step(self):
        if self.steps:
            axis, count, bit = self.steps.pop(0)
            value = self.bag[self.name]
            self.bag[self.name] = value + lax.ppermute(value, axis, [(i, i ^ bit) for i in range(count)])

    def finish(self):
        while self.steps:
            self.step()
        return self.bag.pop(self.name)


def body(links, block_in, doc_ids, mix_gain, proj_x, proj_y, conv_taps, recur_gate, input_gate, decay_param,
         proj_out, ffn_gain, ffn_gate, ffn_up, ffn_down, out_grad):
    micro_count, own_rows, width = block_in.shape
    group_rows = doc_ids.shape[1]
    assert group_rows == LEN and own_rows * 4 == group_rows and micro_count == 2
    d_rows, channels = proj_x.shape
    blocks = channels // BS
    hidden_units = ffn_gate.shape[1]
    assert hidden_units % UNIT == 0
    gate_columns = recur_gate.shape[2]
    dp_me = lax.axis_index("dp")
    me = lax.axis_index("mp").astype(jnp.int32).reshape(1)
    gain_one = mix_gain.astype(f32)
    gain_two = ffn_gain.astype(f32)
    to_core, to_x = links.to_core, links.to_x
    bag = Bag()

    def exchange(name):
        send, keep = bag.pop(name + "_send"), bag.pop(name + "_keep")
        own_rows_of = lambda v, k: v[k * own_rows:(k + 1) * own_rows].astype(f32)
        sent = to_core(send)
        bag[name + "_own"] = (keep, sent)
        bag[name + "_x"] = (own_rows_of(keep, 1) + own_rows_of(sent, 1)).astype(bf16)

    def summed(name):
        keep, sent = bag.pop(name + "_own")
        return (keep[:own_rows].astype(f32) + sent[:own_rows].astype(f32)) + bag.pop(name + "_x").astype(f32)

    def across(name):
        bag[name + "_x"] = to_x(bag[name + "_x"])

    def rows_of(name):
        own, core, x, diagonal = bag.take(name, name + "_core", name + "_x", name + "_diagonal")
        return core, diagonal, own, x

    packed = pack(proj_x, proj_y, proj_out.T, jnp.swapaxes(recur_gate, 1, 2), jnp.swapaxes(input_gate, 1, 2))
    inner_rows, outer_rows = slice(0, d_rows), slice(d_rows, d_rows + gate_columns)
    wide, narrow = slice(0, 2 * channels), slice(2 * channels, 3 * channels)
    first = Gather(links, dp_me, bag, "first", packed, [(inner_rows, wide), (inner_rows, narrow), (outer_rows, wide)])
    bag.fence()

    bag["cot0"], bag["cot1"] = out_grad[0], out_grad[1]
    first.along()
    first.pair()
    for micro in range(2):
        xin = block_in[micro].astype(f32)
        inverse = lax.rsqrt(jnp.mean(xin * xin, axis=-1, keepdims=True) + norm_eps)
        bag[f"inverse_one{micro}"] = inverse
        bag[f"normed{micro}"] = (xin * inverse * gain_one).astype(bf16)
    bag.fence()

    first.along()
    first.pair()
    bag["normed0_x"] = to_x(bag["normed0"])
    bag["normed0_core"] = to_core(bag["normed0"])
    first.place(2, 1)
    decay_values = decay_param.astype(f32)
    bag["rate"] = jnp.broadcast_to((-decay_scale * jax.nn.softplus(-decay_values))[None], (8, channels))
    bag["slope"] = jnp.broadcast_to((decay_scale * jax.nn.sigmoid(-decay_values))[None], (8, channels))
    bag["taps"] = jnp.concatenate([conv_taps.astype(f32), jnp.zeros((8 - KW, channels), f32)])
    bag["table"] = jnp.stack(
        [links.behind(dp_me, step + 1) for step in range(links.line)] + [lax.bitwise_and(dp_me, 1).astype(jnp.int32)])
    bag.fence()

    first.along()
    first.pair()
    bag["normed1_x"] = to_x(bag["normed1"])
    bag["normed0_diagonal"] = to_core(bag["normed0_x"])
    first.place(1, 1)
    gate_up = jnp.stack([ffn_gate.reshape(d_rows, -1, UNIT), ffn_up.reshape(d_rows, -1, UNIT)], axis=2)
    second = Gather(links, dp_me, bag, "second", gate_up.reshape(d_rows, 2 * hidden_units))
    third = PairGather(links, dp_me, bag, "third", ffn_down.T)
    for micro in range(2):
        bag[f"ids{micro}"] = jnp.broadcast_to(doc_ids[micro][:, None], (group_rows, BS))
    bag.fence()

    first.pair()
    second.along()
    third.pair()
    bag["cot0_x"] = to_x(bag["cot0"])
    first.place(1, 1)
    bag.fence()

    def mix(micro):
        bag[f"normed_all{micro}"], branch = project_rows(rows_of(f"normed{micro}"), bag["w_branch"], 256, "branch", hbm_out)
        branch = branch.reshape(4, own_rows, 2 * channels)
        gated, *rest = mixing_forward(me, branch, bag[f"ids{micro}"], bag["taps"], bag["gates"], bag["rate"])
        bag[f"mixed{micro}"] = [branch] + rest
        bag[f"gated{micro}"] = gated.reshape(group_rows, channels)

    def against_of(name, left, weight):
        bag[name + "_send"], bag[name + "_keep"] = against_rows(bag[left], bag[weight], weight + "_turned")

    def middle_of(micro):
        middle = block_in[micro].astype(f32) + summed(f"first{micro}")
        inverse = lax.rsqrt(jnp.mean(middle * middle, axis=-1, keepdims=True) + norm_eps)
        bag[f"middle{micro}"], bag[f"inverse_two{micro}"] = middle, inverse
        bag[f"two{micro}"] = (middle * inverse * gain_two).astype(bf16)

    second.along()
    second.pair()
    third.join()
    bag["cot1_x"] = to_x(bag["cot1"])
    w_branch, w_out, gates = first.finish()
    bag["w_branch"] = w_branch.reshape(width, 2 * channels)
    bag["gates"] = gates.reshape(BS, 2 * channels)
    bag["w_out"] = w_out.reshape(width, channels)
    mix(0)
    against_of("first0", "gated0", "w_out")
    bag.fence()

    bag["normed1_core"] = to_core(bag["normed1"])
    bag["normed1_diagonal"] = to_core(bag["normed1_x"])
    exchange("first0")
    second.place(1)
    bag.fence()

    second.along()
    second.pair()
    across("first0")
    second.place(1)
    mix(1)
    bag.fence()

    bag["cot0_core"] = to_core(bag["cot0"])
    bag["cot0_diagonal"] = to_core(bag["cot0_x"])
    middle_of(0)
    against_of("first1", "gated1", "w_out")
    bag.fence()

    third.along()
    second.pair()
    bag["two0_x"] = to_x(bag["two0"])
    bag["two0_core"] = to_core(bag["two0"])
    exchange("first1")
    bag["cot_all0"] = jnp.concatenate(rows_of("cot0"))
    second.place(3, 2)
    third.place()
    bag.fence()

    def forward(micro):
        bag[f"two_all{micro}"], bag[f"hidden{micro}"], *bag[f"by{micro}"] = ffn_forward(
            rows_of(f"two{micro}"), bag["w_up"])

    third.along()
    second.pair()
    across("first1")
    bag["two0_diagonal"] = to_core(bag["two0_x"])
    bag["cot1_core"] = to_core(bag["cot1"])
    bag["cot1_diagonal"] = to_core(bag["cot1_x"])
    bag["cot_all1"] = jnp.concatenate(rows_of("cot1"))
    second.place(0, 1)
    third.place()
    bag.fence()

    middle_of(1)
    bag.fence()

    third.along()
    bag["two1_x"] = to_x(bag["two1"])
    bag["w_up"] = second.finish()[0].reshape(width, 2 * hidden_units)
    third.place()
    forward(0)
    bag.fence()

    def back(micro):
        name = f"second{micro}"
        bag[f"grad_pre{micro}"], bag[name + "_send"], bag[name + "_keep"] = ffn_backward(
            bag[f"cot_all{micro}"], bag["w_down"], *bag.pop(f"by{micro}"), bag["w_up"])

    def grad_middle_of(micro):
        grad = summed(f"second{micro}")
        inverse, middle = bag[f"inverse_two{micro}"], bag[f"middle{micro}"]
        unit = middle * inverse
        total = out_grad[micro].astype(f32) + norm_back(grad, unit, inverse, gain_two)
        bag[f"grad_middle{micro}"] = total
        bag[f"gain_two{micro}"] = jnp.sum(grad * unit, axis=0)
        bag[f"low{micro}"] = total.astype(bf16)

    bag["two1_core"] = to_core(bag["two1"])
    bag["two1_diagonal"] = to_core(bag["two1_x"])
    bag["w_down"] = third.finish().reshape(width, hidden_units)
    back(0)
    bag.fence()

    exchange("second0")
    forward(1)
    bag.fence()

    across("second0")
    down_grad = Scatter(links, bag, "down_grad", *weight_grad(
        bag["table"], [bag["cot_all0"], bag["cot_all1"]], [bag["hidden0"], bag["hidden1"]], hidden_units, 2))
    bag.fence()

    down_grad.pair()
    back(1)
    bag.fence()

    exchange("second1")
    down_grad.ready()
    grad_middle_of(0)
    bag.fence()

    across("second1")
    down_grad.pair()
    bag["low0_core"] = to_core(bag["low0"])
    up_grad = Scatter(links, bag, "up_grad", *weight_grad(
        bag["table"], bag.take("two_all0", "two_all1"), bag.take("grad_pre0", "grad_pre1"), 2 * UNIT, 4))
    bag.fence()

    def output_of(micro):
        bag[f"output{micro}"] = (bag[f"middle{micro}"] + summed(f"down{micro}")).astype(bf16)

    bag["low0_x"] = to_x(bag["low0"])
    up_grad.pair()
    down_grad.along()
    grad_middle_of(1)
    against_of("down0", "hidden0", "w_down")
    bag.fence()

    def into_mix(micro):
        bag[f"low_all{micro}"], bag[f"grad_gated{micro}"] = project_rows(
            rows_of(f"low{micro}"), bag["w_out"], 256, "grad_gated")

    def mix_back(micro):
        grad, bag[f"gates_grad{micro}"], bag[f"small{micro}"] = mixing_backward(
            me, bag.pop(f"grad_gated{micro}").reshape(4, own_rows, channels), *bag.pop(f"mixed{micro}"),
            bag[f"ids{micro}"], bag["taps"], bag["gates"], bag["rate"], bag["slope"])
        bag[f"grad_branch{micro}"] = grad.reshape(group_rows, 2 * channels)
        against_of(f"third{micro}", f"grad_branch{micro}", "w_branch")

    bag["low1_x"] = to_x(bag["low1"])
    bag["low0_diagonal"] = to_core(bag["low0_x"])
    up_grad.pair()
    up_grad.along()
    exchange("down0")
    into_mix(0)
    mix_back(0)
    bag.fence()

    across("down0")
    bag["low1_core"] = to_core(bag["low1"])
    bag["low1_diagonal"] = to_core(bag["low1_x"])
    exchange("third0")
    up_grad.pair()
    up_grad.along()
    down_grad.ready()
    into_mix(1)
    out_grad_w = Scatter(links, bag, "out_grad", *weight_grad(
        bag["table"], bag.take("low_all0", "low_all1"), bag.take("gated0", "gated1"), 512, 1))
    bag.fence()

    across("third0")
    up_grad.pair()
    up_grad.along()
    down_grad.along()
    mix_back(1)
    bag.fence()

    exchange("third1")
    bag.fence()

    def leave(micro):
        grad = summed(f"third{micro}")
        inverse = bag[f"inverse_one{micro}"]
        unit = block_in[micro].astype(f32) * inverse
        bag[f"input_grad{micro}"] = bag[f"grad_middle{micro}"] + norm_back(grad, unit, inverse, gain_one)
        bag[f"gain_one{micro}"] = jnp.sum(grad * unit, axis=0)

    across("third1")
    out_grad_w.pair()
    down_grad.along()
    gates_grads = [bag.pop(f"gates_grad{micro}").reshape(2, links.dp, gate_columns, channels) for micro in range(2)]
    first_grad = Scatter(links, bag, "first_grad", *weight_grad(
        bag["table"], bag.take("normed_all0", "normed_all1"), bag.take("grad_branch0", "grad_branch1"), channels, 4,
        gates_grads))
    bag.fence()

    first_grad.pair()
    out_grad_w.along()
    leave(1)
    leave(0)
    against_of("down1", "hidden1", "w_down")
    gains = jnp.stack([bag.pop("gain_one0") + bag.pop("gain_one1"), bag.pop("gain_two0") + bag.pop("gain_two1")])
    bag["sums"] = gains.reshape(-1, 128)
    gain_rows = bag["sums"].shape[0]
    bag.fence()

    first_grad.pair()
    first_grad.along()
    sums = AllSum(bag, "gains", bag.pop("sums"), [("mp", links.mp)])
    small = (bag.pop("small0") + bag.pop("small1")).reshape(-1, 128)
    sums = AllSum(bag, "sums", jnp.concatenate([sums.finish(), small]), [("dp", links.dp)])
    exchange("down1")
    output_of(0)
    bag["up_total"] = up_grad.finish(write_gate_up, (d_rows, hidden_units), (d_rows, hidden_units))
    bag.fence()

    first_grad.pair()
    first_grad.along()
    out_grad_w.along()
    sums.step()
    bag["down1_xa"] = to_x(bag["down1_x"][:own_rows // 2])
    bag["down_total"] = down_grad.finish(write_plain, (d_rows, hidden_units))
    bag.fence()

    first_grad.pair()
    first_grad.along()
    out_grad_w.along()
    sums.step()
    bag["down1_xb"] = to_x(bag["down1_x"][own_rows // 2:])
    bag["input_grads"] = jnp.stack([bag.pop("input_grad0"), bag.pop("input_grad1")])
    bag.fence()

    bag["down1_x"] = jnp.concatenate(bag.take("down1_xa", "down1_xb"))
    output_of(1)
    bag["outputs"] = jnp.stack(bag.take("output0", "output1"))
    bag["out_total"] = out_grad_w.finish(write_plain, (d_rows, channels))
    x_grad, y_grad, recur, inp = first_grad.finish(
        write_first, (d_rows, channels), (d_rows, channels), (blocks, gate_columns, BS), (blocks, gate_columns, BS))
    sums = sums.finish()
    gains = sums[:gain_rows].reshape(2, width)
    small = sums[gain_rows:].reshape(8, channels)
    return (
        bag["outputs"],
        bag["input_grads"],
        gains[0],
        x_grad,
        y_grad,
        small[0:KW],
        jnp.swapaxes(recur, 1, 2),
        jnp.swapaxes(inp, 1, 2),
        small[KW],
        bag["out_total"][0].T,
        gains[1],
        *bag["up_total"],
        bag["down_total"][0].T,
    )


def solution(mesh):
    links = Links(mesh.shape["dp"], mesh.shape["mp"])
    tokens = P(None, ("dp", "mp"), None)
    rows, columns, gate = P("dp", "mp"), P("mp", "dp"), P("mp", None, "dp")
    return jax.shard_map(
        functools.partial(body, links),
        mesh=mesh,
        in_specs=(tokens, P(None, "dp"), P(), rows, rows, P(None, "mp"), gate, gate, P("mp"), columns, P(), rows,
                  rows, columns, tokens),
        out_specs=(tokens, tokens, P(), rows, rows, P(None, "mp"), gate, gate, P("mp"), columns, P(), rows, rows,
                   columns),
        check_vma=False,
    )
```

```python
import functools

import jax
import jax.numpy as jnp
import numpy as np
from jax import lax
from jax.experimental import pallas as pl
from jax.experimental.pallas import tpu as pltpu
from jax.sharding import PartitionSpec as P

LEN = 1024
BS = 128
KW = 4

norm_eps = 1e-06
root_floor = 0.01
decay_scale = 8.0
gelu_a = 0.7978845608028654
gelu_b = 0.044715

f32 = jnp.float32
bf16 = jnp.bfloat16


BLOCK_AT = (2, 0, 3, 1)


def project(left, right):
    return jnp.dot(left, right, preferred_element_type=f32)


def inner(left, right):
    return lax.dot_general(left, right, (((0,), (0,)), ((), ())), preferred_element_type=f32)


def against(left, right):
    return lax.dot_general(left, right, (((1,), (1,)), ((), ())), preferred_element_type=f32)


def norm_back(grad_normed, unit_rows, inverse, gain):
    scaled = grad_normed * gain
    return inverse * (scaled - unit_rows * jnp.mean(scaled * unit_rows, axis=-1, keepdims=True))


def gelu_parts(v):
    squared = v * v
    inside = gelu_a * v * (1.0 + gelu_b * squared)
    t = jnp.tanh(inside)
    half = 0.5 * (1.0 + t)
    value = v * half
    slope = half + 0.5 * v * (1.0 - t * t) * (gelu_a * (1.0 + 3.0 * gelu_b * squared))
    return value, slope


def gelu_value(v):
    return 0.5 * v * (1.0 + jnp.tanh(gelu_a * v * (1.0 + gelu_b * v * v)))


def place_of(me, block):
    differ = lax.bitwise_xor(me, block)
    low = lax.bitwise_and(differ, 1)
    high = lax.shift_right_logical(differ, 1)
    return 2 * (1 - low) + high


CHUNK = 64
STEP = 64


def tile_scan(a, b, row):
    for d in (1, 2, 4):
        use = row >= d
        b = b + a * jnp.where(use, pltpu.roll(b, d, 0), 0.0)
        a = a * jnp.where(use, pltpu.roll(a, d, 0), 1.0)
    return a, b


def tile_scan_back(a, b, row):
    for d in (1, 2, 4):
        use = row < 8 - d
        b = b + a * jnp.where(use, pltpu.roll(b, 8 - d, 0), 0.0)
        a = a * jnp.where(use, pltpu.roll(a, 8 - d, 0), 1.0)
    return a, b


def spread(row):
    return jnp.broadcast_to(row, (8, BS))


def mixing_forward_kernel(me_ref, branch, ids, taps, gate_r, gate_i, rate, gated, states, conv, sig_r, sig_i,
                          xpad, idpad, logits, gates):
    gates[0:BS, :] = gate_r[...]
    gates[BS:2 * BS, :] = gate_i[...]
    rows = LEN
    quarter = rows // 4
    me = me_ref[0]
    xpad[0:8, :] = jnp.zeros((8, BS), f32)
    idpad[0:8, :] = jnp.full((8, BS), -1, jnp.int32)
    idpad[8:8 + rows, :] = ids[...]
    for block in range(4):
        at = place_of(me, block)
        xpad[8 + block * quarter: 8 + (block + 1) * quarter, :] = branch[at, :, 0:BS]
    rate_row = rate[0:1, :]

    def convolve(step, _):
        base = pl.multiple_of(step * CHUNK, CHUNK)
        own_ids = idpad[pl.ds(base + 8, CHUNK), :]
        total = taps[0:1, :] * xpad[pl.ds(base + 8, CHUNK), :]
        for k in range(1, KW):
            same = idpad[pl.ds(base + 8 - k, CHUNK), :] == own_ids
            total = total + taps[k:k + 1, :] * jnp.where(same, xpad[pl.ds(base + 8 - k, CHUNK), :], 0.0)
        conv[pl.ds(base, CHUNK), :] = total.astype(bf16)
        return 0

    lax.fori_loop(0, rows // CHUNK, convolve, 0, unroll=2)
    logits[...] = lax.dot_general(conv[...], gates[...], (((1,), (1,)), ((), ())), preferred_element_type=f32)
    row = lax.broadcasted_iota(jnp.int32, (8, BS), 0)

    def advance(step, carry):
        base = pl.multiple_of(step * STEP, STEP)
        here = pl.ds(base, STEP)
        block = lax.div(step, quarter // STEP)
        at = place_of(me, block)
        there = pl.ds(pl.multiple_of(base - block * quarter, STEP), STEP)
        sr = jax.nn.sigmoid(logits[here, 0:BS])
        si = jax.nn.sigmoid(logits[here, BS:2 * BS])
        sig_r[here, :] = sr
        sig_i[here, :] = si
        same = idpad[pl.ds(base + 7, STEP), :] == idpad[pl.ds(base + 8, STEP), :]
        a = jnp.where(same, jnp.exp(rate_row * sr), 0.0)
        margin = jnp.maximum(1.0 - a * a, root_floor)
        b = conv[here, :].astype(f32) * si * (margin * lax.rsqrt(margin))
        tiles = []
        for k in range(STEP // 8):
            part = slice(8 * k, 8 * k + 8)
            product, local = tile_scan(a[part], b[part], row)
            tiles.append(local + product * carry)
            carry = spread(local[7:8]) + spread(product[7:8]) * carry
        state = jnp.concatenate(tiles, axis=0)
        states[here, :] = state
        gated[at, there, :] = (state * gelu_value(branch[at, there, BS:2 * BS])).astype(bf16)
        return carry

    lax.fori_loop(0, rows // STEP, advance, jnp.zeros((8, BS), f32), unroll=2)


def mixing_backward_kernel(me_ref, grad_gated, branch, states, conv, sig_r, sig_i, ids, taps, gate_r, gate_i, rate,
                           slope, grad_branch, grad_gates, small,
                           xpad, idpad, spad, low, gcpad, through, gates):
    gates[0:BS, :] = gate_r[...]
    gates[BS:2 * BS, :] = gate_i[...]
    rows = LEN
    quarter = rows // 4
    me = me_ref[0]
    zero8 = jnp.zeros((8, BS), f32)
    xpad[0:8, :] = zero8
    spad[0:8, :] = zero8
    spad[8:8 + rows, :] = states[...]
    idpad[0:8, :] = jnp.full((8, BS), -1, jnp.int32)
    idpad[8:8 + rows, :] = ids[...]
    idpad[8 + rows:16 + rows, :] = jnp.full((8, BS), -1, jnp.int32)
    gcpad[rows:rows + 8, :] = zero8
    rate_row = rate[0:1, :]
    slope_row = slope[0:1, :]
    for block in range(4):
        at = place_of(me, block)
        xpad[8 + block * quarter: 8 + (block + 1) * quarter, :] = branch[at, :, 0:BS]
    row = lax.broadcasted_iota(jnp.int32, (8, BS), 0)
    fold = lambda v: jnp.sum(v.reshape(v.shape[0] // 8, 8, BS), axis=0)
    steps = rows // STEP

    def retreat(count, held):
        carry, decay_sum = held
        step = steps - 1 - count
        base = pl.multiple_of(step * STEP, STEP)
        here = pl.ds(base, STEP)
        block = lax.div(step, quarter // STEP)
        at = place_of(me, block)
        there = pl.ds(pl.multiple_of(base - block * quarter, STEP), STEP)
        value, gradient = gelu_parts(branch[at, there, BS:2 * BS])
        incoming = grad_gated[at, there, :]
        grad_states = incoming * value
        grad_branch[at, there, BS:2 * BS] = (gradient * states[here, :] * incoming).astype(bf16)
        same = idpad[pl.ds(base + 7, STEP), :] == idpad[pl.ds(base + 8, STEP), :]
        sr = sig_r[here, :]
        si = sig_i[here, :]
        a = jnp.where(same, jnp.exp(rate_row * sr), 0.0)
        pushed = a * grad_states
        us, gs = [], []
        for k in reversed(range(STEP // 8)):
            part = slice(8 * k, 8 * k + 8)
            product, local = tile_scan_back(a[part], pushed[part], row)
            u = local + product * carry
            us.insert(0, u)
            gs.insert(0, grad_states[part] + jnp.where(row == 7, carry, pltpu.roll(u, 7, 0)))
            carry = spread(local[0:1]) + spread(product[0:1]) * carry
        u = jnp.concatenate(us, axis=0)
        g = jnp.concatenate(gs, axis=0)
        square = a * a
        inside = 1.0 - square
        margin = jnp.maximum(inside, root_floor)
        inverse = lax.rsqrt(margin)
        multiplier = margin * inverse
        gsi = g * si
        gcsi = gsi * conv[here, :].astype(f32)
        grad_log = u * spad[pl.ds(base + 7, STEP), :] - jnp.where(inside > root_floor, gcsi * square * inverse, 0.0)
        gcpad[here, :] = gsi * multiplier
        weighted = grad_log * sr
        low[here, 0:BS] = (weighted * (1.0 - sr) * rate_row).astype(bf16)
        low[here, BS:2 * BS] = (gcsi * multiplier * (1.0 - si)).astype(bf16)
        return carry, decay_sum + fold(weighted)

    _, decay_sum = lax.fori_loop(0, steps, retreat, (zero8, zero8), unroll=2)

    both_gates = lax.dot_general(low[...], conv[...], (((0,), (0,)), ((), ())), preferred_element_type=f32)
    grad_gates[0] = both_gates[0:BS]
    grad_gates[1] = both_gates[BS:2 * BS]
    through[...] = lax.dot_general(low[...], gates[...], (((1,), (0,)), ((), ())), preferred_element_type=f32)

    def add_gates(step, _):
        here = pl.ds(pl.multiple_of(step * CHUNK, CHUNK), CHUNK)
        gcpad[here, :] = gcpad[here, :] + through[here, :]
        return 0

    lax.fori_loop(0, rows // CHUNK, add_gates, 0, unroll=4)

    def finish(step, sums):
        base = pl.multiple_of(step * CHUNK, CHUNK)
        block = lax.div(step, quarter // CHUNK)
        at = place_of(me, block)
        there = pl.ds(pl.multiple_of(base - block * quarter, CHUNK), CHUNK)
        gc = gcpad[pl.ds(base, CHUNK), :]
        own_ids = idpad[pl.ds(base + 8, CHUNK), :]
        new = [sums[0] + fold(gc * xpad[pl.ds(base + 8, CHUNK), :])]
        grad_x = taps[0:1, :] * gc
        for k in range(1, KW):
            same = idpad[pl.ds(base + 8 - k, CHUNK), :] == own_ids
            new.append(sums[k] + fold(jnp.where(same, gc * xpad[pl.ds(base + 8 - k, CHUNK), :], 0.0)))
            after = idpad[pl.ds(base + 8 + k, CHUNK), :] == own_ids
            grad_x = grad_x + taps[k:k + 1, :] * jnp.where(after, gcpad[pl.ds(base + k, CHUNK), :], 0.0)
        grad_branch[at, there, 0:BS] = grad_x.astype(bf16)
        return tuple(new)

    sums = lax.fori_loop(0, rows // CHUNK, finish, (zero8,) * KW, unroll=2)
    small[...] = jnp.zeros((8, BS), f32)
    for k in range(KW):
        small[k:k + 1, :] = jnp.sum(sums[k], axis=0, keepdims=True)
    small[KW:KW + 1, :] = jnp.sum(decay_sum, axis=0, keepdims=True) * slope_row


def mixing_forward(me, branch, ids, taps, gates, rate):
    rows = LEN
    blocks = branch.shape[2] // (2 * BS)
    channels = blocks * BS
    flat = lambda n, me: (0, n)
    return pl.pallas_call(
        mixing_forward_kernel,
        grid_spec=pltpu.PrefetchScalarGridSpec(
            num_scalar_prefetch=1,
            grid=(blocks,),
            in_specs=[
                pl.BlockSpec((4, rows // 4, 2 * BS), lambda n, me: (0, 0, n)),
                pl.BlockSpec((rows, BS), lambda n, me: (0, 0)),
                pl.BlockSpec((8, BS), flat),
                pl.BlockSpec((BS, BS), flat),
                pl.BlockSpec((BS, BS), lambda n, me: (0, blocks + n)),
                pl.BlockSpec((8, BS), flat),
            ],
            out_specs=[
                pl.BlockSpec((4, rows // 4, BS), lambda n, me: (0, 0, n)),
                pl.BlockSpec((rows, BS), flat),
                pl.BlockSpec((rows, BS), flat),
                pl.BlockSpec((rows, BS), flat),
                pl.BlockSpec((rows, BS), flat),
            ],
            scratch_shapes=[
                pltpu.VMEM((rows + 8, BS), f32),
                pltpu.VMEM((rows + 8, BS), jnp.int32),
                pltpu.VMEM((rows, 2 * BS), f32),
                pltpu.VMEM((2 * BS, BS), bf16),
            ],
        ),
        out_shape=[
            jax.ShapeDtypeStruct((4, rows // 4, channels), bf16),
            hbm_out((rows, channels), f32),
            hbm_out((rows, channels), bf16),
            hbm_out((rows, channels), f32),
            hbm_out((rows, channels), f32),
        ],
        compiler_params=vmem(16),
        name="mixing_forward",
    )(me, in_hbm(branch), ids, taps, gates, gates, rate)


def mixing_backward(me, grad_gated, branch, states, conv, sig_r, sig_i, ids, taps, gates, rate, slope):
    rows = LEN
    blocks = branch.shape[2] // (2 * BS)
    channels = blocks * BS
    flat = lambda n, me: (0, n)
    cube = lambda n, me: (0, 0, n)
    return pl.pallas_call(
        mixing_backward_kernel,
        grid_spec=pltpu.PrefetchScalarGridSpec(
            num_scalar_prefetch=1,
            grid=(blocks,),
            in_specs=[
                pl.BlockSpec((4, rows // 4, BS), cube),
                pl.BlockSpec((4, rows // 4, 2 * BS), cube),
                pl.BlockSpec((rows, BS), flat),
                pl.BlockSpec((rows, BS), flat),
                pl.BlockSpec((rows, BS), flat),
                pl.BlockSpec((rows, BS), flat),
                pl.BlockSpec((rows, BS), lambda n, me: (0, 0)),
                pl.BlockSpec((8, BS), flat),
                pl.BlockSpec((BS, BS), flat),
                pl.BlockSpec((BS, BS), lambda n, me: (0, blocks + n)),
                pl.BlockSpec((8, BS), flat),
                pl.BlockSpec((8, BS), flat),
            ],
            out_specs=[
                pl.BlockSpec((4, rows // 4, 2 * BS), cube),
                pl.BlockSpec((2, BS, BS), cube),
                pl.BlockSpec((8, BS), flat),
            ],
            scratch_shapes=[
                pltpu.VMEM((rows + 8, BS), f32),
                pltpu.VMEM((rows + 16, BS), jnp.int32),
                pltpu.VMEM((rows + 8, BS), f32),
                pltpu.VMEM((rows, 2 * BS), bf16),
                pltpu.VMEM((rows + 8, BS), f32),
                pltpu.VMEM((rows, BS), f32),
                pltpu.VMEM((2 * BS, BS), bf16),
            ],
        ),
        out_shape=[
            jax.ShapeDtypeStruct((4, rows // 4, 2 * channels), bf16),
            jax.ShapeDtypeStruct((2, BS, channels), f32),
            jax.ShapeDtypeStruct((8, channels), f32),
        ],
        compiler_params=vmem(24),
        name="mixing_backward",
    )(me, grad_gated, *(in_hbm(v) for v in (branch, states, conv, sig_r, sig_i)), ids, taps, gates, gates, rate, slope)


def folded(count):
    return list(range(0, 1)) + list(range(1, count, 2)) + list(range((count - 1) // 2 * 2, 0, -2))


class Links:
    def __init__(self, dp, mp):
        assert mp == 4 and dp % 2 == 0
        self.dp, self.mp = dp, mp
        self.line = dp // 2
        self.order = folded(self.line)
        self.place = {a: k for k, a in enumerate(self.order)}
        self.ring = [
            (2 * a + b, 2 * self.order[(self.place[a] + 1) % self.line] + b)
            for a in range(self.line)
            for b in range(2)
        ]

    def to_core(self, v):
        return lax.ppermute(v, "mp", [(i, i ^ 1) for i in range(self.mp)])

    def to_x(self, v):
        return lax.ppermute(v, "mp", [(i, i ^ 2) for i in range(self.mp)])

    def to_pair(self, v):
        return lax.ppermute(v, "dp", [(i, i ^ 1) for i in range(self.dp)])

    def along(self, v):
        return lax.ppermute(v, "dp", self.ring)

    def behind(self, me, steps):
        at = lax.shift_right_logical(me, 1)
        place = jnp.int32(0)
        for a in range(self.line):
            place = jnp.where(at == a, self.order[(self.place[a] - steps) % self.line], place)
        return place.astype(jnp.int32)


def in_hbm(v):
    return pltpu.with_memory_space_constraint(v, pltpu.HBM)


def hbm_out(shape, dtype):
    return pltpu.HBM(shape, dtype)


def vmem(mib):
    return pltpu.CompilerParams(vmem_limit_bytes=mib * 1024 * 1024)


UNIT = 384


def assemble(pieces, whole):
    @pl.when(pl.program_id(0) == 0)
    def _():
        rows = pieces[0].shape[0]
        for k, piece in enumerate(pieces):
            whole[k * rows:(k + 1) * rows, :] = piece[...]


def rows_call(kernel, pieces, more, more_specs, outs, out_specs, grid, name, mib, scratch=(), streamed=False):
    own, width = pieces[0].shape
    count = len(pieces)
    whole = pl.BlockSpec((count * own, width), lambda n: (0, 0))
    joined = count > 1

    def run(*refs):
        x, others = refs[0], refs[count:]
        if joined:
            x = refs[count + len(more)]
            assemble(refs[:count], x)
            others = refs[count:count + len(more)] + refs[count + len(more) + 1:]
        kernel(x, *others)

    if streamed:
        pieces, more = [in_hbm(v) for v in pieces], [in_hbm(v) for v in more]
        outs = [hbm_out(v.shape, v.dtype) for v in outs]
    return pl.pallas_call(
        run,
        grid=(grid,),
        in_specs=[pl.BlockSpec((own, width), lambda n: (0, 0))] * count + more_specs,
        out_specs=[whole] * joined + out_specs,
        out_shape=[jax.ShapeDtypeStruct((count * own, width), bf16)] * joined + outs,
        scratch_shapes=list(scratch),
        compiler_params=vmem(mib),
        name=name,
    )(*pieces, *more)


def against_kernel(x, w, send, keep):
    half = send.shape[0]
    result = lax.dot_general(x[...], w[...], (((1,), (1,)), ((), ())), preferred_element_type=f32).astype(bf16)
    send[...] = result[:half]
    keep[...] = result[half:]


def against_rows(x, w, name):
    rows, depth = x.shape
    width = w.shape[0]
    tile = 256
    half = pl.BlockSpec((rows // 2, tile), lambda n: (0, n))
    return rows_call(
        against_kernel, [x], [w], [pl.BlockSpec((tile, depth), lambda n: (n, 0))],
        [jax.ShapeDtypeStruct((rows // 2, width), bf16)] * 2, [half] * 2, width // tile,
        name, 20)


def project_kernel(x, w, out):
    out[...] = jnp.dot(x[...], w[...], preferred_element_type=f32)


def project_rows(pieces, w, tile, name, out=jax.ShapeDtypeStruct):
    own, width = pieces[0].shape
    columns = w.shape[1]
    return rows_call(
        project_kernel, pieces, [w], [pl.BlockSpec((width, tile), lambda n: (0, n))],
        [out((4 * own, columns), f32)], [pl.BlockSpec((4 * own, tile), lambda n: (0, n))],
        columns // tile, name, 24)


def ffn_forward_kernel(x, w, hidden, by_gate, by_up):
    both = jnp.dot(x[...], w[...], preferred_element_type=f32)
    up = both[:, UNIT:]
    value, slope = gelu_parts(both[:, :UNIT])
    hidden[...] = (value * up).astype(bf16)
    by_gate[...] = (up * slope).astype(bf16)
    by_up[...] = value.astype(bf16)


def ffn_forward(pieces, w):
    own, width = pieces[0].shape
    units = w.shape[1] // 2
    tile = pl.BlockSpec((4 * own, UNIT), lambda n: (0, n))
    return rows_call(
        ffn_forward_kernel, pieces, [w], [pl.BlockSpec((width, 2 * UNIT), lambda n: (0, n))],
        [jax.ShapeDtypeStruct((4 * own, units), bf16)] * 3, [tile] * 3,
        units // UNIT, "ffn_forward", 34, streamed=True)


def ffn_backward_kernel(tiles, x, w, by_gate, by_up, w_up, out, send, keep, whole):
    at = pl.program_id(0)

    @pl.when(at < tiles)
    def _():
        grad = jnp.dot(x[...], w[...], preferred_element_type=f32)
        out[:, :UNIT] = (grad * by_gate[...].astype(f32)).astype(bf16)
        out[:, UNIT:] = (grad * by_up[...].astype(f32)).astype(bf16)
        whole[at] = out[...]

    @pl.when(at >= tiles)
    def _():
        half = send.shape[0]
        result = sum(
            lax.dot_general(whole[k], w_up[:, 2 * k * UNIT:2 * (k + 1) * UNIT], (((1,), (1,)), ((), ())),
                            preferred_element_type=f32)
            for k in range(tiles))
        result = result.astype(bf16)
        send[...] = result[:half]
        keep[...] = result[half:]


def ffn_backward(x, w, by_gate, by_up, w_up):
    rows, width = x.shape
    units = w.shape[1]
    tiles = units // UNIT
    tile = 256
    first = lambda n: jnp.minimum(n, tiles - 1)
    then = lambda n: jnp.maximum(n - tiles, 0)
    half = pl.BlockSpec((rows // 2, tile), lambda n: (0, then(n)))
    return rows_call(
        functools.partial(ffn_backward_kernel, tiles), [x], [w, by_gate, by_up, w_up],
        [pl.BlockSpec((width, UNIT), lambda n: (0, first(n))), pl.BlockSpec((rows, UNIT), lambda n: (0, first(n))),
         pl.BlockSpec((rows, UNIT), lambda n: (0, first(n))),
         pl.BlockSpec((tile, 2 * units), lambda n: (then(n), 0))],
        [jax.ShapeDtypeStruct((rows, 2 * units), bf16)] + [jax.ShapeDtypeStruct((rows // 2, width), bf16)] * 2,
        [pl.BlockSpec((rows, 2 * UNIT), lambda n: (0, first(n))), half, half],
        tiles + width // tile, "ffn_backward", 46, [pltpu.VMEM((tiles, rows, 2 * UNIT), bf16)], streamed=True)


def pack_kernel(x, y, out, recur, inp, packed):
    rows, channels = x.shape
    columns = recur.shape[1]
    for n in range(channels // BS):
        block = slice(n * BS, (n + 1) * BS)
        packed[0:rows, 2 * n * BS:(2 * n + 1) * BS] = x[:, block]
        packed[0:rows, (2 * n + 1) * BS:(2 * n + 2) * BS] = y[:, block]
        packed[rows:rows + columns, block] = recur[n]
        packed[rows:rows + columns, channels + n * BS:channels + (n + 1) * BS] = inp[n]
    packed[0:rows, 2 * channels:3 * channels] = out[...]
    packed[rows:rows + columns, 2 * channels:3 * channels] = jnp.zeros((columns, channels), bf16)


def pack(x, y, out, recur, inp):
    rows, channels = x.shape
    return pl.pallas_call(
        pack_kernel,
        out_shape=jax.ShapeDtypeStruct((rows + recur.shape[1], 3 * channels), bf16),
        name="pack",
    )(x, y, out, recur, inp)


def weight_grad_kernel(line, shard, extra, groups, table, *refs):
    if extra:
        left_a, right_a, left_b, right_b, extra_a, extra_b, *sent, kept, total = refs
    else:
        left_a, right_a, left_b, right_b, *sent, kept, total = refs
    dims = (((0,), (0,)), ((), ()))
    total[...] = lax.dot_general(
        left_a[...], right_a[...], dims, preferred_element_type=f32
    ) + lax.dot_general(left_b[...], right_b[...], dims, preferred_element_type=f32)
    bit = table[line]
    size = line // groups
    for k in range(line):
        at = 2 * table[k]
        out = sent[k // size]
        mine = pl.ds(pl.multiple_of((at + bit) * shard, 16), shard)
        other = pl.ds(pl.multiple_of((at + 1 - bit) * shard, 16), shard)
        kept[k, 0:shard, :] = total[mine, :]
        out[k % size, 0:shard, :] = total[other, :].astype(bf16)
        if extra:
            kept[k, shard:shard + extra, :] = extra_a[0, at + bit] + extra_b[0, at + bit]
            out[k % size, shard:shard + extra, :] = (
                extra_a[0, at + 1 - bit] + extra_b[0, at + 1 - bit]).astype(bf16)


def weight_grad(table, left, right, tile, groups, extras=None):
    line = table.shape[0] - 1
    rows, width = left[0].shape
    columns = right[0].shape[1]
    shard = width // (2 * line)
    extra = extras[0].shape[2] if extras else 0
    lefts = pl.BlockSpec((rows, width), lambda n, t: (0, 0))
    rights = pl.BlockSpec((rows, tile), lambda n, t: (0, n))
    more = [pl.BlockSpec((1, 2 * line, extra, tile), lambda n, t: (n, 0, 0, 0))] * 2 if extra else []
    parts = lambda count: pl.BlockSpec((count, shard + extra, tile), lambda n, t: (0, 0, n))
    size = line // groups
    *sent, kept = pl.pallas_call(
        functools.partial(weight_grad_kernel, line, shard, extra, groups),
        grid_spec=pltpu.PrefetchScalarGridSpec(
            num_scalar_prefetch=1,
            grid=(columns // tile,),
            in_specs=[lefts, rights, lefts, rights] + more,
            out_specs=[parts(size)] * groups + [parts(line)],
            scratch_shapes=[pltpu.VMEM((width, tile), f32)],
        ),
        out_shape=[jax.ShapeDtypeStruct((size, shard + extra, columns), bf16)] * groups
        + [jax.ShapeDtypeStruct((line, shard + extra, columns), f32)],
        compiler_params=vmem(52 if tile > 1024 else 44),
        name="weight_grad",
    )(table, in_hbm(left[0]), in_hbm(right[0]), in_hbm(left[1]), in_hbm(right[1]), *(extras or ()))
    return sent, kept


def last_sum(write, held, at, outs, name):
    kept, sent, moving = held["kept"], held["sent"][at // held["size"]], held["moving"]
    shape = (1,) + kept.shape[1:]
    inside = at % held["size"]

    def kernel(kept, sent, moving, *outs):
        write(kept[0] + sent[0].astype(f32) + moving[...].astype(f32), *outs)

    return pl.pallas_call(
        kernel,
        grid=(1,),
        in_specs=[pl.BlockSpec(shape, lambda n: (at, 0, 0)), pl.BlockSpec(shape, lambda n: (inside, 0, 0)),
                  pl.BlockSpec(shape[1:], lambda n: (0, 0))],
        out_specs=[pl.BlockSpec(out, lambda n, rank=len(out): (0,) * rank) for out in outs],
        out_shape=[jax.ShapeDtypeStruct(out, f32) for out in outs],
        compiler_params=vmem(16),
        name=name,
    )(in_hbm(kept), sent, moving)


def write_plain(total, out):
    out[...] = total


def write_gate_up(total, gate, up):
    for k in range(gate.shape[1] // UNIT):
        gate[:, k * UNIT:(k + 1) * UNIT] = total[:, 2 * k * UNIT:(2 * k + 1) * UNIT]
        up[:, k * UNIT:(k + 1) * UNIT] = total[:, (2 * k + 1) * UNIT:(2 * k + 2) * UNIT]


def write_first(total, x, y, recur, inp):
    rows, channels = x.shape
    for n in range(channels // BS):
        block = slice(n * BS, (n + 1) * BS)
        x[:, block] = total[:rows, 2 * n * BS:(2 * n + 1) * BS]
        y[:, block] = total[:rows, (2 * n + 1) * BS:(2 * n + 2) * BS]
        recur[n] = total[rows:, block]
        inp[n] = total[rows:, channels + n * BS:channels + (n + 1) * BS]


class Bag(dict):
    def fence(self):
        values, tree = jax.tree.flatten(dict(self))
        values = lax.optimization_barrier(values)
        self.update(jax.tree.unflatten(tree, values))

    def take(self, *names):
        out = [self.pop(name) for name in names]
        return out if len(out) > 1 else out[0]


class Gather:
    def __init__(self, links, me, bag, name, shard, parts=None):
        self.links, self.me, self.bag, self.name = links, me, bag, name
        self.along_steps, self.pair_steps, self.placed, self.other_placed = 0, 0, 0, 0
        self.parts = parts or [(slice(0, shard.shape[0]), slice(0, shard.shape[1]))]
        bag[name] = {"z": [shard], "y": [], "whole": None}

    def along(self, steps=1):
        z = self.bag[self.name]["z"]
        for _ in range(steps):
            if self.along_steps < self.links.line - 1:
                z.append(self.links.along(z[self.along_steps]))
                self.along_steps += 1

    def pair(self, steps=1):
        held = self.bag[self.name]
        for _ in range(steps):
            if self.pair_steps <= self.along_steps and self.pair_steps < self.links.line:
                held["y"].append(self.links.to_pair(held["z"][self.pair_steps]))
                self.pair_steps += 1

    def put(self, pieces, at, bit):
        held = self.bag[self.name]
        base = 2 * self.links.behind(self.me, at)
        wholes = []
        for k, (rows, columns) in enumerate(self.parts):
            piece = pieces[at][rows, columns][None]
            whole = jnp.zeros((self.links.dp,) + piece.shape[1:], bf16) if held["whole"] is None else held["whole"][k]
            wholes.append(lax.dynamic_update_slice(whole, piece, (base + bit, 0, 0)))
        held["whole"] = wholes

    def place(self, z=0, y=0):
        held = self.bag[self.name]
        bit = lax.bitwise_and(self.me, 1)
        for _ in range(z):
            if self.placed <= self.along_steps:
                self.put(held["z"], self.placed, bit)
                self.placed += 1
        for _ in range(y):
            if self.other_placed < self.pair_steps:
                self.put(held["y"], self.other_placed, 1 - bit)
                self.other_placed += 1
        for k in range(min(self.placed, self.pair_steps, self.along_steps)):
            held["z"][k] = None
        for k in range(self.other_placed):
            held["y"][k] = None

    def finish(self):
        line = self.links.line
        while self.pair_steps < line:
            self.along()
            self.pair()
        self.place(line, line)
        return self.bag.pop(self.name)["whole"]


class PairGather:
    def __init__(self, links, me, bag, name, shard):
        self.links, self.me, self.bag, self.name = links, me, bag, name
        self.along_steps, self.placed = 0, 0
        bag[name] = {"own": shard, "other": None, "z": [], "whole": None}

    def pair(self):
        held = self.bag[self.name]
        held["other"] = self.links.to_pair(held["own"])

    def join(self):
        held = self.bag[self.name]
        bit = lax.bitwise_and(self.me, 1)
        both = jnp.zeros((2,) + held["own"].shape, bf16)
        both = lax.dynamic_update_slice(both, held["own"][None], (bit, 0, 0))
        held["z"].append(lax.dynamic_update_slice(both, held["other"][None], (1 - bit, 0, 0)))
        held["own"] = held["other"] = None

    def along(self):
        z = self.bag[self.name]["z"]
        if self.along_steps < self.links.line - 1:
            z.append(self.links.along(z[self.along_steps]))
            self.along_steps += 1

    def place(self, steps=1):
        held = self.bag[self.name]
        for _ in range(steps):
            if self.placed <= self.along_steps:
                piece = held["z"][self.placed][None]
                if held["whole"] is None:
                    held["whole"] = jnp.zeros((self.links.line,) + piece.shape[1:], bf16)
                at = self.links.behind(self.me, self.placed)
                held["whole"] = lax.dynamic_update_slice(held["whole"], piece, (at, 0, 0, 0))
                self.placed += 1
        for k in range(min(self.placed, self.along_steps)):
            held["z"][k] = None

    def finish(self):
        while self.along_steps < self.links.line - 1:
            self.along()
        self.place(self.links.line)
        return self.bag.pop(self.name)["whole"]


class Scatter:
    def __init__(self, links, bag, name, sent, kept):
        self.links, self.bag, self.name = links, bag, name
        self.pair_steps, self.along_steps = 0, 0
        self.size = links.line // len(sent)
        bag[name] = {"sent": list(sent), "kept": kept, "moving": None, "ready": None}

    def pair(self):
        sent = self.bag[self.name]["sent"]
        if self.pair_steps < len(sent):
            sent[self.pair_steps] = self.links.to_pair(sent[self.pair_steps])
            self.pair_steps += 1

    def ready(self):
        held = self.bag[self.name]
        at = self.along_steps
        if at < self.links.line - 1 and at // self.size < self.pair_steps and held["ready"] is None:
            held["ready"] = self.sum_here().astype(bf16)

    def along(self):
        held = self.bag[self.name]
        self.ready()
        if held["ready"] is not None:
            held["moving"], held["ready"] = self.links.along(held["ready"]), None
            self.along_steps += 1

    def sum_here(self):
        held = self.bag[self.name]
        at = self.along_steps
        total = held["kept"][at] + held["sent"][at // self.size][at % self.size].astype(f32)
        if held["moving"] is not None:
            total = total + held["moving"].astype(f32)
        return total

    def finish(self, write, *outs):
        while self.pair_steps < len(self.bag[self.name]["sent"]):
            self.pair()
        while self.along_steps < self.links.line - 1:
            self.along()
        held = self.bag.pop(self.name)
        held.pop("ready")
        return last_sum(write, {**held, "size": self.size}, self.along_steps, outs, self.name)


class AllSum:
    def __init__(self, bag, name, value, axes):
        self.bag, self.name = bag, name
        self.steps = [(axis, count, 1 << k) for axis, count in axes for k in range(count.bit_length() - 1)]
        assert all(count & (count - 1) == 0 for _, count in axes)
        bag[name] = value

    def step(self):
        if self.steps:
            axis, count, bit = self.steps.pop(0)
            value = self.bag[self.name]
            self.bag[self.name] = value + lax.ppermute(value, axis, [(i, i ^ bit) for i in range(count)])

    def finish(self):
        while self.steps:
            self.step()
        return self.bag.pop(self.name)


def body(links, block_in, doc_ids, mix_gain, proj_x, proj_y, conv_taps, recur_gate, input_gate, decay_param,
         proj_out, ffn_gain, ffn_gate, ffn_up, ffn_down, out_grad):
    micro_count, own_rows, width = block_in.shape
    group_rows = doc_ids.shape[1]
    assert group_rows == LEN and own_rows * 4 == group_rows and micro_count == 2
    d_rows, channels = proj_x.shape
    blocks = channels // BS
    hidden_units = ffn_gate.shape[1]
    assert hidden_units % UNIT == 0
    gate_columns = recur_gate.shape[2]
    dp_me = lax.axis_index("dp")
    me = lax.axis_index("mp").astype(jnp.int32).reshape(1)
    gain_one = mix_gain.astype(f32)
    gain_two = ffn_gain.astype(f32)
    to_core, to_x = links.to_core, links.to_x
    bag = Bag()

    def exchange(name):
        send, keep = bag.pop(name + "_send"), bag.pop(name + "_keep")
        own_rows_of = lambda v, k: v[k * own_rows:(k + 1) * own_rows].astype(f32)
        sent = to_core(send)
        bag[name + "_own"] = (keep, sent)
        bag[name + "_x"] = (own_rows_of(keep, 1) + own_rows_of(sent, 1)).astype(bf16)

    def summed(name):
        keep, sent = bag.pop(name + "_own")
        return (keep[:own_rows].astype(f32) + sent[:own_rows].astype(f32)) + bag.pop(name + "_x").astype(f32)

    def across(name):
        bag[name + "_x"] = to_x(bag[name + "_x"])

    def rows_of(name):
        own, core, x, diagonal = bag.take(name, name + "_core", name + "_x", name + "_diagonal")
        return core, diagonal, own, x

    packed = pack(proj_x, proj_y, proj_out.T, jnp.swapaxes(recur_gate, 1, 2), jnp.swapaxes(input_gate, 1, 2))
    inner_rows, outer_rows = slice(0, d_rows), slice(d_rows, d_rows + gate_columns)
    wide, narrow = slice(0, 2 * channels), slice(2 * channels, 3 * channels)
    first = Gather(links, dp_me, bag, "first", packed, [(inner_rows, wide), (inner_rows, narrow), (outer_rows, wide)])
    bag.fence()

    bag["cot0"], bag["cot1"] = out_grad[0], out_grad[1]
    first.along()
    first.pair()
    for micro in range(2):
        xin = block_in[micro].astype(f32)
        inverse = lax.rsqrt(jnp.mean(xin * xin, axis=-1, keepdims=True) + norm_eps)
        bag[f"inverse_one{micro}"] = inverse
        bag[f"normed{micro}"] = (xin * inverse * gain_one).astype(bf16)
    bag.fence()

    first.along()
    first.pair()
    bag["normed0_x"] = to_x(bag["normed0"])
    bag["normed0_core"] = to_core(bag["normed0"])
    first.place(2, 1)
    decay_values = decay_param.astype(f32)
    bag["rate"] = jnp.broadcast_to((-decay_scale * jax.nn.softplus(-decay_values))[None], (8, channels))
    bag["slope"] = jnp.broadcast_to((decay_scale * jax.nn.sigmoid(-decay_values))[None], (8, channels))
    bag["taps"] = jnp.concatenate([conv_taps.astype(f32), jnp.zeros((8 - KW, channels), f32)])
    bag["table"] = jnp.stack(
        [links.behind(dp_me, step + 1) for step in range(links.line)] + [lax.bitwise_and(dp_me, 1).astype(jnp.int32)])
    bag.fence()

    first.along()
    first.pair()
    bag["normed1_x"] = to_x(bag["normed1"])
    bag["normed0_diagonal"] = to_core(bag["normed0_x"])
    first.place(1, 1)
    gate_up = jnp.stack([ffn_gate.reshape(d_rows, -1, UNIT), ffn_up.reshape(d_rows, -1, UNIT)], axis=2)
    second = Gather(links, dp_me, bag, "second", gate_up.reshape(d_rows, 2 * hidden_units))
    third = PairGather(links, dp_me, bag, "third", ffn_down.T)
    for micro in range(2):
        bag[f"ids{micro}"] = jnp.broadcast_to(doc_ids[micro][:, None], (group_rows, BS))
    bag.fence()

    first.pair()
    second.along()
    third.pair()
    bag["cot0_x"] = to_x(bag["cot0"])
    first.place(1, 1)
    bag.fence()

    def mix(micro):
        bag[f"normed_all{micro}"], branch = project_rows(rows_of(f"normed{micro}"), bag["w_branch"], 256, "branch", hbm_out)
        branch = branch.reshape(4, own_rows, 2 * channels)
        gated, *rest = mixing_forward(me, branch, bag[f"ids{micro}"], bag["taps"], bag["gates"], bag["rate"])
        bag[f"mixed{micro}"] = [branch] + rest
        bag[f"gated{micro}"] = gated.reshape(group_rows, channels)

    def against_of(name, left, weight):
        bag[name + "_send"], bag[name + "_keep"] = against_rows(bag[left], bag[weight], weight + "_turned")

    def middle_of(micro):
        middle = block_in[micro].astype(f32) + summed(f"first{micro}")
        inverse = lax.rsqrt(jnp.mean(middle * middle, axis=-1, keepdims=True) + norm_eps)
        bag[f"middle{micro}"], bag[f"inverse_two{micro}"] = middle, inverse
        bag[f"two{micro}"] = (middle * inverse * gain_two).astype(bf16)

    second.along()
    second.pair()
    third.join()
    bag["cot1_x"] = to_x(bag["cot1"])
    w_branch, w_out, gates = first.finish()
    bag["w_branch"] = w_branch.reshape(width, 2 * channels)
    bag["gates"] = gates.reshape(BS, 2 * channels)
    bag["w_out"] = w_out.reshape(width, channels)
    mix(0)
    against_of("first0", "gated0", "w_out")
    bag.fence()

    bag["normed1_core"] = to_core(bag["normed1"])
    bag["normed1_diagonal"] = to_core(bag["normed1_x"])
    exchange("first0")
    second.place(1)
    bag.fence()

    second.along()
    second.pair()
    across("first0")
    second.place(1)
    mix(1)
    bag.fence()

    bag["cot0_core"] = to_core(bag["cot0"])
    bag["cot0_diagonal"] = to_core(bag["cot0_x"])
    middle_of(0)
    against_of("first1", "gated1", "w_out")
    bag.fence()

    third.along()
    second.pair()
    bag["two0_x"] = to_x(bag["two0"])
    bag["two0_core"] = to_core(bag["two0"])
    exchange("first1")
    bag["cot_all0"] = jnp.concatenate(rows_of("cot0"))
    second.place(3, 2)
    third.place()
    bag.fence()

    def forward(micro):
        bag[f"two_all{micro}"], bag[f"hidden{micro}"], *bag[f"by{micro}"] = ffn_forward(
            rows_of(f"two{micro}"), bag["w_up"])

    third.along()
    second.pair()
    across("first1")
    bag["two0_diagonal"] = to_core(bag["two0_x"])
    bag["cot1_core"] = to_core(bag["cot1"])
    bag["cot1_diagonal"] = to_core(bag["cot1_x"])
    bag["cot_all1"] = jnp.concatenate(rows_of("cot1"))
    second.place(0, 1)
    third.place()
    bag.fence()

    middle_of(1)
    bag.fence()

    third.along()
    bag["two1_x"] = to_x(bag["two1"])
    bag["w_up"] = second.finish()[0].reshape(width, 2 * hidden_units)
    third.place()
    forward(0)
    bag.fence()

    def back(micro):
        name = f"second{micro}"
        bag[f"grad_pre{micro}"], bag[name + "_send"], bag[name + "_keep"] = ffn_backward(
            bag[f"cot_all{micro}"], bag["w_down"], *bag.pop(f"by{micro}"), bag["w_up"])

    def grad_middle_of(micro):
        grad = summed(f"second{micro}")
        inverse, middle = bag[f"inverse_two{micro}"], bag[f"middle{micro}"]
        unit = middle * inverse
        total = out_grad[micro].astype(f32) + norm_back(grad, unit, inverse, gain_two)
        bag[f"grad_middle{micro}"] = total
        bag[f"gain_two{micro}"] = jnp.sum(grad * unit, axis=0)
        bag[f"low{micro}"] = total.astype(bf16)

    bag["two1_core"] = to_core(bag["two1"])
    bag["two1_diagonal"] = to_core(bag["two1_x"])
    bag["w_down"] = third.finish().reshape(width, hidden_units)
    back(0)
    bag.fence()

    exchange("second0")
    forward(1)
    bag.fence()

    across("second0")
    down_grad = Scatter(links, bag, "down_grad", *weight_grad(
        bag["table"], [bag["cot_all0"], bag["cot_all1"]], [bag["hidden0"], bag["hidden1"]], hidden_units, 2))
    bag.fence()

    down_grad.pair()
    back(1)
    bag.fence()

    exchange("second1")
    down_grad.ready()
    grad_middle_of(0)
    bag.fence()

    across("second1")
    down_grad.pair()
    bag["low0_core"] = to_core(bag["low0"])
    up_grad = Scatter(links, bag, "up_grad", *weight_grad(
        bag["table"], bag.take("two_all0", "two_all1"), bag.take("grad_pre0", "grad_pre1"), 2 * UNIT, 4))
    bag.fence()

    def output_of(micro):
        bag[f"output{micro}"] = (bag[f"middle{micro}"] + summed(f"down{micro}")).astype(bf16)

    bag["low0_x"] = to_x(bag["low0"])
    up_grad.pair()
    down_grad.along()
    grad_middle_of(1)
    against_of("down0", "hidden0", "w_down")
    against_of("down1", "hidden1", "w_down")
    bag.fence()

    def into_mix(micro):
        bag[f"low_all{micro}"], bag[f"grad_gated{micro}"] = project_rows(
            rows_of(f"low{micro}"), bag["w_out"], 256, "grad_gated")

    def mix_back(micro):
        grad, bag[f"gates_grad{micro}"], bag[f"small{micro}"] = mixing_backward(
            me, bag.pop(f"grad_gated{micro}").reshape(4, own_rows, channels), *bag.pop(f"mixed{micro}"),
            bag[f"ids{micro}"], bag["taps"], bag["gates"], bag["rate"], bag["slope"])
        bag[f"grad_branch{micro}"] = grad.reshape(group_rows, 2 * channels)
        against_of(f"third{micro}", f"grad_branch{micro}", "w_branch")

    bag["low1_x"] = to_x(bag["low1"])
    bag["low0_diagonal"] = to_core(bag["low0_x"])
    up_grad.pair()
    up_grad.along()
    down_grad.ready()
    exchange("down0")
    into_mix(0)
    mix_back(0)
    bag.fence()

    across("down0")
    bag["low1_core"] = to_core(bag["low1"])
    bag["low1_diagonal"] = to_core(bag["low1_x"])
    exchange("third0")
    up_grad.pair()
    down_grad.along()
    up_grad.ready()
    into_mix(1)
    out_grad_w = Scatter(links, bag, "out_grad", *weight_grad(
        bag["table"], bag.take("low_all0", "low_all1"), bag.take("gated0", "gated1"), 512, 1))
    bag.fence()

    across("third0")
    up_grad.pair()
    up_grad.along()
    down_grad.ready()
    mix_back(1)
    bag.fence()

    exchange("third1")
    bag.fence()

    def leave(micro):
        grad = summed(f"third{micro}")
        inverse = bag[f"inverse_one{micro}"]
        unit = block_in[micro].astype(f32) * inverse
        bag[f"input_grad{micro}"] = bag[f"grad_middle{micro}"] + norm_back(grad, unit, inverse, gain_one)
        bag[f"gain_one{micro}"] = jnp.sum(grad * unit, axis=0)

    across("third1")
    out_grad_w.pair()
    up_grad.along()
    gates_grads = [bag.pop(f"gates_grad{micro}").reshape(2, links.dp, gate_columns, channels) for micro in range(2)]
    first_grad = Scatter(links, bag, "first_grad", *weight_grad(
        bag["table"], bag.take("normed_all0", "normed_all1"), bag.take("grad_branch0", "grad_branch1"), channels, 4,
        gates_grads))
    bag.fence()

    first_grad.pair()
    down_grad.along()
    leave(1)
    leave(0)
    gains = jnp.stack([bag.pop("gain_one0") + bag.pop("gain_one1"), bag.pop("gain_two0") + bag.pop("gain_two1")])
    bag["sums"] = gains.reshape(-1, 128)
    gain_rows = bag["sums"].shape[0]
    bag.fence()

    first_grad.pair()
    first_grad.along()
    out_grad_w.along()
    sums = AllSum(bag, "gains", bag.pop("sums"), [("mp", links.mp)])
    small = (bag.pop("small0") + bag.pop("small1")).reshape(-1, 128)
    sums = AllSum(bag, "sums", jnp.concatenate([sums.finish(), small]), [("dp", links.dp)])
    exchange("down1")
    output_of(0)
    bag["up_total"] = up_grad.finish(write_gate_up, (d_rows, hidden_units), (d_rows, hidden_units))
    bag.fence()

    first_grad.pair()
    first_grad.along()
    out_grad_w.along()
    sums.step()
    bag["down1_xa"] = to_x(bag["down1_x"][:own_rows // 2])
    bag["down_total"] = down_grad.finish(write_plain, (d_rows, hidden_units))
    bag.fence()

    first_grad.pair()
    first_grad.along()
    out_grad_w.along()
    sums.step()
    bag["down1_xb"] = to_x(bag["down1_x"][own_rows // 2:])
    bag["input_grads"] = jnp.stack([bag.pop("input_grad0"), bag.pop("input_grad1")])
    bag.fence()

    bag["down1_x"] = jnp.concatenate(bag.take("down1_xa", "down1_xb"))
    output_of(1)
    bag["outputs"] = jnp.stack(bag.take("output0", "output1"))
    bag["out_total"] = out_grad_w.finish(write_plain, (d_rows, channels))
    x_grad, y_grad, recur, inp = first_grad.finish(
        write_first, (d_rows, channels), (d_rows, channels), (blocks, gate_columns, BS), (blocks, gate_columns, BS))
    sums = sums.finish()
    gains = sums[:gain_rows].reshape(2, width)
    small = sums[gain_rows:].reshape(8, channels)
    return (
        bag["outputs"],
        bag["input_grads"],
        gains[0],
        x_grad,
        y_grad,
        small[0:KW],
        jnp.swapaxes(recur, 1, 2),
        jnp.swapaxes(inp, 1, 2),
        small[KW],
        bag["out_total"][0].T,
        gains[1],
        *bag["up_total"],
        bag["down_total"][0].T,
    )


def solution(mesh):
    links = Links(mesh.shape["dp"], mesh.shape["mp"])
    tokens = P(None, ("dp", "mp"), None)
    rows, columns, gate = P("dp", "mp"), P("mp", "dp"), P("mp", None, "dp")
    return jax.shard_map(
        functools.partial(body, links),
        mesh=mesh,
        in_specs=(tokens, P(None, "dp"), P(), rows, rows, P(None, "mp"), gate, gate, P("mp"), columns, P(), rows,
                  rows, columns, tokens),
        out_specs=(tokens, tokens, P(), rows, rows, P(None, "mp"), gate, gate, P("mp"), columns, P(), rows, rows,
                   columns),
        check_vma=False,
    )
```

```python
import functools

import jax
import jax.numpy as jnp
import numpy as np
from jax import lax
from jax.experimental import pallas as pl
from jax.experimental.pallas import tpu as pltpu
from jax.sharding import PartitionSpec as P

LEN = 1024
BS = 128
KW = 4

norm_eps = 1e-06
root_floor = 0.01
decay_scale = 8.0
gelu_a = 0.7978845608028654
gelu_b = 0.044715

f32 = jnp.float32
bf16 = jnp.bfloat16


BLOCK_AT = (2, 0, 3, 1)


def project(left, right):
    return jnp.dot(left, right, preferred_element_type=f32)


def inner(left, right):
    return lax.dot_general(left, right, (((0,), (0,)), ((), ())), preferred_element_type=f32)


def against(left, right):
    return lax.dot_general(left, right, (((1,), (1,)), ((), ())), preferred_element_type=f32)


def norm_back(grad_normed, unit_rows, inverse, gain):
    scaled = grad_normed * gain
    return inverse * (scaled - unit_rows * jnp.mean(scaled * unit_rows, axis=-1, keepdims=True))


def gelu_parts(v):
    squared = v * v
    inside = gelu_a * v * (1.0 + gelu_b * squared)
    t = jnp.tanh(inside)
    half = 0.5 * (1.0 + t)
    value = v * half
    slope = half + 0.5 * v * (1.0 - t * t) * (gelu_a * (1.0 + 3.0 * gelu_b * squared))
    return value, slope


def gelu_value(v):
    return 0.5 * v * (1.0 + jnp.tanh(gelu_a * v * (1.0 + gelu_b * v * v)))


def place_of(me, block):
    differ = lax.bitwise_xor(me, block)
    low = lax.bitwise_and(differ, 1)
    high = lax.shift_right_logical(differ, 1)
    return 2 * (1 - low) + high


CHUNK = 64
STEP = 64


def tile_scan(a, b, row):
    for d in (1, 2, 4):
        use = row >= d
        b = b + a * jnp.where(use, pltpu.roll(b, d, 0), 0.0)
        a = a * jnp.where(use, pltpu.roll(a, d, 0), 1.0)
    return a, b


def tile_scan_back(a, b, row):
    for d in (1, 2, 4):
        use = row < 8 - d
        b = b + a * jnp.where(use, pltpu.roll(b, 8 - d, 0), 0.0)
        a = a * jnp.where(use, pltpu.roll(a, 8 - d, 0), 1.0)
    return a, b


def spread(row):
    return jnp.broadcast_to(row, (8, BS))


def mixing_forward_kernel(me_ref, branch, ids, taps, gate_r, gate_i, rate, gated, states, conv, sig_r, sig_i,
                          xpad, idpad, logits, gates):
    gates[0:BS, :] = gate_r[...]
    gates[BS:2 * BS, :] = gate_i[...]
    rows = LEN
    quarter = rows // 4
    me = me_ref[0]
    xpad[0:8, :] = jnp.zeros((8, BS), f32)
    idpad[0:8, :] = jnp.full((8, BS), -1, jnp.int32)
    idpad[8:8 + rows, :] = ids[...]
    for block in range(4):
        at = place_of(me, block)
        xpad[8 + block * quarter: 8 + (block + 1) * quarter, :] = branch[at, :, 0:BS]
    rate_row = rate[0:1, :]

    def convolve(step, _):
        base = pl.multiple_of(step * CHUNK, CHUNK)
        own_ids = idpad[pl.ds(base + 8, CHUNK), :]
        total = taps[0:1, :] * xpad[pl.ds(base + 8, CHUNK), :]
        for k in range(1, KW):
            same = idpad[pl.ds(base + 8 - k, CHUNK), :] == own_ids
            total = total + taps[k:k + 1, :] * jnp.where(same, xpad[pl.ds(base + 8 - k, CHUNK), :], 0.0)
        conv[pl.ds(base, CHUNK), :] = total.astype(bf16)
        return 0

    lax.fori_loop(0, rows // CHUNK, convolve, 0, unroll=2)
    logits[...] = lax.dot_general(conv[...], gates[...], (((1,), (1,)), ((), ())), preferred_element_type=f32)
    row = lax.broadcasted_iota(jnp.int32, (8, BS), 0)

    def advance(step, carry):
        base = pl.multiple_of(step * STEP, STEP)
        here = pl.ds(base, STEP)
        block = lax.div(step, quarter // STEP)
        at = place_of(me, block)
        there = pl.ds(pl.multiple_of(base - block * quarter, STEP), STEP)
        sr = jax.nn.sigmoid(logits[here, 0:BS])
        si = jax.nn.sigmoid(logits[here, BS:2 * BS])
        sig_r[here, :] = sr
        sig_i[here, :] = si
        same = idpad[pl.ds(base + 7, STEP), :] == idpad[pl.ds(base + 8, STEP), :]
        a = jnp.where(same, jnp.exp(rate_row * sr), 0.0)
        margin = jnp.maximum(1.0 - a * a, root_floor)
        b = conv[here, :].astype(f32) * si * (margin * lax.rsqrt(margin))
        tiles = []
        for k in range(STEP // 8):
            part = slice(8 * k, 8 * k + 8)
            product, local = tile_scan(a[part], b[part], row)
            tiles.append(local + product * carry)
            carry = spread(local[7:8]) + spread(product[7:8]) * carry
        state = jnp.concatenate(tiles, axis=0)
        states[here, :] = state
        gated[at, there, :] = (state * gelu_value(branch[at, there, BS:2 * BS])).astype(bf16)
        return carry

    lax.fori_loop(0, rows // STEP, advance, jnp.zeros((8, BS), f32), unroll=2)


def mixing_backward_kernel(me_ref, grad_gated, branch, states, conv, sig_r, sig_i, ids, taps, gate_r, gate_i, rate,
                           slope, grad_branch, grad_gates, small,
                           xpad, idpad, spad, low, gcpad, through, gates):
    gates[0:BS, :] = gate_r[...]
    gates[BS:2 * BS, :] = gate_i[...]
    rows = LEN
    quarter = rows // 4
    me = me_ref[0]
    zero8 = jnp.zeros((8, BS), f32)
    xpad[0:8, :] = zero8
    spad[0:8, :] = zero8
    spad[8:8 + rows, :] = states[...]
    idpad[0:8, :] = jnp.full((8, BS), -1, jnp.int32)
    idpad[8:8 + rows, :] = ids[...]
    idpad[8 + rows:16 + rows, :] = jnp.full((8, BS), -1, jnp.int32)
    gcpad[rows:rows + 8, :] = zero8
    rate_row = rate[0:1, :]
    slope_row = slope[0:1, :]
    for block in range(4):
        at = place_of(me, block)
        xpad[8 + block * quarter: 8 + (block + 1) * quarter, :] = branch[at, :, 0:BS]
    row = lax.broadcasted_iota(jnp.int32, (8, BS), 0)
    fold = lambda v: jnp.sum(v.reshape(v.shape[0] // 8, 8, BS), axis=0)
    steps = rows // STEP

    def retreat(count, held):
        carry, decay_sum = held
        step = steps - 1 - count
        base = pl.multiple_of(step * STEP, STEP)
        here = pl.ds(base, STEP)
        block = lax.div(step, quarter // STEP)
        at = place_of(me, block)
        there = pl.ds(pl.multiple_of(base - block * quarter, STEP), STEP)
        value, gradient = gelu_parts(branch[at, there, BS:2 * BS])
        incoming = grad_gated[at, there, :]
        grad_states = incoming * value
        grad_branch[at, there, BS:2 * BS] = (gradient * states[here, :] * incoming).astype(bf16)
        same = idpad[pl.ds(base + 7, STEP), :] == idpad[pl.ds(base + 8, STEP), :]
        sr = sig_r[here, :]
        si = sig_i[here, :]
        a = jnp.where(same, jnp.exp(rate_row * sr), 0.0)
        pushed = a * grad_states
        us, gs = [], []
        for k in reversed(range(STEP // 8)):
            part = slice(8 * k, 8 * k + 8)
            product, local = tile_scan_back(a[part], pushed[part], row)
            u = local + product * carry
            us.insert(0, u)
            gs.insert(0, grad_states[part] + jnp.where(row == 7, carry, pltpu.roll(u, 7, 0)))
            carry = spread(local[0:1]) + spread(product[0:1]) * carry
        u = jnp.concatenate(us, axis=0)
        g = jnp.concatenate(gs, axis=0)
        square = a * a
        inside = 1.0 - square
        margin = jnp.maximum(inside, root_floor)
        inverse = lax.rsqrt(margin)
        multiplier = margin * inverse
        gsi = g * si
        gcsi = gsi * conv[here, :].astype(f32)
        grad_log = u * spad[pl.ds(base + 7, STEP), :] - jnp.where(inside > root_floor, gcsi * square * inverse, 0.0)
        gcpad[here, :] = gsi * multiplier
        weighted = grad_log * sr
        low[here, 0:BS] = (weighted * (1.0 - sr) * rate_row).astype(bf16)
        low[here, BS:2 * BS] = (gcsi * multiplier * (1.0 - si)).astype(bf16)
        return carry, decay_sum + fold(weighted)

    _, decay_sum = lax.fori_loop(0, steps, retreat, (zero8, zero8), unroll=2)

    both_gates = lax.dot_general(low[...], conv[...], (((0,), (0,)), ((), ())), preferred_element_type=f32)
    grad_gates[0] = both_gates[0:BS]
    grad_gates[1] = both_gates[BS:2 * BS]
    through[...] = lax.dot_general(low[...], gates[...], (((1,), (0,)), ((), ())), preferred_element_type=f32)

    def add_gates(step, _):
        here = pl.ds(pl.multiple_of(step * CHUNK, CHUNK), CHUNK)
        gcpad[here, :] = gcpad[here, :] + through[here, :]
        return 0

    lax.fori_loop(0, rows // CHUNK, add_gates, 0, unroll=4)

    def finish(step, sums):
        base = pl.multiple_of(step * CHUNK, CHUNK)
        block = lax.div(step, quarter // CHUNK)
        at = place_of(me, block)
        there = pl.ds(pl.multiple_of(base - block * quarter, CHUNK), CHUNK)
        gc = gcpad[pl.ds(base, CHUNK), :]
        own_ids = idpad[pl.ds(base + 8, CHUNK), :]
        new = [sums[0] + fold(gc * xpad[pl.ds(base + 8, CHUNK), :])]
        grad_x = taps[0:1, :] * gc
        for k in range(1, KW):
            same = idpad[pl.ds(base + 8 - k, CHUNK), :] == own_ids
            new.append(sums[k] + fold(jnp.where(same, gc * xpad[pl.ds(base + 8 - k, CHUNK), :], 0.0)))
            after = idpad[pl.ds(base + 8 + k, CHUNK), :] == own_ids
            grad_x = grad_x + taps[k:k + 1, :] * jnp.where(after, gcpad[pl.ds(base + k, CHUNK), :], 0.0)
        grad_branch[at, there, 0:BS] = grad_x.astype(bf16)
        return tuple(new)

    sums = lax.fori_loop(0, rows // CHUNK, finish, (zero8,) * KW, unroll=2)
    small[...] = jnp.zeros((8, BS), f32)
    for k in range(KW):
        small[k:k + 1, :] = jnp.sum(sums[k], axis=0, keepdims=True)
    small[KW:KW + 1, :] = jnp.sum(decay_sum, axis=0, keepdims=True) * slope_row


def mixing_forward(me, branch, ids, taps, gates, rate):
    rows = LEN
    blocks = branch.shape[2] // (2 * BS)
    channels = blocks * BS
    flat = lambda n, me: (0, n)
    return pl.pallas_call(
        mixing_forward_kernel,
        grid_spec=pltpu.PrefetchScalarGridSpec(
            num_scalar_prefetch=1,
            grid=(blocks,),
            in_specs=[
                pl.BlockSpec((4, rows // 4, 2 * BS), lambda n, me: (0, 0, n)),
                pl.BlockSpec((rows, BS), lambda n, me: (0, 0)),
                pl.BlockSpec((8, BS), flat),
                pl.BlockSpec((BS, BS), flat),
                pl.BlockSpec((BS, BS), lambda n, me: (0, blocks + n)),
                pl.BlockSpec((8, BS), flat),
            ],
            out_specs=[
                pl.BlockSpec((4, rows // 4, BS), lambda n, me: (0, 0, n)),
                pl.BlockSpec((rows, BS), flat),
                pl.BlockSpec((rows, BS), flat),
                pl.BlockSpec((rows, BS), flat),
                pl.BlockSpec((rows, BS), flat),
            ],
            scratch_shapes=[
                pltpu.VMEM((rows + 8, BS), f32),
                pltpu.VMEM((rows + 8, BS), jnp.int32),
                pltpu.VMEM((rows, 2 * BS), f32),
                pltpu.VMEM((2 * BS, BS), bf16),
            ],
        ),
        out_shape=[
            jax.ShapeDtypeStruct((4, rows // 4, channels), bf16),
            hbm_out((rows, channels), f32),
            hbm_out((rows, channels), bf16),
            hbm_out((rows, channels), f32),
            hbm_out((rows, channels), f32),
        ],
        compiler_params=vmem(16),
        name="mixing_forward",
    )(me, in_hbm(branch), ids, taps, gates, gates, rate)


def mixing_backward(me, grad_gated, branch, states, conv, sig_r, sig_i, ids, taps, gates, rate, slope):
    rows = LEN
    blocks = branch.shape[2] // (2 * BS)
    channels = blocks * BS
    flat = lambda n, me: (0, n)
    cube = lambda n, me: (0, 0, n)
    return pl.pallas_call(
        mixing_backward_kernel,
        grid_spec=pltpu.PrefetchScalarGridSpec(
            num_scalar_prefetch=1,
            grid=(blocks,),
            in_specs=[
                pl.BlockSpec((4, rows // 4, BS), cube),
                pl.BlockSpec((4, rows // 4, 2 * BS), cube),
                pl.BlockSpec((rows, BS), flat),
                pl.BlockSpec((rows, BS), flat),
                pl.BlockSpec((rows, BS), flat),
                pl.BlockSpec((rows, BS), flat),
                pl.BlockSpec((rows, BS), lambda n, me: (0, 0)),
                pl.BlockSpec((8, BS), flat),
                pl.BlockSpec((BS, BS), flat),
                pl.BlockSpec((BS, BS), lambda n, me: (0, blocks + n)),
                pl.BlockSpec((8, BS), flat),
                pl.BlockSpec((8, BS), flat),
            ],
            out_specs=[
                pl.BlockSpec((4, rows // 4, 2 * BS), cube),
                pl.BlockSpec((2, BS, BS), cube),
                pl.BlockSpec((8, BS), flat),
            ],
            scratch_shapes=[
                pltpu.VMEM((rows + 8, BS), f32),
                pltpu.VMEM((rows + 16, BS), jnp.int32),
                pltpu.VMEM((rows + 8, BS), f32),
                pltpu.VMEM((rows, 2 * BS), bf16),
                pltpu.VMEM((rows + 8, BS), f32),
                pltpu.VMEM((rows, BS), f32),
                pltpu.VMEM((2 * BS, BS), bf16),
            ],
        ),
        out_shape=[
            jax.ShapeDtypeStruct((4, rows // 4, 2 * channels), bf16),
            jax.ShapeDtypeStruct((2, BS, channels), f32),
            jax.ShapeDtypeStruct((8, channels), f32),
        ],
        compiler_params=vmem(24),
        name="mixing_backward",
    )(me, grad_gated, *(in_hbm(v) for v in (branch, states, conv, sig_r, sig_i)), ids, taps, gates, gates, rate, slope)


def folded(count):
    return list(range(0, 1)) + list(range(1, count, 2)) + list(range((count - 1) // 2 * 2, 0, -2))


class Links:
    def __init__(self, dp, mp):
        assert mp == 4 and dp % 2 == 0
        self.dp, self.mp = dp, mp
        self.line = dp // 2
        self.order = folded(self.line)
        self.place = {a: k for k, a in enumerate(self.order)}
        self.ring = [
            (2 * a + b, 2 * self.order[(self.place[a] + 1) % self.line] + b)
            for a in range(self.line)
            for b in range(2)
        ]

    def to_core(self, v):
        return lax.ppermute(v, "mp", [(i, i ^ 1) for i in range(self.mp)])

    def to_x(self, v):
        return lax.ppermute(v, "mp", [(i, i ^ 2) for i in range(self.mp)])

    def to_pair(self, v):
        return lax.ppermute(v, "dp", [(i, i ^ 1) for i in range(self.dp)])

    def along(self, v):
        return lax.ppermute(v, "dp", self.ring)

    def behind(self, me, steps):
        at = lax.shift_right_logical(me, 1)
        place = jnp.int32(0)
        for a in range(self.line):
            place = jnp.where(at == a, self.order[(self.place[a] - steps) % self.line], place)
        return place.astype(jnp.int32)


def in_hbm(v):
    return pltpu.with_memory_space_constraint(v, pltpu.HBM)


def hbm_out(shape, dtype):
    return pltpu.HBM(shape, dtype)


def vmem(mib):
    return pltpu.CompilerParams(vmem_limit_bytes=mib * 1024 * 1024)


UNIT = 384


def assemble(pieces, whole):
    @pl.when(pl.program_id(0) == 0)
    def _():
        rows = pieces[0].shape[0]
        for k, piece in enumerate(pieces):
            whole[k * rows:(k + 1) * rows, :] = piece[...]


def rows_call(kernel, pieces, more, more_specs, outs, out_specs, grid, name, mib, scratch=(), streamed=False):
    own, width = pieces[0].shape
    count = len(pieces)
    whole = pl.BlockSpec((count * own, width), lambda n: (0, 0))
    joined = count > 1

    def run(*refs):
        x, others = refs[0], refs[count:]
        if joined:
            x = refs[count + len(more)]
            assemble(refs[:count], x)
            others = refs[count:count + len(more)] + refs[count + len(more) + 1:]
        kernel(x, *others)

    if streamed:
        pieces, more = [in_hbm(v) for v in pieces], [in_hbm(v) for v in more]
        outs = [hbm_out(v.shape, v.dtype) for v in outs]
    return pl.pallas_call(
        run,
        grid=(grid,),
        in_specs=[pl.BlockSpec((own, width), lambda n: (0, 0))] * count + more_specs,
        out_specs=[whole] * joined + out_specs,
        out_shape=[jax.ShapeDtypeStruct((count * own, width), bf16)] * joined + outs,
        scratch_shapes=list(scratch),
        compiler_params=vmem(mib),
        name=name,
    )(*pieces, *more)


def against_kernel(x, w, send, keep):
    half = send.shape[0]
    result = lax.dot_general(x[...], w[...], (((1,), (1,)), ((), ())), preferred_element_type=f32).astype(bf16)
    send[...] = result[:half]
    keep[...] = result[half:]


def against_rows(x, w, name):
    rows, depth = x.shape
    width = w.shape[0]
    tile = 256
    half = pl.BlockSpec((rows // 2, tile), lambda n: (0, n))
    return rows_call(
        against_kernel, [x], [w], [pl.BlockSpec((tile, depth), lambda n: (n, 0))],
        [jax.ShapeDtypeStruct((rows // 2, width), bf16)] * 2, [half] * 2, width // tile,
        name, 20)


def project_kernel(x, w, out):
    out[...] = jnp.dot(x[...], w[...], preferred_element_type=f32)


def project_rows(pieces, w, tile, name, out=jax.ShapeDtypeStruct):
    own, width = pieces[0].shape
    columns = w.shape[1]
    return rows_call(
        project_kernel, pieces, [w], [pl.BlockSpec((width, tile), lambda n: (0, n))],
        [out((4 * own, columns), f32)], [pl.BlockSpec((4 * own, tile), lambda n: (0, n))],
        columns // tile, name, 24)


def ffn_forward_kernel(x, w, hidden, by_gate, by_up):
    both = jnp.dot(x[...], w[...], preferred_element_type=f32)
    up = both[:, UNIT:]
    value, slope = gelu_parts(both[:, :UNIT])
    hidden[...] = (value * up).astype(bf16)
    by_gate[...] = (up * slope).astype(bf16)
    by_up[...] = value.astype(bf16)


def ffn_forward(pieces, w):
    own, width = pieces[0].shape
    units = w.shape[1] // 2
    tile = pl.BlockSpec((4 * own, UNIT), lambda n: (0, n))
    return rows_call(
        ffn_forward_kernel, pieces, [w], [pl.BlockSpec((width, 2 * UNIT), lambda n: (0, n))],
        [jax.ShapeDtypeStruct((4 * own, units), bf16)] * 3, [tile] * 3,
        units // UNIT, "ffn_forward", 34, streamed=True)


def ffn_backward_kernel(tiles, x, w, by_gate, by_up, w_up, out, send, keep, whole):
    at = pl.program_id(0)

    @pl.when(at < tiles)
    def _():
        grad = jnp.dot(x[...], w[...], preferred_element_type=f32)
        out[:, :UNIT] = (grad * by_gate[...].astype(f32)).astype(bf16)
        out[:, UNIT:] = (grad * by_up[...].astype(f32)).astype(bf16)
        whole[at] = out[...]

    @pl.when(at >= tiles)
    def _():
        half = send.shape[0]
        result = sum(
            lax.dot_general(whole[k], w_up[:, 2 * k * UNIT:2 * (k + 1) * UNIT], (((1,), (1,)), ((), ())),
                            preferred_element_type=f32)
            for k in range(tiles))
        result = result.astype(bf16)
        send[...] = result[:half]
        keep[...] = result[half:]


def ffn_backward(x, w, by_gate, by_up, w_up):
    rows, width = x.shape
    units = w.shape[1]
    tiles = units // UNIT
    tile = 256
    first = lambda n: jnp.minimum(n, tiles - 1)
    then = lambda n: jnp.maximum(n - tiles, 0)
    half = pl.BlockSpec((rows // 2, tile), lambda n: (0, then(n)))
    return rows_call(
        functools.partial(ffn_backward_kernel, tiles), [x], [w, by_gate, by_up, w_up],
        [pl.BlockSpec((width, UNIT), lambda n: (0, first(n))), pl.BlockSpec((rows, UNIT), lambda n: (0, first(n))),
         pl.BlockSpec((rows, UNIT), lambda n: (0, first(n))),
         pl.BlockSpec((tile, 2 * units), lambda n: (then(n), 0))],
        [jax.ShapeDtypeStruct((rows, 2 * units), bf16)] + [jax.ShapeDtypeStruct((rows // 2, width), bf16)] * 2,
        [pl.BlockSpec((rows, 2 * UNIT), lambda n: (0, first(n))), half, half],
        tiles + width // tile, "ffn_backward", 46, [pltpu.VMEM((tiles, rows, 2 * UNIT), bf16)], streamed=True)


def pack_kernel(x, y, out, recur, inp, packed):
    rows, channels = x.shape
    columns = recur.shape[1]
    for n in range(channels // BS):
        block = slice(n * BS, (n + 1) * BS)
        packed[0:rows, 2 * n * BS:(2 * n + 1) * BS] = x[:, block]
        packed[0:rows, (2 * n + 1) * BS:(2 * n + 2) * BS] = y[:, block]
        packed[rows:rows + columns, block] = recur[n]
        packed[rows:rows + columns, channels + n * BS:channels + (n + 1) * BS] = inp[n]
    packed[0:rows, 2 * channels:3 * channels] = out[...]
    packed[rows:rows + columns, 2 * channels:3 * channels] = jnp.zeros((columns, channels), bf16)


def pack(x, y, out, recur, inp):
    rows, channels = x.shape
    return pl.pallas_call(
        pack_kernel,
        out_shape=jax.ShapeDtypeStruct((rows + recur.shape[1], 3 * channels), bf16),
        name="pack",
    )(x, y, out, recur, inp)


def weight_grad_kernel(line, shard, extra, groups, table, *refs):
    if extra:
        left_a, right_a, left_b, right_b, extra_a, extra_b, *sent, kept, total = refs
    else:
        left_a, right_a, left_b, right_b, *sent, kept, total = refs
    dims = (((0,), (0,)), ((), ()))
    total[...] = lax.dot_general(
        left_a[...], right_a[...], dims, preferred_element_type=f32
    ) + lax.dot_general(left_b[...], right_b[...], dims, preferred_element_type=f32)
    bit = table[line]
    size = line // groups
    for k in range(line):
        at = 2 * table[k]
        out = sent[k // size]
        mine = pl.ds(pl.multiple_of((at + bit) * shard, 16), shard)
        other = pl.ds(pl.multiple_of((at + 1 - bit) * shard, 16), shard)
        kept[k, 0:shard, :] = total[mine, :]
        out[k % size, 0:shard, :] = total[other, :].astype(bf16)
        if extra:
            kept[k, shard:shard + extra, :] = extra_a[0, at + bit] + extra_b[0, at + bit]
            out[k % size, shard:shard + extra, :] = (
                extra_a[0, at + 1 - bit] + extra_b[0, at + 1 - bit]).astype(bf16)


def weight_grad(table, left, right, tile, groups, extras=None):
    line = table.shape[0] - 1
    rows, width = left[0].shape
    columns = right[0].shape[1]
    shard = width // (2 * line)
    extra = extras[0].shape[2] if extras else 0
    lefts = pl.BlockSpec((rows, width), lambda n, t: (0, 0))
    rights = pl.BlockSpec((rows, tile), lambda n, t: (0, n))
    more = [pl.BlockSpec((1, 2 * line, extra, tile), lambda n, t: (n, 0, 0, 0))] * 2 if extra else []
    parts = lambda count: pl.BlockSpec((count, shard + extra, tile), lambda n, t: (0, 0, n))
    size = line // groups
    *sent, kept = pl.pallas_call(
        functools.partial(weight_grad_kernel, line, shard, extra, groups),
        grid_spec=pltpu.PrefetchScalarGridSpec(
            num_scalar_prefetch=1,
            grid=(columns // tile,),
            in_specs=[lefts, rights, lefts, rights] + more,
            out_specs=[parts(size)] * groups + [parts(line)],
            scratch_shapes=[pltpu.VMEM((width, tile), f32)],
        ),
        out_shape=[jax.ShapeDtypeStruct((size, shard + extra, columns), bf16)] * groups
        + [jax.ShapeDtypeStruct((line, shard + extra, columns), f32)],
        compiler_params=vmem(52 if tile > 1024 else 44),
        name="weight_grad",
    )(table, in_hbm(left[0]), in_hbm(right[0]), in_hbm(left[1]), in_hbm(right[1]), *(extras or ()))
    return sent, kept


def last_sum(write, held, at, outs, name):
    kept, sent, moving = held["kept"], held["sent"][at // held["size"]], held["moving"]
    shape = (1,) + kept.shape[1:]
    inside = at % held["size"]

    def kernel(kept, sent, moving, *outs):
        write(kept[0] + sent[0].astype(f32) + moving[...].astype(f32), *outs)

    return pl.pallas_call(
        kernel,
        grid=(1,),
        in_specs=[pl.BlockSpec(shape, lambda n: (at, 0, 0)), pl.BlockSpec(shape, lambda n: (inside, 0, 0)),
                  pl.BlockSpec(shape[1:], lambda n: (0, 0))],
        out_specs=[pl.BlockSpec(out, lambda n, rank=len(out): (0,) * rank) for out in outs],
        out_shape=[jax.ShapeDtypeStruct(out, f32) for out in outs],
        compiler_params=vmem(16),
        name=name,
    )(in_hbm(kept), sent, moving)


def write_plain(total, out):
    out[...] = total


def write_gate_up(total, gate, up):
    for k in range(gate.shape[1] // UNIT):
        gate[:, k * UNIT:(k + 1) * UNIT] = total[:, 2 * k * UNIT:(2 * k + 1) * UNIT]
        up[:, k * UNIT:(k + 1) * UNIT] = total[:, (2 * k + 1) * UNIT:(2 * k + 2) * UNIT]


def write_first(total, x, y, recur, inp):
    rows, channels = x.shape
    for n in range(channels // BS):
        block = slice(n * BS, (n + 1) * BS)
        x[:, block] = total[:rows, 2 * n * BS:(2 * n + 1) * BS]
        y[:, block] = total[:rows, (2 * n + 1) * BS:(2 * n + 2) * BS]
        recur[n] = total[rows:, block]
        inp[n] = total[rows:, channels + n * BS:channels + (n + 1) * BS]


class Bag(dict):
    def fence(self):
        values, tree = jax.tree.flatten(dict(self))
        values = lax.optimization_barrier(values)
        self.update(jax.tree.unflatten(tree, values))

    def take(self, *names):
        out = [self.pop(name) for name in names]
        return out if len(out) > 1 else out[0]


class Gather:
    def __init__(self, links, me, bag, name, shard, parts=None):
        self.links, self.me, self.bag, self.name = links, me, bag, name
        self.along_steps, self.pair_steps, self.placed, self.other_placed = 0, 0, 0, 0
        self.parts = parts or [(slice(0, shard.shape[0]), slice(0, shard.shape[1]))]
        bag[name] = {"z": [shard], "y": [], "whole": None}

    def along(self, steps=1):
        z = self.bag[self.name]["z"]
        for _ in range(steps):
            if self.along_steps < self.links.line - 1:
                z.append(self.links.along(z[self.along_steps]))
                self.along_steps += 1

    def pair(self, steps=1):
        held = self.bag[self.name]
        for _ in range(steps):
            if self.pair_steps <= self.along_steps and self.pair_steps < self.links.line:
                held["y"].append(self.links.to_pair(held["z"][self.pair_steps]))
                self.pair_steps += 1

    def put(self, pieces, at, bit):
        held = self.bag[self.name]
        base = 2 * self.links.behind(self.me, at)
        wholes = []
        for k, (rows, columns) in enumerate(self.parts):
            piece = pieces[at][rows, columns][None]
            whole = jnp.zeros((self.links.dp,) + piece.shape[1:], bf16) if held["whole"] is None else held["whole"][k]
            wholes.append(lax.dynamic_update_slice(whole, piece, (base + bit, 0, 0)))
        held["whole"] = wholes

    def place(self, z=0, y=0):
        held = self.bag[self.name]
        bit = lax.bitwise_and(self.me, 1)
        for _ in range(z):
            if self.placed <= self.along_steps:
                self.put(held["z"], self.placed, bit)
                self.placed += 1
        for _ in range(y):
            if self.other_placed < self.pair_steps:
                self.put(held["y"], self.other_placed, 1 - bit)
                self.other_placed += 1
        for k in range(min(self.placed, self.pair_steps, self.along_steps)):
            held["z"][k] = None
        for k in range(self.other_placed):
            held["y"][k] = None

    def finish(self):
        line = self.links.line
        while self.pair_steps < line:
            self.along()
            self.pair()
        self.place(line, line)
        return self.bag.pop(self.name)["whole"]


class PairGather:
    def __init__(self, links, me, bag, name, shard):
        self.links, self.me, self.bag, self.name = links, me, bag, name
        self.along_steps, self.placed = 0, 0
        bag[name] = {"own": shard, "other": None, "z": [], "whole": None}

    def pair(self):
        held = self.bag[self.name]
        held["other"] = self.links.to_pair(held["own"])

    def join(self):
        held = self.bag[self.name]
        bit = lax.bitwise_and(self.me, 1)
        both = jnp.zeros((2,) + held["own"].shape, bf16)
        both = lax.dynamic_update_slice(both, held["own"][None], (bit, 0, 0))
        held["z"].append(lax.dynamic_update_slice(both, held["other"][None], (1 - bit, 0, 0)))
        held["own"] = held["other"] = None

    def along(self):
        z = self.bag[self.name]["z"]
        if self.along_steps < self.links.line - 1:
            z.append(self.links.along(z[self.along_steps]))
            self.along_steps += 1

    def place(self, steps=1):
        held = self.bag[self.name]
        for _ in range(steps):
            if self.placed <= self.along_steps:
                piece = held["z"][self.placed][None]
                if held["whole"] is None:
                    held["whole"] = jnp.zeros((self.links.line,) + piece.shape[1:], bf16)
                at = self.links.behind(self.me, self.placed)
                held["whole"] = lax.dynamic_update_slice(held["whole"], piece, (at, 0, 0, 0))
                self.placed += 1
        for k in range(min(self.placed, self.along_steps)):
            held["z"][k] = None

    def finish(self):
        while self.along_steps < self.links.line - 1:
            self.along()
        self.place(self.links.line)
        return self.bag.pop(self.name)["whole"]


class Scatter:
    def __init__(self, links, bag, name, sent, kept):
        self.links, self.bag, self.name = links, bag, name
        self.pair_steps, self.along_steps = 0, 0
        self.size = links.line // len(sent)
        bag[name] = {"sent": list(sent), "kept": kept, "moving": None, "ready": None}

    def pair(self):
        sent = self.bag[self.name]["sent"]
        if self.pair_steps < len(sent):
            sent[self.pair_steps] = self.links.to_pair(sent[self.pair_steps])
            self.pair_steps += 1

    def ready(self):
        held = self.bag[self.name]
        at = self.along_steps
        if at < self.links.line - 1 and at // self.size < self.pair_steps and held["ready"] is None:
            held["ready"] = self.sum_here().astype(bf16)

    def along(self):
        held = self.bag[self.name]
        self.ready()
        if held["ready"] is not None:
            held["moving"], held["ready"] = self.links.along(held["ready"]), None
            self.along_steps += 1

    def sum_here(self):
        held = self.bag[self.name]
        at = self.along_steps
        total = held["kept"][at] + held["sent"][at // self.size][at % self.size].astype(f32)
        if held["moving"] is not None:
            total = total + held["moving"].astype(f32)
        return total

    def finish(self, write, *outs):
        while self.pair_steps < len(self.bag[self.name]["sent"]):
            self.pair()
        while self.along_steps < self.links.line - 1:
            self.along()
        held = self.bag.pop(self.name)
        held.pop("ready")
        return last_sum(write, {**held, "size": self.size}, self.along_steps, outs, self.name)


class AllSum:
    def __init__(self, bag, name, value, axes):
        self.bag, self.name = bag, name
        self.steps = [(axis, count, 1 << k) for axis, count in axes for k in range(count.bit_length() - 1)]
        assert all(count & (count - 1) == 0 for _, count in axes)
        bag[name] = value

    def step(self):
        if self.steps:
            axis, count, bit = self.steps.pop(0)
            value = self.bag[self.name]
            self.bag[self.name] = value + lax.ppermute(value, axis, [(i, i ^ bit) for i in range(count)])

    def finish(self):
        while self.steps:
            self.step()
        return self.bag.pop(self.name)


def body(links, block_in, doc_ids, mix_gain, proj_x, proj_y, conv_taps, recur_gate, input_gate, decay_param,
         proj_out, ffn_gain, ffn_gate, ffn_up, ffn_down, out_grad):
    micro_count, own_rows, width = block_in.shape
    group_rows = doc_ids.shape[1]
    assert group_rows == LEN and own_rows * 4 == group_rows and micro_count == 2
    d_rows, channels = proj_x.shape
    blocks = channels // BS
    hidden_units = ffn_gate.shape[1]
    assert hidden_units % UNIT == 0
    gate_columns = recur_gate.shape[2]
    dp_me = lax.axis_index("dp")
    me = lax.axis_index("mp").astype(jnp.int32).reshape(1)
    gain_one = mix_gain.astype(f32)
    gain_two = ffn_gain.astype(f32)
    to_core, to_x = links.to_core, links.to_x
    bag = Bag()

    def exchange(name):
        send, keep = bag.pop(name + "_send"), bag.pop(name + "_keep")
        own_rows_of = lambda v, k: v[k * own_rows:(k + 1) * own_rows].astype(f32)
        sent = to_core(send)
        bag[name + "_own"] = (keep, sent)
        bag[name + "_x"] = (own_rows_of(keep, 1) + own_rows_of(sent, 1)).astype(bf16)

    def summed(name):
        keep, sent = bag.pop(name + "_own")
        return (keep[:own_rows].astype(f32) + sent[:own_rows].astype(f32)) + bag.pop(name + "_x").astype(f32)

    def across(name):
        bag[name + "_x"] = to_x(bag[name + "_x"])

    def rows_of(name):
        own, core, x, diagonal = bag.take(name, name + "_core", name + "_x", name + "_diagonal")
        return core, diagonal, own, x

    packed = pack(proj_x, proj_y, proj_out.T, jnp.swapaxes(recur_gate, 1, 2), jnp.swapaxes(input_gate, 1, 2))
    inner_rows, outer_rows = slice(0, d_rows), slice(d_rows, d_rows + gate_columns)
    wide, narrow = slice(0, 2 * channels), slice(2 * channels, 3 * channels)
    first = Gather(links, dp_me, bag, "first", packed, [(inner_rows, wide), (inner_rows, narrow), (outer_rows, wide)])
    bag.fence()

    bag["cot0"], bag["cot1"] = out_grad[0], out_grad[1]
    first.along()
    first.pair()
    for micro in range(2):
        xin = block_in[micro].astype(f32)
        inverse = lax.rsqrt(jnp.mean(xin * xin, axis=-1, keepdims=True) + norm_eps)
        bag[f"inverse_one{micro}"] = inverse
        bag[f"normed{micro}"] = (xin * inverse * gain_one).astype(bf16)
    bag.fence()

    first.along()
    first.pair()
    bag["normed0_x"] = to_x(bag["normed0"])
    bag["normed0_core"] = to_core(bag["normed0"])
    first.place(2, 1)
    decay_values = decay_param.astype(f32)
    bag["rate"] = jnp.broadcast_to((-decay_scale * jax.nn.softplus(-decay_values))[None], (8, channels))
    bag["slope"] = jnp.broadcast_to((decay_scale * jax.nn.sigmoid(-decay_values))[None], (8, channels))
    bag["taps"] = jnp.concatenate([conv_taps.astype(f32), jnp.zeros((8 - KW, channels), f32)])
    bag["table"] = jnp.stack(
        [links.behind(dp_me, step + 1) for step in range(links.line)] + [lax.bitwise_and(dp_me, 1).astype(jnp.int32)])
    bag.fence()

    first.along()
    first.pair()
    bag["normed1_x"] = to_x(bag["normed1"])
    bag["normed0_diagonal"] = to_core(bag["normed0_x"])
    first.place(1, 1)
    gate_up = jnp.stack([ffn_gate.reshape(d_rows, -1, UNIT), ffn_up.reshape(d_rows, -1, UNIT)], axis=2)
    second = Gather(links, dp_me, bag, "second", gate_up.reshape(d_rows, 2 * hidden_units))
    third = PairGather(links, dp_me, bag, "third", ffn_down.T)
    for micro in range(2):
        bag[f"ids{micro}"] = jnp.broadcast_to(doc_ids[micro][:, None], (group_rows, BS))
    bag.fence()

    first.pair()
    second.along()
    third.pair()
    bag["cot0_x"] = to_x(bag["cot0"])
    first.place(1, 1)
    bag.fence()

    def mix(micro):
        bag[f"normed_all{micro}"], branch = project_rows(rows_of(f"normed{micro}"), bag["w_branch"], 256, "branch", hbm_out)
        branch = branch.reshape(4, own_rows, 2 * channels)
        gated, *rest = mixing_forward(me, branch, bag[f"ids{micro}"], bag["taps"], bag["gates"], bag["rate"])
        bag[f"mixed{micro}"] = [branch] + rest
        bag[f"gated{micro}"] = gated.reshape(group_rows, channels)

    def against_of(name, left, weight):
        bag[name + "_send"], bag[name + "_keep"] = against_rows(bag[left], bag[weight], weight + "_turned")

    def middle_of(micro):
        middle = block_in[micro].astype(f32) + summed(f"first{micro}")
        inverse = lax.rsqrt(jnp.mean(middle * middle, axis=-1, keepdims=True) + norm_eps)
        bag[f"middle{micro}"], bag[f"inverse_two{micro}"] = middle, inverse
        bag[f"two{micro}"] = (middle * inverse * gain_two).astype(bf16)

    second.along()
    second.pair()
    third.join()
    bag["cot1_x"] = to_x(bag["cot1"])
    w_branch, w_out, gates = first.finish()
    bag["w_branch"] = w_branch.reshape(width, 2 * channels)
    bag["gates"] = gates.reshape(BS, 2 * channels)
    bag["w_out"] = w_out.reshape(width, channels)
    mix(0)
    against_of("first0", "gated0", "w_out")
    bag.fence()

    bag["normed1_core"] = to_core(bag["normed1"])
    bag["normed1_diagonal"] = to_core(bag["normed1_x"])
    exchange("first0")
    second.place(1)
    bag.fence()

    second.along()
    second.pair()
    across("first0")
    second.place(1)
    mix(1)
    bag.fence()

    bag["cot0_core"] = to_core(bag["cot0"])
    bag["cot0_diagonal"] = to_core(bag["cot0_x"])
    middle_of(0)
    against_of("first1", "gated1", "w_out")
    bag.fence()

    third.along()
    second.pair()
    bag["two0_x"] = to_x(bag["two0"])
    bag["two0_core"] = to_core(bag["two0"])
    exchange("first1")
    bag["cot_all0"] = jnp.concatenate(rows_of("cot0"))
    second.place(3, 2)
    third.place()
    bag.fence()

    def forward(micro):
        bag[f"two_all{micro}"], bag[f"hidden{micro}"], *bag[f"by{micro}"] = ffn_forward(
            rows_of(f"two{micro}"), bag["w_up"])

    third.along()
    second.pair()
    across("first1")
    bag["two0_diagonal"] = to_core(bag["two0_x"])
    bag["cot1_core"] = to_core(bag["cot1"])
    bag["cot1_diagonal"] = to_core(bag["cot1_x"])
    bag["cot_all1"] = jnp.concatenate(rows_of("cot1"))
    second.place(0, 1)
    third.place()
    bag.fence()

    middle_of(1)
    bag.fence()

    third.along()
    bag["two1_x"] = to_x(bag["two1"])
    bag["w_up"] = second.finish()[0].reshape(width, 2 * hidden_units)
    third.place()
    forward(0)
    bag.fence()

    def back(micro):
        name = f"second{micro}"
        bag[f"grad_pre{micro}"], bag[name + "_send"], bag[name + "_keep"] = ffn_backward(
            bag[f"cot_all{micro}"], bag["w_down"], *bag.pop(f"by{micro}"), bag["w_up"])

    def grad_middle_of(micro):
        grad = summed(f"second{micro}")
        inverse, middle = bag[f"inverse_two{micro}"], bag[f"middle{micro}"]
        unit = middle * inverse
        total = out_grad[micro].astype(f32) + norm_back(grad, unit, inverse, gain_two)
        bag[f"grad_middle{micro}"] = total
        bag[f"gain_two{micro}"] = jnp.sum(grad * unit, axis=0)
        bag[f"low{micro}"] = total.astype(bf16)

    bag["two1_core"] = to_core(bag["two1"])
    bag["two1_diagonal"] = to_core(bag["two1_x"])
    bag["w_down"] = third.finish().reshape(width, hidden_units)
    back(0)
    bag.fence()

    exchange("second0")
    forward(1)
    bag.fence()

    across("second0")
    down_grad = Scatter(links, bag, "down_grad", *weight_grad(
        bag["table"], [bag["cot_all0"], bag["cot_all1"]], [bag["hidden0"], bag["hidden1"]], hidden_units, 2))
    bag.fence()

    down_grad.pair()
    back(1)
    bag.fence()

    exchange("second1")
    down_grad.ready()
    grad_middle_of(0)
    bag.fence()

    across("second1")
    down_grad.pair()
    bag["low0_core"] = to_core(bag["low0"])
    up_grad = Scatter(links, bag, "up_grad", *weight_grad(
        bag["table"], bag.take("two_all0", "two_all1"), bag.take("grad_pre0", "grad_pre1"), 2 * UNIT, 4))
    bag.fence()

    def output_of(micro):
        bag[f"output{micro}"] = (bag[f"middle{micro}"] + summed(f"down{micro}")).astype(bf16)

    bag["low0_x"] = to_x(bag["low0"])
    up_grad.pair()
    down_grad.along()
    grad_middle_of(1)
    against_of("down0", "hidden0", "w_down")
    against_of("down1", "hidden1", "w_down")
    bag.fence()

    def into_mix(micro):
        bag[f"low_all{micro}"], bag[f"grad_gated{micro}"] = project_rows(
            rows_of(f"low{micro}"), bag["w_out"], 256, "grad_gated")

    def mix_back(micro):
        grad, bag[f"gates_grad{micro}"], bag[f"small{micro}"] = mixing_backward(
            me, bag.pop(f"grad_gated{micro}").reshape(4, own_rows, channels), *bag.pop(f"mixed{micro}"),
            bag[f"ids{micro}"], bag["taps"], bag["gates"], bag["rate"], bag["slope"])
        bag[f"grad_branch{micro}"] = grad.reshape(group_rows, 2 * channels)
        against_of(f"third{micro}", f"grad_branch{micro}", "w_branch")

    bag["low1_x"] = to_x(bag["low1"])
    bag["low0_diagonal"] = to_core(bag["low0_x"])
    up_grad.pair()
    up_grad.along()
    down_grad.ready()
    exchange("down0")
    into_mix(0)
    mix_back(0)
    bag.fence()

    across("down0")
    bag["low1_core"] = to_core(bag["low1"])
    bag["low1_diagonal"] = to_core(bag["low1_x"])
    exchange("third0")
    up_grad.pair()
    down_grad.along()
    up_grad.ready()
    into_mix(1)
    out_grad_w = Scatter(links, bag, "out_grad", *weight_grad(
        bag["table"], bag.take("low_all0", "low_all1"), bag.take("gated0", "gated1"), 512, 1))
    bag.fence()

    across("third0")
    up_grad.pair()
    up_grad.along()
    down_grad.ready()
    mix_back(1)
    bag.fence()

    exchange("third1")
    bag.fence()

    def leave(micro):
        grad = summed(f"third{micro}")
        inverse = bag[f"inverse_one{micro}"]
        unit = block_in[micro].astype(f32) * inverse
        bag[f"input_grad{micro}"] = bag[f"grad_middle{micro}"] + norm_back(grad, unit, inverse, gain_one)
        bag[f"gain_one{micro}"] = jnp.sum(grad * unit, axis=0)

    across("third1")
    out_grad_w.pair()
    up_grad.along()
    gates_grads = [bag.pop(f"gates_grad{micro}").reshape(2, links.dp, gate_columns, channels) for micro in range(2)]
    first_grad = Scatter(links, bag, "first_grad", *weight_grad(
        bag["table"], bag.take("normed_all0", "normed_all1"), bag.take("grad_branch0", "grad_branch1"), channels, 4,
        gates_grads))
    bag.fence()

    first_grad.pair()
    down_grad.along()
    leave(1)
    leave(0)
    exchange("down1")
    gains = jnp.stack([bag.pop("gain_one0") + bag.pop("gain_one1"), bag.pop("gain_two0") + bag.pop("gain_two1")])
    bag["sums"] = gains.reshape(-1, 128)
    gain_rows = bag["sums"].shape[0]
    bag.fence()

    first_grad.pair()
    first_grad.along()
    out_grad_w.along()
    sums = AllSum(bag, "gains", bag.pop("sums"), [("mp", links.mp)])
    small = (bag.pop("small0") + bag.pop("small1")).reshape(-1, 128)
    sums = AllSum(bag, "sums", jnp.concatenate([sums.finish(), small]), [("dp", links.dp)])
    bag["down1_xa"] = to_x(bag["down1_x"][:own_rows // 2])
    output_of(0)
    bag["up_total"] = up_grad.finish(write_gate_up, (d_rows, hidden_units), (d_rows, hidden_units))
    bag.fence()

    first_grad.pair()
    first_grad.along()
    out_grad_w.along()
    sums.step()
    bag["down1_xb"] = to_x(bag["down1_x"][own_rows // 2:])
    bag["down_total"] = down_grad.finish(write_plain, (d_rows, hidden_units))
    bag.fence()

    first_grad.pair()
    first_grad.along()
    out_grad_w.along()
    sums.step()
    bag["down1_x"] = jnp.concatenate(bag.take("down1_xa", "down1_xb"))
    output_of(1)
    bag["outputs"] = jnp.stack(bag.take("output0", "output1"))
    bag["input_grads"] = jnp.stack([bag.pop("input_grad0"), bag.pop("input_grad1")])
    bag.fence()

    bag["out_total"] = out_grad_w.finish(write_plain, (d_rows, channels))
    x_grad, y_grad, recur, inp = first_grad.finish(
        write_first, (d_rows, channels), (d_rows, channels), (blocks, gate_columns, BS), (blocks, gate_columns, BS))
    sums = sums.finish()
    gains = sums[:gain_rows].reshape(2, width)
    small = sums[gain_rows:].reshape(8, channels)
    return (
        bag["outputs"],
        bag["input_grads"],
        gains[0],
        x_grad,
        y_grad,
        small[0:KW],
        jnp.swapaxes(recur, 1, 2),
        jnp.swapaxes(inp, 1, 2),
        small[KW],
        bag["out_total"][0].T,
        gains[1],
        *bag["up_total"],
        bag["down_total"][0].T,
    )


def solution(mesh):
    links = Links(mesh.shape["dp"], mesh.shape["mp"])
    tokens = P(None, ("dp", "mp"), None)
    rows, columns, gate = P("dp", "mp"), P("mp", "dp"), P("mp", None, "dp")
    return jax.shard_map(
        functools.partial(body, links),
        mesh=mesh,
        in_specs=(tokens, P(None, "dp"), P(), rows, rows, P(None, "mp"), gate, gate, P("mp"), columns, P(), rows,
                  rows, columns, tokens),
        out_specs=(tokens, tokens, P(), rows, rows, P(None, "mp"), gate, gate, P("mp"), columns, P(), rows, rows,
                   columns),
        check_vma=False,
    )
```
